32 devices in a mesh: groups: 2 (over y), rows: 4 (over z), mp: 2 (over x), pair: 2 (over core).
Axes of the slice: x: 2, y: 2, z: 4, core: 2. Of those that a mesh axis runs over, the one named last changes fastest.
Arguments:
- query_rows: bfloat16 [2048, 512], P(('groups', 'rows', 'pair'), 'mp'), parts along dimension 0, may hold values from -240 to 240
- key_rows: bfloat16 [65536, 512], P(('groups', 'rows', 'pair'), 'mp'), parts along dimension 0, may hold values from -24 to 24
- value_rows: bfloat16 [65536, 512], P(('groups', 'rows', 'pair'), 'mp'), parts along dimension 0, may hold values from -6 to 6
- cotangent: bfloat16 [2048, 512], P(('groups', 'rows', 'pair'), 'mp'), parts along dimension 0, may hold values from -1536 to 1536
- train_rows: int32 [16], P('groups'), parts along dimension 0, may hold values from 1 to 12288, as said below
- test_rows: int32 [16], P('groups'), parts along dimension 0, may hold values from 32 to 128
- block_table: int32 [128], P('groups'), parts along dimension 0, may hold values from 0 to 7, as said below
Outputs:
- query_grad: bfloat16 [2048, 512], P(('groups', 'rows', 'pair'), 'mp'), parts along dimension 0
- key_grad: bfloat16 [65536, 512], P(('groups', 'rows', 'pair'), 'mp'), parts along dimension 0
- value_grad: bfloat16 [65536, 512], P(('groups', 'rows', 'pair'), 'mp'), parts along dimension 0
The draws below stay inside these ranges and needn't reach their ends.
There are 2 independent parts, one for each index of `groups`. The reference program is written for one: setup_inputs(seed, part) draws one part's arguments, and reference() takes and returns one part's arrays. A program takes and returns all parts, laid end to end along the dimension named above; each array names one. Nothing has to cross between parts.
Inputs may be any that keep to these rules, and one draw needn't show every extreme that they name: block_table names table t exactly ceil(train_rows[t] / 512) times; the largest table has 24 full blocks. `block_table`: every table is named at least once.
All inputs are finite; a program needn't handle non-finite values.
Results may differ from the reference program's by a relative error of at most 0.0075.
Values may be sent and summed in bfloat16 or wider, within the bound.
No kernel may reach another device: no remote copies, remote signals or barrier semaphores. Data moves between devices by JAX's collectives and lax.ppermute only.
A program may use at most 64 MiB of HBM per device.

```python
import math
import jax
import jax.numpy as jnp
from jax import lax

D = 512
HEADS = 8
HD = 64
TABLES = 8
TEST = 128
BLK = 512
TBLK = 64
TRAIN = 32768
QALL = 1024
MAXIMAL_SEGMENTS = 24


def block_counts(key):
    base = jax.random.fold_in(key, 101)
    shares = jax.random.randint(jax.random.fold_in(base, 1), (TABLES,), 1, 5)
    order = jax.random.permutation(jax.random.fold_in(base, 2), TABLES)
    largest = order[0]
    is_biggest_dataset = jnp.arange(TABLES) == largest
    remaining = TBLK - MAXIMAL_SEGMENTS - (TABLES - 1)
    shares = jnp.where(is_biggest_dataset, 0, shares)
    additional_segments = remaining * shares // jnp.sum(shares)
    residual_segments = remaining - jnp.sum(additional_segments)
    dataset_ordering = jnp.argsort(order)
    surplus_segments = jnp.where(jnp.logical_not(is_biggest_dataset) & (dataset_ordering <= residual_segments), 1, 0)
    dataset_tallies = jnp.where(is_biggest_dataset, MAXIMAL_SEGMENTS, 1 + additional_segments + surplus_segments)
    return (dataset_tallies.astype(jnp.int32), largest)


def block_owners(key):
    dataset_tallies, largest = block_counts(key)
    bounds = jnp.cumsum(dataset_tallies)
    slots = jnp.arange(TBLK)
    sorted_owner = jnp.sum(jnp.where(slots[:, None] >= bounds[None, :], 1, 0), axis=1)
    shuffle = jax.random.permutation(jax.random.fold_in(key, 107), TBLK)
    return sorted_owner[shuffle].astype(jnp.int32)


def key_field(key):
    base = jax.random.truncated_normal(jax.random.fold_in(key, 113), -6.0, 6.0, (TRAIN, D), jnp.float32)
    return base


def draw_train_rows(key, part):
    dataset_tallies, largest = block_counts(key)
    fill = jax.random.randint(jax.random.fold_in(key, 103), (TABLES,), 1, BLK + 1)
    fill = jnp.where(jnp.arange(TABLES) == largest, BLK, fill)
    return ((dataset_tallies - 1) * BLK + fill).astype(jnp.int32)


def draw_block_table(key, part):
    return block_owners(key)


def draw_test_rows(key, part):
    base = jax.random.fold_in(key, 109)
    dataset_tallies = jax.random.randint(jax.random.fold_in(base, 1), (TABLES,), TEST // 4, TEST + 1)
    order = jax.random.permutation(jax.random.fold_in(base, 2), TABLES)
    positions = jnp.arange(TABLES)
    dataset_tallies = jnp.where(positions == order[0], TEST, dataset_tallies)
    dataset_tallies = jnp.where(positions == order[1], TEST // 4, dataset_tallies)
    return dataset_tallies.astype(jnp.int32)


def draw_key_rows(key, part):
    field = key_field(key)
    return field.astype(jnp.bfloat16)


def draw_query_rows(key, part):
    base = jax.random.truncated_normal(jax.random.fold_in(key, 131), -6.0, 6.0, (QALL, D), jnp.float32)
    return base.astype(jnp.bfloat16)


def block_scale(rng, extent, cuts, least, high):
    def one(dim, shards_of):
        draws = jax.random.uniform(jax.random.fold_in(jax.random.fold_in(rng, 6), dim), (shards_of,), jnp.float32, least / len(cuts), high / len(cuts))
        return jnp.repeat(jnp.exp(draws), extent[dim] // shards_of).reshape((-1,) + (1,) * (len(extent) - dim - 1))

    level = one(*cuts[0])
    for cut in cuts[1:]:
        level = level * one(*cut)
    return level


def normal_values(rng, extent, deviation, bound, split=(), kind=jnp.bfloat16):
    values = deviation * jax.random.normal(rng, extent, jnp.float32)
    if split:
        values = values * block_scale(rng, extent, split, -0.22, 0.18)
    return jnp.clip(values, -bound, bound).astype(kind)


def setup_inputs(seed: int = 0, part: int = 0) -> dict:
    arg_keys = jax.random.split(jax.random.key(seed), 8)
    part_keys = jax.random.split(jax.random.fold_in(arg_keys[7], part), 8)
    return {
        "query_rows": draw_query_rows(jax.random.fold_in(jax.random.fold_in(arg_keys[7], part), 71), part),
        "key_rows": draw_key_rows(jax.random.fold_in(jax.random.fold_in(arg_keys[7], part), 71), part),
        "value_rows": normal_values(part_keys[2], (TRAIN, D), 1.0, 6.0, ((0, 8), (1, 2))),
        "cotangent": normal_values(part_keys[3], (QALL, D), 256.0, 1536.0, ((0, 8), (1, 2))),
        "train_rows": draw_train_rows(jax.random.fold_in(jax.random.fold_in(arg_keys[7], part), 71), part),
        "test_rows": draw_test_rows(jax.random.fold_in(jax.random.fold_in(arg_keys[7], part), 71), part),
        "block_table": draw_block_table(jax.random.fold_in(jax.random.fold_in(arg_keys[7], part), 71), part),
    }


NEG = -1e+30

def table_lookup(positions, entries):
    matches = positions[:, None] == jnp.arange(entries.shape[0], dtype=jnp.int32)[None, :]
    return lax.optimization_barrier(jnp.sum(jnp.where(matches, entries[None, :], 0), axis=1)).astype(jnp.int32)

def reference(query_rows, key_rows, value_rows, cotangent, train_rows, test_rows, block_table):
    score_scale = 1.0 / math.sqrt(HD)
    block_ids = jnp.arange(TBLK, dtype=jnp.int32)
    earlier = (block_table[None, :] == block_table[:, None]) & (block_ids[None, :] < block_ids[:, None])
    ordinal = lax.optimization_barrier(jnp.sum(jnp.where(earlier, 1, 0), axis=1)).astype(jnp.int32)
    live_keys = table_lookup(block_table, train_rows) - ordinal * BLK
    row_ids = jnp.arange(QALL, dtype=jnp.int32)
    query_live = row_ids % TEST < table_lookup(row_ids // TEST, test_rows)
    live_grads = jnp.where(query_live[:, None], cotangent, jnp.zeros_like(cotangent))
    query_heads = query_rows.reshape(TABLES, TEST, HEADS, HD)
    grad_heads = live_grads.reshape(TABLES, TEST, HEADS, HD)
    key_blocks = key_rows.reshape(TBLK, BLK, HEADS, HD)
    value_blocks = value_rows.reshape(TBLK, BLK, HEADS, HD)
    key_index = jnp.arange(BLK, dtype=jnp.int32)

    def block_scores(which_table, live_count, key_block):
        query_block = query_heads[which_table]
        raw_scores = jnp.einsum('qhd,khd->hqk', query_block.astype(jnp.float32), key_block.astype(jnp.float32)) * score_scale
        return (query_block, jnp.where(key_index[None, None, :] < live_count, raw_scores, NEG))

    def stats_step(running, inputs):
        which_table, live_count, key_block, value_block = inputs
        _, scores = block_scores(which_table, live_count, key_block)
        block_peak = lax.optimization_barrier(jnp.max(scores, axis=2))
        weights = jnp.exp(scores - block_peak[:, :, None])
        block_mass = lax.optimization_barrier(jnp.sum(weights, axis=2))
        weights_low = lax.optimization_barrier(weights.astype(jnp.bfloat16)).astype(jnp.float32)
        block_output = jnp.einsum('hqk,khd->qhd', weights_low, value_block.astype(jnp.float32))
        peaks, masses, outputs = running
        old_peak = peaks[which_table]
        new_peak = jnp.maximum(old_peak, block_peak)
        old_weight = jnp.exp(old_peak - new_peak)
        new_weight = jnp.exp(block_peak - new_peak)
        masses = masses.at[which_table].set(masses[which_table] * old_weight + block_mass * new_weight)
        outputs = outputs.at[which_table].set(outputs[which_table] * old_weight.T[:, :, None] + block_output * new_weight.T[:, :, None])
        peaks = peaks.at[which_table].set(new_peak)
        return ((peaks, masses, outputs), None)
    initial = (jnp.full((TABLES, HEADS, TEST), NEG, jnp.float32), jnp.zeros((TABLES, HEADS, TEST), jnp.float32), jnp.zeros((TABLES, TEST, HEADS, HD), jnp.float32))
    (peaks, masses, outputs), _ = lax.scan(stats_step, initial, (block_table, live_keys, key_blocks, value_blocks))
    attended = outputs / jnp.transpose(masses, (0, 2, 1))[:, :, :, None]
    inner = jnp.transpose(lax.optimization_barrier(jnp.sum(grad_heads.astype(jnp.float32) * attended, axis=3)), (0, 2, 1))

    def grad_step(running, inputs):
        which_table, live_count, key_block, value_block = inputs
        query_block, scores = block_scores(which_table, live_count, key_block)
        probs = jnp.exp(scores - peaks[which_table][:, :, None]) / masses[which_table][:, :, None]
        probs_low = lax.optimization_barrier(probs.astype(jnp.bfloat16)).astype(jnp.float32)
        grad_block = grad_heads[which_table].astype(jnp.float32)
        value_part = jnp.einsum('hqk,qhd->khd', probs_low, grad_block)
        dprobs = jnp.einsum('qhd,khd->hqk', grad_block, value_block.astype(jnp.float32))
        dscores = lax.optimization_barrier((probs * (dprobs - inner[which_table][:, :, None])).astype(jnp.bfloat16)).astype(jnp.float32)
        key_part = jnp.einsum('hqk,qhd->khd', dscores, query_block.astype(jnp.float32)) * score_scale
        query_part = jnp.einsum('hqk,khd->qhd', dscores, key_block.astype(jnp.float32)) * score_scale
        running = running.at[which_table].add(query_part)
        return (running, (key_part.astype(jnp.bfloat16), value_part.astype(jnp.bfloat16)))
    query_sums, (key_parts, value_parts) = lax.scan(grad_step, jnp.zeros((TABLES, TEST, HEADS, HD), jnp.float32), (block_table, live_keys, key_blocks, value_blocks))
    query_grad = query_sums.reshape(QALL, D).astype(jnp.bfloat16)
    return (query_grad, key_parts.reshape(TRAIN, D), value_parts.reshape(TRAIN, D))
```

```python
import math

import jax
import jax.numpy as jnp
from jax import lax
from jax.experimental import pallas as pl
from jax.experimental.pallas import tpu as pltpu
from jax.sharding import PartitionSpec as P

HD = 64
TEST = 128
BLK = 512
LANES = 128
WIDE = 2 * TEST

NEG = -1e30
SCORE_SCALE = 1.0 / math.sqrt(HD)
LOG2_SCALE = SCORE_SCALE * math.log2(math.e)
RP = ("rows", "pair")
PAIR = [(0, 1), (1, 0)]


def table_lookup(positions, entries):
    matches = positions[:, None] == jnp.arange(entries.shape[0], dtype=jnp.int32)[None, :]
    return jnp.sum(jnp.where(matches, entries[None, :], 0), axis=1)


def params(mib):
    return pltpu.CompilerParams(
        dimension_semantics=("arbitrary",), vmem_limit_bytes=mib * 1024 * 1024
    )


def two_heads(rows):
    feature = lax.broadcasted_iota(jnp.int32, rows.shape, 0)
    zero = jnp.zeros_like(rows)
    return jnp.concatenate(
        [jnp.where(feature < HD, rows, zero), jnp.where(feature < HD, zero, rows)], axis=1
    )


def scores_kernel(features, piece_slots, owner, live, testn, slot, *refs):
    count = len(piece_slots)
    pieces = refs[:count]
    key_ref, value_ref, qgt_ref, e_ref, u_ref, blk_ref, tab_ref, qg_s, sem = refs[count:]
    b = pl.program_id(0)
    table = owner[b]

    @pl.when(b == 0)
    def _():
        copies = []
        for n, (start, size) in enumerate(piece_slots):
            copies.append(
                pltpu.make_async_copy(pieces[n], qg_s.at[pl.ds(start, size)], sem.at[n])
            )
        for copy in copies:
            copy.start()
        tab_ref[0] = jnp.full(tab_ref.shape[1:], NEG, jnp.float32)
        tab_ref[1] = jnp.zeros(tab_ref.shape[1:], jnp.float32)
        tab_ref[2] = jnp.zeros(tab_ref.shape[1:], jnp.float32)
        for copy in copies:
            copy.wait()

    turned = qg_s[slot[table]].T
    query = lax.broadcasted_iota(jnp.int32, (LANES, TEST), 1)
    grad_live = query < testn[table]
    key_live = lax.broadcasted_iota(jnp.int32, (BLK, WIDE), 0) < live[b]
    for p in range(features // LANES):
        at = slice(p * LANES, (p + 1) * LANES)
        wide = slice(p * WIDE, (p + 1) * WIDE)
        q_t = turned[at]
        g_t = turned[features + p * LANES : features + (p + 1) * LANES]
        g_t = jnp.where(grad_live, g_t, jnp.zeros_like(g_t))
        qgt_ref[0, at, :] = q_t
        qgt_ref[0, pl.ds(features + p * LANES, LANES), :] = g_t
        scores = jnp.dot(key_ref[:, at], two_heads(q_t), preferred_element_type=jnp.float32)
        dprobs = jnp.dot(value_ref[:, at], two_heads(g_t), preferred_element_type=jnp.float32)
        scores = jnp.where(key_live, scores, NEG)
        peak = jnp.max(scores, axis=0, keepdims=True) * LOG2_SCALE
        weights = jnp.exp2(scores * LOG2_SCALE - peak)
        mass = jnp.sum(weights, axis=0, keepdims=True)
        part = jnp.sum(weights * dprobs, axis=0, keepdims=True)
        e_ref[0, :, wide] = weights.astype(jnp.bfloat16)
        u_ref[0, :, wide] = (weights * (dprobs - part / mass)).astype(jnp.bfloat16)
        blk_ref[0, pl.ds(b, 1), wide] = peak
        blk_ref[1, pl.ds(b, 1), wide] = mass
        blk_ref[2, pl.ds(b, 1), wide] = part
        old = tab_ref[0, pl.ds(table, 1), wide]
        new = jnp.maximum(old, peak)
        old_weight = jnp.exp2(old - new)
        new_weight = jnp.exp2(peak - new)
        tab_ref[0, pl.ds(table, 1), wide] = new
        tab_ref[1, pl.ds(table, 1), wide] = (
            tab_ref[1, pl.ds(table, 1), wide] * old_weight + mass * new_weight
        )
        tab_ref[2, pl.ds(table, 1), wide] = (
            tab_ref[2, pl.ds(table, 1), wide] * old_weight + part * new_weight
        )


def block_scores(owner, live, testn, slot, pieces, key_rows, value_rows):
    features = key_rows.shape[1]
    blocks = owner.shape[0]
    tables = testn.shape[0]
    stacked = features // HD * TEST
    starts, total = [], 0
    for piece in pieces:
        starts.append((total, piece.shape[0]))
        total += piece.shape[0]
    row_block = pl.BlockSpec((BLK, features), lambda b, *_: (b, 0))
    block_out = lambda *shape: pl.BlockSpec((1,) + shape, lambda b, *_: (b, 0, 0))
    whole = lambda *shape: pl.BlockSpec(shape, lambda b, *_: (0,) * len(shape))
    return pl.pallas_call(
        lambda *refs: scores_kernel(features, tuple(starts), *refs),
        grid_spec=pltpu.PrefetchScalarGridSpec(
            num_scalar_prefetch=4,
            grid=(blocks,),
            in_specs=[pl.BlockSpec(memory_space=pl.ANY) for _ in pieces]
            + [row_block, row_block],
            out_specs=[
                block_out(2 * features, TEST),
                block_out(BLK, stacked),
                block_out(BLK, stacked),
                whole(3, blocks, stacked),
                whole(3, tables, stacked),
            ],
            scratch_shapes=[
                pltpu.VMEM((tables, TEST, 2 * features), jnp.bfloat16),
                pltpu.SemaphoreType.DMA((len(pieces),)),
            ],
        ),
        out_shape=[
            jax.ShapeDtypeStruct((blocks, 2 * features, TEST), jnp.bfloat16),
            jax.ShapeDtypeStruct((blocks, BLK, stacked), jnp.bfloat16),
            jax.ShapeDtypeStruct((blocks, BLK, stacked), jnp.bfloat16),
            jax.ShapeDtypeStruct((3, blocks, stacked), jnp.float32),
            jax.ShapeDtypeStruct((3, tables, stacked), jnp.float32),
        ],
        compiler_params=params(40),
        name="block_scores",
    )(owner, live, testn, slot, *pieces, key_rows, value_rows)


def query_sums_kernel(features, key_ref, e_ref, u_ref, out_ref):
    for p in range(features // LANES):
        at = slice(p * LANES, (p + 1) * LANES)
        wide = slice(p * WIDE, (p + 1) * WIDE)
        keys = key_ref[:, at]
        for n, ref in enumerate((u_ref, e_ref)):
            product = lax.dot_general(
                keys, ref[0, :, wide], (((0,), (0,)), ((), ())), preferred_element_type=jnp.float32
            )
            out_ref[0, n, pl.ds(p * LANES, HD), :] = product[:HD, :TEST]
            out_ref[0, n, pl.ds(p * LANES + HD, HD), :] = product[HD:, TEST:]


def query_sums(key_rows, e_all, u_all):
    features = key_rows.shape[1]
    blocks, _, stacked = e_all.shape
    return pl.pallas_call(
        lambda *refs: query_sums_kernel(features, *refs),
        grid=(blocks,),
        in_specs=[
            pl.BlockSpec((BLK, features), lambda b: (b, 0)),
            pl.BlockSpec((1, BLK, stacked), lambda b: (b, 0, 0)),
            pl.BlockSpec((1, BLK, stacked), lambda b: (b, 0, 0)),
        ],
        out_specs=pl.BlockSpec((1, 2, features, TEST), lambda b: (b, 0, 0, 0)),
        out_shape=jax.ShapeDtypeStruct((blocks, 2, features, TEST), jnp.float32),
        compiler_params=params(40),
        name="query_sums",
    )(key_rows, e_all, u_all)


def merged(pieces):
    peak = pieces[0][0]
    for piece in pieces[1:]:
        peak = jnp.maximum(peak, piece[0])
    mass = part = 0.0
    for piece in pieces:
        weight = jnp.exp2(piece[0] - peak)
        mass = mass + piece[1] * weight
        part = part + piece[2] * weight
    return peak, mass, part


def merge_kernel(a_ref, b_ref, out_ref):
    out_ref[0], out_ref[1], out_ref[2] = merged([a_ref, b_ref])


def merge_stats(a, b):
    return pl.pallas_call(
        merge_kernel, out_shape=jax.ShapeDtypeStruct(a.shape, jnp.float32), name="merge_stats"
    )(a, b)


def query_grad_kernel(features, count, owner, slot, *refs):
    pieces = refs[:count]
    blk_ref, ab_ref = refs[count : count + 2]
    outs = refs[count + 2 : -2]
    c_ref, d_ref, *q_refs = outs
    tab_s, acc_s = refs[-2:]
    blocks = blk_ref.shape[1]
    tab_s[0], tab_s[1], tab_s[2] = merged(pieces)
    acc_s[...] = jnp.zeros_like(acc_s)
    for b in range(blocks):
        table = owner[b]
        at = slot[table]
        mass = tab_s[1, pl.ds(table, 1), :]
        c = jnp.exp2(blk_ref[0, b : b + 1, :] - tab_s[0, pl.ds(table, 1), :]) / mass
        shift = blk_ref[2, b : b + 1, :] / blk_ref[1, b : b + 1, :]
        d = c * (shift - tab_s[2, pl.ds(table, 1), :] / mass)
        c_ref[b : b + 1, :] = c
        d_ref[b : b + 1, :] = d
        for h in range(features // HD):
            rows = slice(h * HD, (h + 1) * HD)
            lanes = slice(h * TEST, (h + 1) * TEST)
            acc_s[at, rows, :] += c[:, lanes] * ab_ref[b, 0, rows, :] + d[:, lanes] * ab_ref[b, 1, rows, :]
    tables = acc_s.shape[0]
    per = tables // len(q_refs)
    for n in range(tables):
        ref = q_refs[n // per]
        ref[n % per] = (acc_s[n] * SCORE_SCALE).T.astype(ref.dtype)


def query_grads(owner, slot, pieces, blk, ab, q_dtypes):
    blocks, _, features, _ = ab.shape
    tables = slot.shape[0]
    stacked = blk.shape[2]
    per = tables // len(q_dtypes)
    vmem = pl.BlockSpec(memory_space=pltpu.VMEM)
    smem = pl.BlockSpec(memory_space=pltpu.SMEM)
    return pl.pallas_call(
        lambda *refs: query_grad_kernel(features, len(pieces), *refs),
        in_specs=[smem, smem] + [vmem] * (len(pieces) + 2),
        out_specs=[vmem] * (2 + len(q_dtypes)),
        out_shape=[
            jax.ShapeDtypeStruct((blocks, stacked), jnp.float32),
            jax.ShapeDtypeStruct((blocks, stacked), jnp.float32),
        ]
        + [jax.ShapeDtypeStruct((per, TEST, features), dtype) for dtype in q_dtypes],
        scratch_shapes=[
            pltpu.VMEM((3, tables, stacked), jnp.float32),
            pltpu.VMEM((tables, features, TEST), jnp.float32),
        ],
        compiler_params=pltpu.CompilerParams(vmem_limit_bytes=40 * 1024 * 1024),
        name="query_grads",
    )(owner, slot, *pieces, blk, ab)


def row_grads_kernel(features, qgt_ref, c_ref, d_ref, e_ref, u_ref, dk_ref, dv_ref):
    b = pl.program_id(0)
    turned = (((1,), (1,)), ((), ()))
    for p in range(features // LANES):
        at = slice(p * LANES, (p + 1) * LANES)
        wide = slice(p * WIDE, (p + 1) * WIDE)
        c = c_ref[pl.ds(b, 1), wide]
        d = d_ref[pl.ds(b, 1), wide]
        q_t = two_heads(qgt_ref[0, at, :].astype(jnp.float32))
        g_t = two_heads(qgt_ref[0, pl.ds(features + p * LANES, LANES), :].astype(jnp.float32))
        for_u = (q_t * (c * SCORE_SCALE)).astype(jnp.bfloat16)
        for_e = jnp.concatenate([g_t * c, q_t * (d * SCORE_SCALE)], axis=0).astype(jnp.bfloat16)
        from_e = lax.dot_general(e_ref[0, :, wide], for_e, turned, preferred_element_type=jnp.float32)
        from_u = lax.dot_general(u_ref[0, :, wide], for_u, turned, preferred_element_type=jnp.float32)
        dv_ref[:, at] = from_e[:, :LANES].astype(jnp.bfloat16)
        dk_ref[:, at] = (from_u + from_e[:, LANES:]).astype(jnp.bfloat16)


def row_grads(qgt, c, d, e_all, u_all):
    blocks, _, stacked = e_all.shape
    features = qgt.shape[1] // 2
    one = lambda *shape: pl.BlockSpec((1,) + shape, lambda b: (b, 0, 0))
    whole = pl.BlockSpec((blocks, stacked), lambda b: (0, 0))
    rows = pl.BlockSpec((BLK, features), lambda b: (b, 0))
    return pl.pallas_call(
        lambda *refs: row_grads_kernel(features, *refs),
        grid=(blocks,),
        in_specs=[one(2 * features, TEST), whole, whole, one(BLK, stacked), one(BLK, stacked)],
        out_specs=[rows, rows],
        out_shape=[jax.ShapeDtypeStruct((blocks * BLK, features), jnp.bfloat16)] * 2,
        compiler_params=params(40),
        name="row_grads",
    )(qgt, c, d, e_all, u_all)


def local(small, query_rows, key_rows, value_rows, cotangent, train_rows, test_rows, block_table):
    chip = lax.axis_index("rows").astype(jnp.int32)
    core = lax.axis_index("pair").astype(jnp.int32)
    device = lax.axis_index(RP).astype(jnp.int32)
    local_rows, features = query_rows.shape
    blocks = key_rows.shape[0] // BLK
    tables = train_rows.shape[0]
    stacked = features // HD * TEST

    my_blocks = device * blocks + jnp.arange(blocks, dtype=jnp.int32)
    block_ids = jnp.arange(block_table.shape[0], dtype=jnp.int32)
    owner = lax.dynamic_slice_in_dim(block_table, device * blocks, blocks)
    earlier = (block_table[None, :] == owner[:, None]) & (block_ids[None, :] < my_blocks[:, None])
    ordinal = jnp.sum(jnp.where(earlier, 1, 0), axis=1).astype(jnp.int32)
    live = jnp.minimum(table_lookup(owner, train_rows) - ordinal * BLK, BLK).astype(jnp.int32)
    ids = jnp.arange(tables, dtype=jnp.int32)

    both = jnp.concatenate([query_rows, cotangent], axis=1)
    if small:
        cross = [(2 * z + c, 2 * (z ^ (1 + c)) + c) for z in range(4) for c in range(2)]
        far = [(2 * z + c, 2 * (z ^ 3) + c) for z in range(4) for c in range(2)]
        mine = chip ^ (1 + core)
        other = chip ^ (2 - core)
        table_chip, table_core = ids // 2, ids % 2
        is_far = jnp.where(table_core == core, 6, 7)
        slot_in = jnp.where(
            table_chip == chip,
            table_core,
            jnp.where(
                table_chip == mine, 2 + table_core, jnp.where(table_chip == other, 4 + table_core, is_far)
            ),
        ).astype(jnp.int32)
        not_mine = jnp.where(table_core == core, 0, 1)
        slot_out = jnp.where(
            table_chip == mine,
            not_mine,
            jnp.where(
                table_chip == other,
                5 - not_mine,
                jnp.where(table_chip == chip, 3 + 4 * not_mine, 2 + 4 * not_mine),
            ),
        ).astype(jnp.int32)

        own = both.reshape(1, TEST, 2 * features)
        from_far = lax.ppermute(own, RP, far)
        chip_rows = lax.all_gather(own, "pair", axis=0, tiled=True)
        from_mine = lax.ppermute(chip_rows, RP, cross)
        from_other = lax.ppermute(from_mine, "pair", PAIR)
        peer_far = lax.ppermute(from_far, "pair", PAIR)
        pieces = [chip_rows, from_mine, from_other, from_far, peer_far]
    else:
        slot_in = slot_out = ids
        everyone = lax.all_gather(both, RP, axis=0, tiled=True)
        pieces = [everyone.reshape(tables, TEST, 2 * features)]

    qgt, e_all, u_all, blk, tab = block_scores(
        owner, live, test_rows, slot_in, pieces, key_rows, value_rows
    )
    if small:
        chip_tab = merge_stats(tab, lax.ppermute(tab, "pair", PAIR))
        far_tab = lax.ppermute(chip_tab, RP, far)
        mine_tab = lax.ppermute(chip_tab, RP, cross)
        other_tab = lax.ppermute(mine_tab, "pair", PAIR)
        stats = [chip_tab, far_tab, mine_tab, other_tab]
        dtypes = [jnp.float32, jnp.bfloat16]
    else:
        peak = lax.pmax(tab[0], RP)
        sums = lax.psum(tab[1:] * jnp.exp2(tab[0] - peak)[None], RP)
        stats = [jnp.concatenate([peak[None], sums], axis=0)]
        dtypes = [jnp.float32]
    ab = query_sums(key_rows, e_all, u_all)
    c, d, *q_terms = query_grads(owner, slot_out, stats, blk, ab, dtypes)
    if small:
        keep, send = q_terms
        total = keep + lax.ppermute(send, "pair", PAIR).astype(jnp.float32)
        to_mine = total[:2].astype(jnp.bfloat16)
        to_far = total[2].astype(jnp.bfloat16)
        got_far = lax.ppermute(to_far, RP, far)
        got_mine = lax.ppermute(to_mine, RP, cross)
        got_other = lax.ppermute(got_mine[1], "pair", PAIR)
        wide = lambda value: value.astype(jnp.float32)
        query_grad = total[3] + wide(got_far) + wide(got_mine[0]) + wide(got_other)
    else:
        query_grad = lax.psum_scatter(
            q_terms[0].reshape(tables * TEST, features), RP, scatter_dimension=0, tiled=True
        )
    key_grad, value_grad = row_grads(qgt, c, d, e_all, u_all)
    return query_grad.astype(jnp.bfloat16), key_grad, value_grad


def solution(mesh):
    sizes = mesh.shape
    tables_of_rows = P(("groups", "rows", "pair"), "mp")
    in_specs = (tables_of_rows,) * 4 + (P("groups"),) * 3
    out_specs = (tables_of_rows,) * 3

    def run(query_rows, *rest):
        local_rows = query_rows.shape[0] // (sizes["groups"] * sizes["rows"] * sizes["pair"])
        small = sizes["rows"] == 4 and sizes["pair"] == 2 and local_rows == TEST
        return jax.shard_map(
            lambda *args: local(small, *args),
            mesh=mesh,
            in_specs=in_specs,
            out_specs=out_specs,
            check_vma=False,
        )(query_rows, *rest)

    return run
```

```python
import math

import jax
import jax.numpy as jnp
from jax import lax
from jax.experimental import pallas as pl
from jax.experimental.pallas import tpu as pltpu
from jax.sharding import PartitionSpec as P

HD = 64
TEST = 128
BLK = 512
LANES = 128
WIDE = 2 * TEST

NEG = -1e30
SCORE_SCALE = 1.0 / math.sqrt(HD)
LOG2_SCALE = SCORE_SCALE * math.log2(math.e)
RP = ("rows", "pair")
PAIR = [(0, 1), (1, 0)]


def table_lookup(positions, entries):
    matches = positions[:, None] == jnp.arange(entries.shape[0], dtype=jnp.int32)[None, :]
    return jnp.sum(jnp.where(matches, entries[None, :], 0), axis=1)


def params(mib):
    return pltpu.CompilerParams(vmem_limit_bytes=mib * 1024 * 1024)


def two_heads(rows):
    feature = lax.broadcasted_iota(jnp.int32, rows.shape, 0)
    zero = jnp.zeros_like(rows)
    return jnp.concatenate(
        [jnp.where(feature < HD, rows, zero), jnp.where(feature < HD, zero, rows)], axis=1
    )


def pack_kernel(query_ref, grad_ref, out_ref, sem):
    first = pltpu.make_async_copy(query_ref, out_ref.at[0, 0], sem.at[0])
    second = pltpu.make_async_copy(grad_ref, out_ref.at[0, 1], sem.at[1])
    first.start()
    second.start()
    first.wait()
    second.wait()


def pack(query_rows, cotangent):
    rows, features = query_rows.shape
    hbm = pl.BlockSpec(memory_space=pltpu.HBM)
    return pl.pallas_call(
        pack_kernel,
        in_specs=[hbm, hbm],
        out_specs=pl.BlockSpec(memory_space=pltpu.VMEM),
        out_shape=jax.ShapeDtypeStruct((1, 2, rows, features), query_rows.dtype),
        scratch_shapes=[pltpu.SemaphoreType.DMA((2,))],
        name="pack",
    )(query_rows, cotangent)


def scores_kernel(count, owner, live, testn, slot, table_of, *refs):
    pieces = refs[:count]
    key_hbm, value_hbm = refs[count : count + 2]
    qgt_ref, e_ref, u_ref, ab_ref, blk_ref, tab_ref, key_s, value_s, sem = refs[count + 2 :]
    blocks, _, features = key_s.shape

    def fetch(b):
        rows = pl.ds(b * BLK, BLK)
        return (
            pltpu.make_async_copy(key_hbm.at[rows], key_s.at[b], sem.at[0, b]),
            pltpu.make_async_copy(value_hbm.at[rows], value_s.at[b], sem.at[1, b]),
        )

    for b in range(blocks):
        for copy in fetch(b):
            copy.start()
    tab_ref[0] = jnp.full(tab_ref.shape[1:], NEG, jnp.float32)
    tab_ref[1] = jnp.zeros(tab_ref.shape[1:], jnp.float32)
    tab_ref[2] = jnp.zeros(tab_ref.shape[1:], jnp.float32)
    query = lax.broadcasted_iota(jnp.int32, (features, TEST), 1)
    at_slot = 0
    for piece in pieces:
        for n in range(piece.shape[0]):
            grads = piece[n, 1].T
            qgt_ref[at_slot, :features, :] = piece[n, 0].T
            qgt_ref[at_slot, features:, :] = jnp.where(
                query < testn[table_of[at_slot]], grads, jnp.zeros_like(grads)
            )
            at_slot += 1

    def block(b, carry):
        for copy in fetch(b):
            copy.wait()
        table = owner[b]
        at_slot = slot[table]
        key_live = lax.broadcasted_iota(jnp.int32, (BLK, WIDE), 0) < live[b]
        for p in range(features // LANES):
            at = slice(p * LANES, (p + 1) * LANES)
            wide = slice(p * WIDE, (p + 1) * WIDE)
            q_t = qgt_ref[at_slot, at, :]
            g_t = qgt_ref[at_slot, features + p * LANES : features + (p + 1) * LANES, :]
            keys = key_s[b, :, at]
            scores = jnp.dot(keys, two_heads(q_t), preferred_element_type=jnp.float32)
            dprobs = jnp.dot(value_s[b, :, at], two_heads(g_t), preferred_element_type=jnp.float32)
            scores = jnp.where(key_live, scores, NEG)
            peak = jnp.max(scores, axis=0, keepdims=True) * LOG2_SCALE
            weights = jnp.exp2(scores * LOG2_SCALE - peak)
            mass = jnp.sum(weights, axis=0, keepdims=True)
            part = jnp.sum(weights * dprobs, axis=0, keepdims=True)
            low = weights.astype(jnp.bfloat16)
            moved = (weights * (dprobs - part / mass)).astype(jnp.bfloat16)
            e_ref[b, :, wide] = low
            u_ref[b, :, wide] = moved
            for n, value in enumerate((moved, low)):
                product = lax.dot_general(
                    keys, value, (((0,), (0,)), ((), ())), preferred_element_type=jnp.float32
                )
                ab_ref[b, n, p * LANES : p * LANES + HD, :] = product[:HD, :TEST]
                ab_ref[b, n, p * LANES + HD : (p + 1) * LANES, :] = product[HD:, TEST:]
            blk_ref[0, pl.ds(b, 1), wide] = peak
            blk_ref[1, pl.ds(b, 1), wide] = mass
            blk_ref[2, pl.ds(b, 1), wide] = part
            old = tab_ref[0, pl.ds(table, 1), wide]
            new = jnp.maximum(old, peak)
            old_weight = jnp.exp2(old - new)
            new_weight = jnp.exp2(peak - new)
            tab_ref[0, pl.ds(table, 1), wide] = new
            tab_ref[1, pl.ds(table, 1), wide] = (
                tab_ref[1, pl.ds(table, 1), wide] * old_weight + mass * new_weight
            )
            tab_ref[2, pl.ds(table, 1), wide] = (
                tab_ref[2, pl.ds(table, 1), wide] * old_weight + part * new_weight
            )
        return carry

    lax.fori_loop(0, blocks, block, 0)


def block_scores(owner, live, testn, slot, table_of, pieces, key_rows, value_rows):
    features = key_rows.shape[1]
    blocks = owner.shape[0]
    tables = testn.shape[0]
    stacked = features // HD * TEST
    vmem = pl.BlockSpec(memory_space=pltpu.VMEM)
    smem = pl.BlockSpec(memory_space=pltpu.SMEM)
    hbm = pl.BlockSpec(memory_space=pltpu.HBM)
    return pl.pallas_call(
        lambda *refs: scores_kernel(len(pieces), *refs),
        in_specs=[smem] * 5 + [vmem] * len(pieces) + [hbm, hbm],
        out_specs=[vmem] * 6,
        out_shape=[
            pltpu.VMEM((tables, 2 * features, TEST), jnp.bfloat16),
            pltpu.VMEM((blocks, BLK, stacked), jnp.bfloat16),
            pltpu.VMEM((blocks, BLK, stacked), jnp.bfloat16),
            pltpu.VMEM((blocks, 2, features, TEST), jnp.float32),
            pltpu.VMEM((3, blocks, stacked), jnp.float32),
            jax.ShapeDtypeStruct((3, tables, stacked), jnp.float32),
        ],
        scratch_shapes=[
            pltpu.VMEM((blocks, BLK, features), jnp.bfloat16),
            pltpu.VMEM((blocks, BLK, features), jnp.bfloat16),
            pltpu.SemaphoreType.DMA((2, blocks)),
        ],
        compiler_params=params(40),
        name="block_scores",
    )(owner, live, testn, slot, table_of, *pieces, key_rows, value_rows)


def merged(pieces):
    peak = pieces[0][0]
    for piece in pieces[1:]:
        peak = jnp.maximum(peak, piece[0])
    mass = part = 0.0
    for piece in pieces:
        weight = jnp.exp2(piece[0] - peak)
        mass = mass + piece[1] * weight
        part = part + piece[2] * weight
    return peak, mass, part


def query_grad_kernel(features, count, owner, slot, *refs):
    pieces = refs[:count]
    blk_ref, ab_ref = refs[count : count + 2]
    outs = refs[count + 2 : -2]
    c_ref, d_ref, *q_refs = outs
    tab_s, acc_s = refs[-2:]
    blocks = blk_ref.shape[1]
    tab_s[0], tab_s[1], tab_s[2] = merged(
        [piece.at[n] for piece in pieces for n in range(piece.shape[0])]
    )
    acc_s[...] = jnp.zeros_like(acc_s)
    for b in range(blocks):
        table = owner[b]
        at = slot[table]
        mass = tab_s[1, pl.ds(table, 1), :]
        c = jnp.exp2(blk_ref[0, b : b + 1, :] - tab_s[0, pl.ds(table, 1), :]) / mass
        shift = blk_ref[2, b : b + 1, :] / blk_ref[1, b : b + 1, :]
        d = c * (shift - tab_s[2, pl.ds(table, 1), :] / mass)
        c_ref[b : b + 1, :] = c
        d_ref[b : b + 1, :] = d
        for h in range(features // HD):
            rows = slice(h * HD, (h + 1) * HD)
            lanes = slice(h * TEST, (h + 1) * TEST)
            acc_s[at, rows, :] += c[:, lanes] * ab_ref[b, 0, rows, :] + d[:, lanes] * ab_ref[b, 1, rows, :]
    tables = acc_s.shape[0]
    per = tables // len(q_refs)
    for n in range(tables):
        ref = q_refs[n // per]
        ref[n % per] = (acc_s[n] * SCORE_SCALE).T.astype(ref.dtype)


def query_grads(owner, slot, pieces, blk, ab, q_dtypes):
    blocks, _, features, _ = ab.shape
    tables = slot.shape[0]
    stacked = blk.shape[2]
    per = tables // len(q_dtypes)
    vmem = pl.BlockSpec(memory_space=pltpu.VMEM)
    smem = pl.BlockSpec(memory_space=pltpu.SMEM)
    return pl.pallas_call(
        lambda *refs: query_grad_kernel(features, len(pieces), *refs),
        in_specs=[smem, smem] + [vmem] * (len(pieces) + 2),
        out_specs=[vmem] * (2 + len(q_dtypes)),
        out_shape=[
            pltpu.VMEM((blocks, stacked), jnp.float32),
            pltpu.VMEM((blocks, stacked), jnp.float32),
        ]
        + [jax.ShapeDtypeStruct((per, TEST, features), dtype) for dtype in q_dtypes],
        scratch_shapes=[
            pltpu.VMEM((3, tables, stacked), jnp.float32),
            pltpu.VMEM((tables, features, TEST), jnp.float32),
        ],
        compiler_params=params(32),
        name="query_grads",
    )(owner, slot, *pieces, blk, ab)


def row_grads_kernel(owner, slot, qgt_ref, c_ref, d_ref, e_ref, u_ref, dk_hbm, dv_hbm, dk_s, dv_s, sem):
    blocks, _, features = dk_s.shape
    turned = (((1,), (1,)), ((), ()))

    def flush(b):
        rows = pl.ds(b * BLK, BLK)
        return (
            pltpu.make_async_copy(dk_s.at[b], dk_hbm.at[rows], sem.at[0, b]),
            pltpu.make_async_copy(dv_s.at[b], dv_hbm.at[rows], sem.at[1, b]),
        )

    def block(b, carry):
        at_slot = slot[owner[b]]
        for p in range(features // LANES):
            at = slice(p * LANES, (p + 1) * LANES)
            wide = slice(p * WIDE, (p + 1) * WIDE)
            c = c_ref[pl.ds(b, 1), wide]
            d = d_ref[pl.ds(b, 1), wide]
            q_t = two_heads(qgt_ref[at_slot, at, :].astype(jnp.float32))
            g_t = two_heads(
                qgt_ref[at_slot, features + p * LANES : features + (p + 1) * LANES, :].astype(jnp.float32)
            )
            for_u = (q_t * (c * SCORE_SCALE)).astype(jnp.bfloat16)
            for_e = jnp.concatenate([g_t * c, q_t * (d * SCORE_SCALE)], axis=0).astype(jnp.bfloat16)
            from_e = lax.dot_general(
                e_ref[b, :, wide], for_e, turned, preferred_element_type=jnp.float32
            )
            from_u = lax.dot_general(
                u_ref[b, :, wide], for_u, turned, preferred_element_type=jnp.float32
            )
            dv_s[b, :, at] = from_e[:, :LANES].astype(jnp.bfloat16)
            dk_s[b, :, at] = (from_u + from_e[:, LANES:]).astype(jnp.bfloat16)
        for copy in flush(b):
            copy.start()
        return carry

    lax.fori_loop(0, blocks, block, 0)
    for b in range(blocks):
        for copy in flush(b):
            copy.wait()


def row_grads(owner, slot, qgt, c, d, e_all, u_all):
    blocks, _, stacked = e_all.shape
    features = qgt.shape[1] // 2
    vmem = pl.BlockSpec(memory_space=pltpu.VMEM)
    smem = pl.BlockSpec(memory_space=pltpu.SMEM)
    hbm = pl.BlockSpec(memory_space=pltpu.HBM)
    return pl.pallas_call(
        row_grads_kernel,
        in_specs=[smem] * 2 + [vmem] * 5,
        out_specs=[hbm, hbm],
        out_shape=[jax.ShapeDtypeStruct((blocks * BLK, features), jnp.bfloat16)] * 2,
        scratch_shapes=[
            pltpu.VMEM((blocks, BLK, features), jnp.bfloat16),
            pltpu.VMEM((blocks, BLK, features), jnp.bfloat16),
            pltpu.SemaphoreType.DMA((2, blocks)),
        ],
        compiler_params=params(32),
        name="row_grads",
    )(owner, slot, qgt, c, d, e_all, u_all)


def local(small, query_rows, key_rows, value_rows, cotangent, train_rows, test_rows, block_table):
    chip = lax.axis_index("rows").astype(jnp.int32)
    core = lax.axis_index("pair").astype(jnp.int32)
    device = lax.axis_index(RP).astype(jnp.int32)
    local_rows, features = query_rows.shape
    blocks = key_rows.shape[0] // BLK
    tables = train_rows.shape[0]

    my_blocks = device * blocks + jnp.arange(blocks, dtype=jnp.int32)
    block_ids = jnp.arange(block_table.shape[0], dtype=jnp.int32)
    owner = lax.dynamic_slice_in_dim(block_table, device * blocks, blocks)
    earlier = (block_table[None, :] == owner[:, None]) & (block_ids[None, :] < my_blocks[:, None])
    ordinal = jnp.sum(jnp.where(earlier, 1, 0), axis=1).astype(jnp.int32)
    live = jnp.minimum(table_lookup(owner, train_rows) - ordinal * BLK, BLK).astype(jnp.int32)
    ids = jnp.arange(tables, dtype=jnp.int32)

    both = pack(query_rows, cotangent)
    if small:
        pair = lambda value: lax.ppermute(value, "pair", PAIR)
        step = lambda value, s: lax.ppermute(value, "rows", [(z, z ^ s) for z in range(4)])
        cross = [(2 * z + c, 2 * (z ^ (1 + c)) + c) for z in range(4) for c in range(2)]
        mine = chip ^ (1 + core)
        other = chip ^ (2 - core)
        table_chip, table_core = ids // 2, ids % 2
        not_mine = jnp.where(table_core == core, 0, 1)
        slot_in = 2 * (table_chip ^ chip) + not_mine
        table_of = 2 * (chip ^ (ids // 2)) + (core ^ (ids % 2))
        slot_out = jnp.where(
            table_chip == mine,
            not_mine,
            jnp.where(
                table_chip == other,
                5 - not_mine,
                jnp.where(table_chip == chip, 3 + 4 * not_mine, 2 + 4 * not_mine),
            ),
        ).astype(jnp.int32)
        pieces = []
        for value in [both] + [step(both, s) for s in (1, 2, 3)]:
            pieces += [value, pair(value)]
    else:
        slot_in = slot_out = table_of = ids
        everyone = lax.all_gather(both[0], RP, axis=1, tiled=True)
        pieces = [everyone.reshape(2, tables, TEST, features).swapaxes(0, 1)]

    qgt, e_all, u_all, ab, blk, tab = block_scores(
        owner, live, test_rows, slot_in, table_of, pieces, key_rows, value_rows
    )
    if small:
        tab = tab[None]
        far_tab = step(tab, 3)
        chip_tab = lax.all_gather(tab, "pair", axis=0, tiled=True)
        mine_tab = lax.ppermute(chip_tab, RP, cross)
        stats = [chip_tab, far_tab, pair(far_tab), mine_tab, pair(mine_tab)]
        dtypes = [jnp.float32, jnp.bfloat16]
    else:
        peak = lax.pmax(tab[0], RP)
        sums = lax.psum(tab[1:] * jnp.exp2(tab[0] - peak)[None], RP)
        stats = [jnp.concatenate([peak[None], sums], axis=0)[None]]
        dtypes = [jnp.float32]
    c, d, *q_terms = query_grads(owner, slot_out, stats, blk, ab, dtypes)
    if small:
        keep, send = q_terms
        total = keep + pair(send).astype(jnp.float32)
        to_mine = total[:2].astype(jnp.bfloat16)
        to_far = total[2].astype(jnp.bfloat16)
        got_far = step(to_far, 3)
        got_mine = lax.ppermute(to_mine, RP, cross)
        key_grad, value_grad = row_grads(owner, slot_in, qgt, c, d, e_all, u_all)
        got_mine, key_grad = lax.optimization_barrier((got_mine, key_grad))
        got_other = pair(got_mine[1])
        wide = lambda value: value.astype(jnp.float32)
        query_grad = total[3] + wide(got_far) + wide(got_mine[0]) + wide(got_other)
    else:
        query_grad = lax.psum_scatter(
            q_terms[0].reshape(tables * TEST, features), RP, scatter_dimension=0, tiled=True
        )
        key_grad, value_grad = row_grads(owner, slot_in, qgt, c, d, e_all, u_all)
    return query_grad.astype(jnp.bfloat16), key_grad, value_grad


def solution(mesh):
    sizes = mesh.shape
    tables_of_rows = P(("groups", "rows", "pair"), "mp")
    in_specs = (tables_of_rows,) * 4 + (P("groups"),) * 3
    out_specs = (tables_of_rows,) * 3

    def run(query_rows, *rest):
        local_rows = query_rows.shape[0] // (sizes["groups"] * sizes["rows"] * sizes["pair"])
        small = sizes["rows"] == 4 and sizes["pair"] == 2 and local_rows == TEST
        return jax.shard_map(
            lambda *args: local(small, *args),
            mesh=mesh,
            in_specs=in_specs,
            out_specs=out_specs,
            check_vma=False,
        )(query_rows, *rest)

    return run
```

```python
import math

import jax
import jax.numpy as jnp
from jax import lax
from jax.experimental import pallas as pl
from jax.experimental.pallas import tpu as pltpu
from jax.sharding import PartitionSpec as P

HD = 64
TEST = 128
BLK = 512
LANES = 128
WIDE = 2 * TEST

NEG = -1e30
SCORE_SCALE = 1.0 / math.sqrt(HD)
LOG2_SCALE = SCORE_SCALE * math.log2(math.e)
RP = ("rows", "pair")
PAIR = [(0, 1), (1, 0)]


def table_lookup(positions, entries):
    matches = positions[:, None] == jnp.arange(entries.shape[0], dtype=jnp.int32)[None, :]
    return jnp.sum(jnp.where(matches, entries[None, :], 0), axis=1)


def params(mib):
    return pltpu.CompilerParams(vmem_limit_bytes=mib * 1024 * 1024)


def two_heads(rows):
    feature = lax.broadcasted_iota(jnp.int32, rows.shape, 0)
    zero = jnp.zeros_like(rows)
    return jnp.concatenate(
        [jnp.where(feature < HD, rows, zero), jnp.where(feature < HD, zero, rows)], axis=1
    )


def every_copy(copies):
    for copy in copies:
        copy.start()
    return copies


def scores_kernel(count, held, meta, *refs):
    query_pieces, grad_pieces = refs[:count], refs[count : 2 * count]
    key_hbm, value_hbm = refs[2 * count : 2 * count + 2]
    qgt_hbm, e_hbm, u_hbm, blk_hbm, tab_ref = refs[2 * count + 2 : 2 * count + 7]
    qgt_s, e_s, u_s, blk_s, key_s, value_s, held_s, in_sem, out_sem, held_sem, small_sem = refs[
        2 * count + 7 :
    ]
    blocks, _, features = key_s.shape
    tables = qgt_s.shape[0]
    early = every_copy(
        [
            pltpu.make_async_copy(pieces[n], held_s.at[n, m], held_sem.at[n, m])
            for n in range(held)
            for m, pieces in enumerate((query_pieces, grad_pieces))
        ]
    )
    loads = []
    for b in range(blocks):
        rows = pl.ds(b * BLK, BLK)
        loads.append(
            every_copy(
                [
                    pltpu.make_async_copy(key_hbm.at[rows], key_s.at[b], in_sem.at[0, b]),
                    pltpu.make_async_copy(value_hbm.at[rows], value_s.at[b], in_sem.at[1, b]),
                ]
            )
        )
    tab_ref[0] = jnp.full(tab_ref.shape[1:], NEG, jnp.float32)
    tab_ref[1] = jnp.zeros(tab_ref.shape[1:], jnp.float32)
    tab_ref[2] = jnp.zeros(tab_ref.shape[1:], jnp.float32)
    query = lax.broadcasted_iota(jnp.int32, (features, TEST), 1)

    def turn(at_slot, queries, grads):
        grads = grads.T
        qgt_s[at_slot, :features, :] = queries.T
        qgt_s[at_slot, features:, :] = jnp.where(
            query < meta[TESTN, meta[TABLE_OF, at_slot]], grads, jnp.zeros_like(grads)
        )

    per = tables // count
    for n in range(held, count):
        for m in range(per):
            rows = slice(m * TEST, (m + 1) * TEST)
            turn(n * per + m, query_pieces[n][rows, :], grad_pieces[n][rows, :])
    for copy in early:
        copy.wait()
    for n in range(held):
        turn(n, held_s[n, 0], held_s[n, 1])
    stores = every_copy([pltpu.make_async_copy(qgt_s, qgt_hbm, small_sem.at[0])])

    for b in range(blocks):
        for copy in loads[b]:
            copy.wait()
        table = meta[OWNER, b]
        at_slot = meta[SLOT_IN, table]
        key_live = lax.broadcasted_iota(jnp.int32, (BLK, WIDE), 0) < meta[LIVE, b]
        for p in range(features // LANES):
            at = slice(p * LANES, (p + 1) * LANES)
            wide = slice(p * WIDE, (p + 1) * WIDE)
            q_t = qgt_s[at_slot, at, :]
            g_t = qgt_s[at_slot, features + p * LANES : features + (p + 1) * LANES, :]
            scores = jnp.dot(key_s[b, :, at], two_heads(q_t), preferred_element_type=jnp.float32)
            dprobs = jnp.dot(value_s[b, :, at], two_heads(g_t), preferred_element_type=jnp.float32)
            scores = jnp.where(key_live, scores, NEG)
            peak = jnp.max(scores, axis=0, keepdims=True) * LOG2_SCALE
            weights = jnp.exp2(scores * LOG2_SCALE - peak)
            mass = jnp.sum(weights, axis=0, keepdims=True)
            part = jnp.sum(weights * dprobs, axis=0, keepdims=True)
            e_s[b, :, wide] = weights.astype(jnp.bfloat16)
            u_s[b, :, wide] = (weights * (dprobs - part / mass)).astype(jnp.bfloat16)
            blk_s[0, b : b + 1, wide] = peak
            blk_s[1, b : b + 1, wide] = mass
            blk_s[2, b : b + 1, wide] = part
            old = tab_ref[0, pl.ds(table, 1), wide]
            new = jnp.maximum(old, peak)
            old_weight = jnp.exp2(old - new)
            new_weight = jnp.exp2(peak - new)
            tab_ref[0, pl.ds(table, 1), wide] = new
            tab_ref[1, pl.ds(table, 1), wide] = (
                tab_ref[1, pl.ds(table, 1), wide] * old_weight + mass * new_weight
            )
            tab_ref[2, pl.ds(table, 1), wide] = (
                tab_ref[2, pl.ds(table, 1), wide] * old_weight + part * new_weight
            )
        stores += every_copy(
            [
                pltpu.make_async_copy(e_s.at[b], e_hbm.at[b], out_sem.at[0, b]),
                pltpu.make_async_copy(u_s.at[b], u_hbm.at[b], out_sem.at[1, b]),
            ]
        )
    stores += every_copy([pltpu.make_async_copy(blk_s, blk_hbm, small_sem.at[1])])
    for copy in stores:
        copy.wait()


OWNER, LIVE, TESTN, SLOT_IN, TABLE_OF, SLOT_OUT = range(6)


def vmem_spec():
    return pl.BlockSpec(memory_space=pltpu.VMEM)


def smem_spec():
    return pl.BlockSpec(memory_space=pltpu.SMEM)


def hbm_spec():
    return pl.BlockSpec(memory_space=pltpu.HBM)


def in_hbm(value):
    return pltpu.with_memory_space_constraint(value, pltpu.HBM)


def block_scores(meta, tables, held, query_pieces, grad_pieces, key_rows, value_rows):
    features = key_rows.shape[1]
    blocks = key_rows.shape[0] // BLK
    stacked = features // HD * TEST
    count = len(query_pieces)
    pieces = []
    for group in (query_pieces, grad_pieces):
        pieces += [in_hbm(piece) if n < held else piece for n, piece in enumerate(group)]
    specs = [hbm_spec() if n % count < held else vmem_spec() for n in range(2 * count)]
    weights = (blocks, BLK, stacked)
    turned = (tables, 2 * features, TEST)
    return pl.pallas_call(
        lambda *refs: scores_kernel(count, held, *refs),
        in_specs=[smem_spec()] + specs + [hbm_spec()] * 2,
        out_specs=[hbm_spec()] * 4 + [vmem_spec()],
        out_shape=[
            pltpu.HBM(turned, jnp.bfloat16),
            pltpu.HBM(weights, jnp.bfloat16),
            pltpu.HBM(weights, jnp.bfloat16),
            pltpu.HBM((3, blocks, stacked), jnp.float32),
            jax.ShapeDtypeStruct((3, tables, stacked), jnp.float32),
        ],
        scratch_shapes=[
            pltpu.VMEM(turned, jnp.bfloat16),
            pltpu.VMEM(weights, jnp.bfloat16),
            pltpu.VMEM(weights, jnp.bfloat16),
            pltpu.VMEM((3, blocks, stacked), jnp.float32),
            pltpu.VMEM((blocks, BLK, features), jnp.bfloat16),
            pltpu.VMEM((blocks, BLK, features), jnp.bfloat16),
            pltpu.VMEM((max(held, 1), 2, TEST, features), jnp.bfloat16),
            pltpu.SemaphoreType.DMA((2, blocks)),
            pltpu.SemaphoreType.DMA((2, blocks)),
            pltpu.SemaphoreType.DMA((max(held, 1), 2)),
            pltpu.SemaphoreType.DMA((2,)),
        ],
        compiler_params=params(28),
        name="block_scores",
    )(meta, *pieces, in_hbm(key_rows), in_hbm(value_rows))


def query_sums_kernel(key_hbm, e_hbm, u_hbm, blk_hbm, ab_ref, blk_ref, key_s, e_s, u_s, sem, blk_sem):
    blocks, _, features = key_s.shape
    first = every_copy([pltpu.make_async_copy(blk_hbm, blk_ref, blk_sem.at[0])])
    loads = []
    for b in range(blocks):
        loads.append(
            every_copy(
                [
                    pltpu.make_async_copy(key_hbm.at[pl.ds(b * BLK, BLK)], key_s.at[b], sem.at[0, b]),
                    pltpu.make_async_copy(u_hbm.at[b], u_s.at[b], sem.at[1, b]),
                    pltpu.make_async_copy(e_hbm.at[b], e_s.at[b], sem.at[2, b]),
                ]
            )
        )
    for b in range(blocks):
        for copy in loads[b]:
            copy.wait()
        for p in range(features // LANES):
            wide = slice(p * WIDE, (p + 1) * WIDE)
            keys = key_s[b, :, p * LANES : (p + 1) * LANES]
            for n, ref in enumerate((u_s, e_s)):
                product = lax.dot_general(
                    keys, ref[b, :, wide], (((0,), (0,)), ((), ())), preferred_element_type=jnp.float32
                )
                ab_ref[b, n, p * LANES : p * LANES + HD, :] = product[:HD, :TEST]
                ab_ref[b, n, p * LANES + HD : (p + 1) * LANES, :] = product[HD:, TEST:]
    for copy in first:
        copy.wait()


def query_sums(key_rows, e_all, u_all, blk):
    features = key_rows.shape[1]
    blocks, _, stacked = e_all.shape
    return pl.pallas_call(
        query_sums_kernel,
        in_specs=[hbm_spec()] * 4,
        out_specs=[vmem_spec()] * 2,
        out_shape=[
            pltpu.VMEM((blocks, 2, features, TEST), jnp.float32),
            pltpu.VMEM(blk.shape, jnp.float32),
        ],
        scratch_shapes=[
            pltpu.VMEM((blocks, BLK, features), jnp.bfloat16),
            pltpu.VMEM((blocks, BLK, stacked), jnp.bfloat16),
            pltpu.VMEM((blocks, BLK, stacked), jnp.bfloat16),
            pltpu.SemaphoreType.DMA((3, blocks)),
            pltpu.SemaphoreType.DMA((1,)),
        ],
        compiler_params=params(20),
        name="query_sums",
    )(in_hbm(key_rows), in_hbm(e_all), in_hbm(u_all), in_hbm(blk))


def merged(pieces):
    peak = pieces[0][0]
    for piece in pieces[1:]:
        peak = jnp.maximum(peak, piece[0])
    mass = part = 0.0
    for piece in pieces:
        weight = jnp.exp2(piece[0] - peak)
        mass = mass + piece[1] * weight
        part = part + piece[2] * weight
    return peak, mass, part


def query_grad_kernel(count, meta, *refs):
    pieces = refs[:count]
    blk_ref, ab_ref = refs[count : count + 2]
    c_ref, d_ref, *q_refs = refs[count + 2 : -2]
    tab_s, acc_s = refs[-2:]
    blocks = blk_ref.shape[1]
    tables, features, _ = acc_s.shape
    tab_s[0], tab_s[1], tab_s[2] = merged(pieces)
    acc_s[...] = jnp.zeros_like(acc_s)
    for b in range(blocks):
        table = meta[OWNER, b]
        at = meta[SLOT_OUT, table]
        mass = tab_s[1, pl.ds(table, 1), :]
        c = jnp.exp2(blk_ref[0, b : b + 1, :] - tab_s[0, pl.ds(table, 1), :]) / mass
        shift = blk_ref[2, b : b + 1, :] / blk_ref[1, b : b + 1, :]
        d = c * (shift - tab_s[2, pl.ds(table, 1), :] / mass)
        c_ref[b : b + 1, :] = c
        d_ref[b : b + 1, :] = d
        for h in range(features // HD):
            rows = slice(h * HD, (h + 1) * HD)
            lanes = slice(h * TEST, (h + 1) * TEST)
            acc_s[at, rows, :] += c[:, lanes] * ab_ref[b, 0, rows, :] + d[:, lanes] * ab_ref[b, 1, rows, :]
    per = tables // len(q_refs)
    for n in range(tables):
        ref = q_refs[n // per]
        ref[n % per] = (acc_s[n] * SCORE_SCALE).T.astype(ref.dtype)


def query_grads(meta, tables, pieces, blk, ab, q_dtypes):
    blocks, _, features, _ = ab.shape
    stacked = blk.shape[2]
    per = tables // len(q_dtypes)
    return pl.pallas_call(
        lambda *refs: query_grad_kernel(len(pieces), *refs),
        in_specs=[smem_spec()] + [vmem_spec()] * (len(pieces) + 2),
        out_specs=[vmem_spec()] * (2 + len(q_dtypes)),
        out_shape=[
            jax.ShapeDtypeStruct((blocks, stacked), jnp.float32),
            jax.ShapeDtypeStruct((blocks, stacked), jnp.float32),
        ]
        + [jax.ShapeDtypeStruct((per, TEST, features), dtype) for dtype in q_dtypes],
        scratch_shapes=[
            pltpu.VMEM((3, tables, stacked), jnp.float32),
            pltpu.VMEM((tables, features, TEST), jnp.float32),
        ],
        compiler_params=params(10),
        name="query_grads",
    )(meta, *pieces, blk, ab)


def row_grads_kernel(meta, c_ref, d_ref, qgt_hbm, e_hbm, u_hbm, dk_hbm, dv_hbm, *scratch):
    qgt_s, e_s, u_s, dk_s, dv_s, in_sem, out_sem, qgt_sem = scratch
    blocks, _, features = dk_s.shape
    turned = (((1,), (1,)), ((), ()))
    first = every_copy([pltpu.make_async_copy(qgt_hbm, qgt_s, qgt_sem.at[0])])
    loads = []
    for b in range(blocks):
        loads.append(
            every_copy(
                [
                    pltpu.make_async_copy(e_hbm.at[b], e_s.at[b], in_sem.at[0, b]),
                    pltpu.make_async_copy(u_hbm.at[b], u_s.at[b], in_sem.at[1, b]),
                ]
            )
        )
    for copy in first:
        copy.wait()
    stores = []
    for b in range(blocks):
        at_slot = meta[SLOT_IN, meta[OWNER, b]]
        for copy in loads[b]:
            copy.wait()
        for p in range(features // LANES):
            at = slice(p * LANES, (p + 1) * LANES)
            wide = slice(p * WIDE, (p + 1) * WIDE)
            c = c_ref[b : b + 1, wide]
            d = d_ref[b : b + 1, wide]
            q_t = two_heads(qgt_s[at_slot, at, :].astype(jnp.float32))
            g_t = two_heads(
                qgt_s[at_slot, features + p * LANES : features + (p + 1) * LANES, :].astype(jnp.float32)
            )
            for_u = (q_t * (c * SCORE_SCALE)).astype(jnp.bfloat16)
            for_e = jnp.concatenate([g_t * c, q_t * (d * SCORE_SCALE)], axis=0).astype(jnp.bfloat16)
            from_e = lax.dot_general(
                e_s[b, :, wide], for_e, turned, preferred_element_type=jnp.float32
            )
            from_u = lax.dot_general(
                u_s[b, :, wide], for_u, turned, preferred_element_type=jnp.float32
            )
            dv_s[b, :, at] = from_e[:, :LANES].astype(jnp.bfloat16)
            dk_s[b, :, at] = (from_u + from_e[:, LANES:]).astype(jnp.bfloat16)
        rows = pl.ds(b * BLK, BLK)
        stores += every_copy(
            [
                pltpu.make_async_copy(dk_s.at[b], dk_hbm.at[rows], out_sem.at[0, b]),
                pltpu.make_async_copy(dv_s.at[b], dv_hbm.at[rows], out_sem.at[1, b]),
            ]
        )
    for copy in stores:
        copy.wait()


def row_grads(meta, c, d, qgt, e_all, u_all):
    blocks, _, stacked = e_all.shape
    features = qgt.shape[1] // 2
    return pl.pallas_call(
        row_grads_kernel,
        in_specs=[smem_spec()] + [vmem_spec()] * 2 + [hbm_spec()] * 3,
        out_specs=[hbm_spec()] * 2,
        out_shape=[jax.ShapeDtypeStruct((blocks * BLK, features), jnp.bfloat16)] * 2,
        scratch_shapes=[
            pltpu.VMEM(qgt.shape, jnp.bfloat16),
            pltpu.VMEM((blocks, BLK, stacked), jnp.bfloat16),
            pltpu.VMEM((blocks, BLK, stacked), jnp.bfloat16),
            pltpu.VMEM((blocks, BLK, features), jnp.bfloat16),
            pltpu.VMEM((blocks, BLK, features), jnp.bfloat16),
            pltpu.SemaphoreType.DMA((2, blocks)),
            pltpu.SemaphoreType.DMA((2, blocks)),
            pltpu.SemaphoreType.DMA((1,)),
        ],
        compiler_params=params(24),
        name="row_grads",
    )(meta, c, d, in_hbm(qgt), in_hbm(e_all), in_hbm(u_all))


def local(small, query_rows, key_rows, value_rows, cotangent, train_rows, test_rows, block_table):
    chip = lax.axis_index("rows").astype(jnp.int32)
    core = lax.axis_index("pair").astype(jnp.int32)
    device = lax.axis_index(RP).astype(jnp.int32)
    local_rows, features = query_rows.shape
    blocks = key_rows.shape[0] // BLK
    tables = train_rows.shape[0]

    my_blocks = device * blocks + jnp.arange(blocks, dtype=jnp.int32)
    block_ids = jnp.arange(block_table.shape[0], dtype=jnp.int32)
    owner = lax.dynamic_slice_in_dim(block_table, device * blocks, blocks)
    earlier = (block_table[None, :] == owner[:, None]) & (block_ids[None, :] < my_blocks[:, None])
    ordinal = jnp.sum(jnp.where(earlier, 1, 0), axis=1).astype(jnp.int32)
    live = jnp.minimum(table_lookup(owner, train_rows) - ordinal * BLK, BLK).astype(jnp.int32)
    ids = jnp.arange(tables, dtype=jnp.int32)

    pair = lambda value: lax.ppermute(value, "pair", PAIR)
    step = lambda value, s: lax.ppermute(value, "rows", [(z, z ^ s) for z in range(4)])
    if small:
        away = (ids // 2) ^ chip
        not_mine = (ids % 2) ^ core
        slot_in = 2 * away + not_mine
        table_of = 2 * (chip ^ (ids // 2)) + (core ^ (ids % 2))
        slot_out = 4 * not_mine + (away + 3) % 4
        held = 1

        def spread(value):
            pieces = []
            for near in [value] + [step(value, s) for s in (1, 2, 3)]:
                pieces += [near, pair(near)]
            return pieces

    else:
        slot_in = slot_out = table_of = ids
        held = 0
        spread = lambda value: [lax.all_gather(value, RP, axis=0, tiled=True)]

    pad = lambda values: jnp.pad(values, (0, max(blocks, tables) - values.shape[0]))
    meta = jnp.stack([pad(v) for v in (owner, live, test_rows, slot_in, table_of, slot_out)])
    qgt, e_all, u_all, blk, tab = block_scores(
        meta, tables, held, spread(query_rows), spread(cotangent), key_rows, value_rows
    )
    if small:
        stats = spread(tab)
        dtypes = [jnp.float32, jnp.bfloat16]
    else:
        peak = lax.pmax(tab[0], RP)
        sums = lax.psum(tab[1:] * jnp.exp2(tab[0] - peak)[None], RP)
        stats = [jnp.concatenate([peak[None], sums], axis=0)]
        dtypes = [jnp.float32]
    ab, blk = query_sums(key_rows, e_all, u_all, blk)
    c, d, *q_terms = query_grads(meta, tables, stats, blk, ab, dtypes)
    if small:
        keep, send = q_terms
        total = keep + pair(send).astype(jnp.float32)
        low = total.astype(jnp.bfloat16)
        got = [step(low[s - 1], s) for s in (1, 2, 3)]
        low, c = lax.optimization_barrier((low, c))
        key_grad, value_grad = row_grads(meta, c, d, qgt, e_all, u_all)
        query_grad = total[3]
        for value in got:
            query_grad = query_grad + value.astype(jnp.float32)
    else:
        query_grad = lax.psum_scatter(
            q_terms[0].reshape(tables * TEST, features), RP, scatter_dimension=0, tiled=True
        )
        key_grad, value_grad = row_grads(meta, c, d, qgt, e_all, u_all)
    return query_grad.astype(jnp.bfloat16), key_grad, value_grad


def solution(mesh):
    sizes = mesh.shape
    tables_of_rows = P(("groups", "rows", "pair"), "mp")
    in_specs = (tables_of_rows,) * 4 + (P("groups"),) * 3
    out_specs = (tables_of_rows,) * 3

    def run(query_rows, *rest):
        local_rows = query_rows.shape[0] // (sizes["groups"] * sizes["rows"] * sizes["pair"])
        small = sizes["rows"] == 4 and sizes["pair"] == 2 and local_rows == TEST
        return jax.shard_map(
            lambda *args: local(small, *args),
            mesh=mesh,
            in_specs=in_specs,
            out_specs=out_specs,
            check_vma=False,
        )(query_rows, *rest)

    return run
```

```python
import math

import jax
import jax.numpy as jnp
from jax import lax
from jax.experimental import pallas as pl
from jax.experimental.pallas import tpu as pltpu
from jax.sharding import PartitionSpec as P

HD = 64
TEST = 128
BLK = 512
LANES = 128
WIDE = 2 * TEST

NEG = -1e30
SCORE_SCALE = 1.0 / math.sqrt(HD)
LOG2_SCALE = SCORE_SCALE * math.log2(math.e)
RP = ("rows", "pair")
PAIR = [(0, 1), (1, 0)]


def params(mib):
    return pltpu.CompilerParams(vmem_limit_bytes=mib * 1024 * 1024)


def two_heads(rows):
    feature = lax.broadcasted_iota(jnp.int32, rows.shape, 0)
    zero = jnp.zeros_like(rows)
    return jnp.concatenate(
        [jnp.where(feature < HD, rows, zero), jnp.where(feature < HD, zero, rows)], axis=1
    )


def every_copy(copies):
    for copy in copies:
        copy.start()
    return copies


def scores_kernel(count, held, meta, *refs):
    query_pieces, grad_pieces = refs[:count], refs[count : 2 * count]
    key_hbm, value_hbm = refs[2 * count : 2 * count + 2]
    qgt_s, state, blk_hbm, tab_ref = refs[2 * count + 2 : 2 * count + 6]
    blk_s, value_s, held_s, in_sem, held_sem, small_sem = refs[2 * count + 6 :]
    blocks, _, features = value_s.shape
    stacked = features // HD * TEST
    tables = qgt_s.shape[0]
    early = every_copy(
        [
            pltpu.make_async_copy(pieces[n], held_s.at[n, m], held_sem.at[n, m])
            for n in range(held)
            for m, pieces in enumerate((query_pieces, grad_pieces))
        ]
    )
    loads = []
    for b in range(blocks):
        rows = pl.ds(b * BLK, BLK)
        loads.append(
            every_copy(
                [
                    pltpu.make_async_copy(
                        key_hbm.at[rows], state.at[b, :, pl.ds(2 * stacked, features)], in_sem.at[0, b]
                    ),
                    pltpu.make_async_copy(value_hbm.at[rows], value_s.at[b], in_sem.at[1, b]),
                ]
            )
        )
    tab_ref[0] = jnp.full(tab_ref.shape[1:], NEG, jnp.float32)
    tab_ref[1] = jnp.zeros(tab_ref.shape[1:], jnp.float32)
    tab_ref[2] = jnp.zeros(tab_ref.shape[1:], jnp.float32)
    query = lax.broadcasted_iota(jnp.int32, (features, TEST), 1)

    def turn(at_slot, queries, grads):
        grads = grads.T
        qgt_s[at_slot, :features, :] = queries.T
        qgt_s[at_slot, features:, :] = jnp.where(
            query < meta[TESTN, meta[TABLE_OF, at_slot]], grads, jnp.zeros_like(grads)
        )

    per = tables // count
    for n in range(held, count):
        for m in range(per):
            rows = slice(m * TEST, (m + 1) * TEST)
            turn(n * per + m, query_pieces[n][rows, :], grad_pieces[n][rows, :])
    for copy in early:
        copy.wait()
    for n in range(held):
        turn(n, held_s[n, 0], held_s[n, 1])

    for b in range(blocks):
        for copy in loads[b]:
            copy.wait()
        table = meta[OWNER, b]
        at_slot = meta[SLOT_IN, table]
        key_live = lax.broadcasted_iota(jnp.int32, (BLK, WIDE), 0) < meta[LIVE, b]
        for p in range(features // LANES):
            at = slice(p * LANES, (p + 1) * LANES)
            wide = slice(p * WIDE, (p + 1) * WIDE)
            q_t = qgt_s[at_slot, at, :]
            g_t = qgt_s[at_slot, features + p * LANES : features + (p + 1) * LANES, :]
            keys = state[b, :, 2 * stacked + p * LANES : 2 * stacked + (p + 1) * LANES]
            scores = jnp.dot(keys, two_heads(q_t), preferred_element_type=jnp.float32)
            dprobs = jnp.dot(value_s[b, :, at], two_heads(g_t), preferred_element_type=jnp.float32)
            scores = jnp.where(key_live, scores, NEG)
            peak = jnp.max(scores, axis=0, keepdims=True) * LOG2_SCALE
            weights = jnp.exp2(scores * LOG2_SCALE - peak)
            mass = jnp.sum(weights, axis=0, keepdims=True)
            part = jnp.sum(weights * dprobs, axis=0, keepdims=True)
            state[b, :, wide] = weights.astype(jnp.bfloat16)
            state[b, :, stacked + p * WIDE : stacked + (p + 1) * WIDE] = (
                weights * (dprobs - part / mass)
            ).astype(jnp.bfloat16)
            blk_s[0, b : b + 1, wide] = peak
            blk_s[1, b : b + 1, wide] = mass
            blk_s[2, b : b + 1, wide] = part
            old = tab_ref[0, pl.ds(table, 1), wide]
            new = jnp.maximum(old, peak)
            old_weight = jnp.exp2(old - new)
            new_weight = jnp.exp2(peak - new)
            tab_ref[0, pl.ds(table, 1), wide] = new
            tab_ref[1, pl.ds(table, 1), wide] = (
                tab_ref[1, pl.ds(table, 1), wide] * old_weight + mass * new_weight
            )
            tab_ref[2, pl.ds(table, 1), wide] = (
                tab_ref[2, pl.ds(table, 1), wide] * old_weight + part * new_weight
            )
    for copy in every_copy([pltpu.make_async_copy(blk_s, blk_hbm, small_sem.at[0])]):
        copy.wait()


OWNER, LIVE, TESTN, SLOT_IN, TABLE_OF, SLOT_OUT = range(6)


def vmem_spec():
    return pl.BlockSpec(memory_space=pltpu.VMEM)


def smem_spec():
    return pl.BlockSpec(memory_space=pltpu.SMEM)


def hbm_spec():
    return pl.BlockSpec(memory_space=pltpu.HBM)


def in_hbm(value):
    return pltpu.with_memory_space_constraint(value, pltpu.HBM)


def block_scores(meta, tables, held, query_pieces, grad_pieces, key_rows, value_rows):
    features = key_rows.shape[1]
    blocks = key_rows.shape[0] // BLK
    stacked = features // HD * TEST
    count = len(query_pieces)
    pieces = []
    for group in (query_pieces, grad_pieces):
        pieces += [in_hbm(piece) if n < held else piece for n, piece in enumerate(group)]
    specs = [hbm_spec() if n % count < held else vmem_spec() for n in range(2 * count)]
    state = (blocks, BLK, 2 * stacked + features)
    turned = (tables, 2 * features, TEST)
    return pl.pallas_call(
        lambda *refs: scores_kernel(count, held, *refs),
        in_specs=[smem_spec()] + specs + [hbm_spec()] * 2,
        out_specs=[vmem_spec(), vmem_spec(), hbm_spec(), vmem_spec()],
        out_shape=[
            pltpu.VMEM(turned, jnp.bfloat16),
            pltpu.VMEM(state, jnp.bfloat16),
            pltpu.HBM((3, blocks, stacked), jnp.float32),
            jax.ShapeDtypeStruct((3, tables, stacked), jnp.float32),
        ],
        scratch_shapes=[
            pltpu.VMEM((3, blocks, stacked), jnp.float32),
            pltpu.VMEM((blocks, BLK, features), jnp.bfloat16),
            pltpu.VMEM((max(held, 1), 2, TEST, features), jnp.bfloat16),
            pltpu.SemaphoreType.DMA((2, blocks)),
            pltpu.SemaphoreType.DMA((max(held, 1), 2)),
            pltpu.SemaphoreType.DMA((1,)),
        ],
        compiler_params=params(16),
        name="block_scores",
    )(meta, *pieces, in_hbm(key_rows), in_hbm(value_rows))


def query_sums_kernel(state, blk_hbm, ab_ref, blk_ref, state_out, blk_sem):
    blocks, _, features, _ = ab_ref.shape
    stacked = features // HD * TEST
    copy = pltpu.make_async_copy(blk_hbm, blk_ref, blk_sem.at[0])
    copy.start()
    for b in range(blocks):
        for p in range(features // LANES):
            keys = state[b, :, 2 * stacked + p * LANES : 2 * stacked + (p + 1) * LANES]
            for n, first in enumerate((stacked, 0)):
                values = state[b, :, first + p * WIDE : first + (p + 1) * WIDE]
                product = lax.dot_general(
                    keys, values, (((0,), (0,)), ((), ())), preferred_element_type=jnp.float32
                )
                ab_ref[b, n, p * LANES : p * LANES + HD, :] = product[:HD, :TEST]
                ab_ref[b, n, p * LANES + HD : (p + 1) * LANES, :] = product[HD:, TEST:]
    copy.wait()


def query_sums(features, state, blk):
    blocks = state.shape[0]
    return pl.pallas_call(
        query_sums_kernel,
        in_specs=[vmem_spec(), hbm_spec()],
        out_specs=[vmem_spec()] * 3,
        out_shape=[
            pltpu.VMEM((blocks, 2, features, TEST), jnp.float32),
            pltpu.VMEM(blk.shape, jnp.float32),
            pltpu.VMEM(state.shape, jnp.bfloat16),
        ],
        input_output_aliases={0: 2},
        scratch_shapes=[pltpu.SemaphoreType.DMA((1,))],
        compiler_params=params(8),
        name="query_sums",
    )(state, in_hbm(blk))


def merged(pieces):
    peak = pieces[0][0]
    for piece in pieces[1:]:
        peak = jnp.maximum(peak, piece[0])
    mass = part = 0.0
    for piece in pieces:
        weight = jnp.exp2(piece[0] - peak)
        mass = mass + piece[1] * weight
        part = part + piece[2] * weight
    return peak, mass, part


def query_grad_kernel(count, meta, *refs):
    pieces = refs[:count]
    blk_ref, ab_ref = refs[count : count + 2]
    c_ref, d_ref, *q_refs = refs[count + 2 : -2]
    tab_s, acc_s = refs[-2:]
    blocks = blk_ref.shape[1]
    tables, features, _ = acc_s.shape
    tab_s[0], tab_s[1], tab_s[2] = merged(pieces)
    acc_s[...] = jnp.zeros_like(acc_s)
    for b in range(blocks):
        table = meta[OWNER, b]
        at = meta[SLOT_OUT, table]
        mass = tab_s[1, pl.ds(table, 1), :]
        c = jnp.exp2(blk_ref[0, b : b + 1, :] - tab_s[0, pl.ds(table, 1), :]) / mass
        shift = blk_ref[2, b : b + 1, :] / blk_ref[1, b : b + 1, :]
        d = c * (shift - tab_s[2, pl.ds(table, 1), :] / mass)
        c_ref[b : b + 1, :] = c
        d_ref[b : b + 1, :] = d
        for h in range(features // HD):
            rows = slice(h * HD, (h + 1) * HD)
            lanes = slice(h * TEST, (h + 1) * TEST)
            acc_s[at, rows, :] += c[:, lanes] * ab_ref[b, 0, rows, :] + d[:, lanes] * ab_ref[b, 1, rows, :]
    per = tables // len(q_refs)
    for n in range(tables):
        ref = q_refs[n // per]
        ref[n % per] = (acc_s[n] * SCORE_SCALE).T.astype(ref.dtype)


def query_grads(meta, tables, pieces, blk, ab, q_dtypes):
    blocks, _, features, _ = ab.shape
    stacked = blk.shape[2]
    per = tables // len(q_dtypes)
    return pl.pallas_call(
        lambda *refs: query_grad_kernel(len(pieces), *refs),
        in_specs=[smem_spec()] + [vmem_spec()] * (len(pieces) + 2),
        out_specs=[vmem_spec()] * (2 + len(q_dtypes)),
        out_shape=[
            jax.ShapeDtypeStruct((blocks, stacked), jnp.float32),
            jax.ShapeDtypeStruct((blocks, stacked), jnp.float32),
        ]
        + [jax.ShapeDtypeStruct((per, TEST, features), dtype) for dtype in q_dtypes],
        scratch_shapes=[
            pltpu.VMEM((3, tables, stacked), jnp.float32),
            pltpu.VMEM((tables, features, TEST), jnp.float32),
        ],
        compiler_params=params(10),
        name="query_grads",
    )(meta, *pieces, blk, ab)


def row_grads_kernel(meta, c_ref, d_ref, qgt_s, state, dk_hbm, dv_hbm, dk_s, dv_s, out_sem):
    blocks, _, features = dk_s.shape
    stacked = features // HD * TEST
    turned = (((1,), (1,)), ((), ()))
    stores = []
    for b in range(blocks):
        at_slot = meta[SLOT_IN, meta[OWNER, b]]
        for p in range(features // LANES):
            at = slice(p * LANES, (p + 1) * LANES)
            wide = slice(p * WIDE, (p + 1) * WIDE)
            c = c_ref[b : b + 1, wide]
            d = d_ref[b : b + 1, wide]
            q_t = two_heads(qgt_s[at_slot, at, :].astype(jnp.float32))
            g_t = two_heads(
                qgt_s[at_slot, features + p * LANES : features + (p + 1) * LANES, :].astype(jnp.float32)
            )
            for_u = (q_t * (c * SCORE_SCALE)).astype(jnp.bfloat16)
            for_e = jnp.concatenate([g_t * c, q_t * (d * SCORE_SCALE)], axis=0).astype(jnp.bfloat16)
            from_e = lax.dot_general(
                state[b, :, wide], for_e, turned, preferred_element_type=jnp.float32
            )
            moved = state[b, :, stacked + p * WIDE : stacked + (p + 1) * WIDE]
            from_u = lax.dot_general(moved, for_u, turned, preferred_element_type=jnp.float32)
            dv_s[b, :, at] = from_e[:, :LANES].astype(jnp.bfloat16)
            dk_s[b, :, at] = (from_u + from_e[:, LANES:]).astype(jnp.bfloat16)
        rows = pl.ds(b * BLK, BLK)
        stores += every_copy(
            [
                pltpu.make_async_copy(dk_s.at[b], dk_hbm.at[rows], out_sem.at[0, b]),
                pltpu.make_async_copy(dv_s.at[b], dv_hbm.at[rows], out_sem.at[1, b]),
            ]
        )
    for copy in stores:
        copy.wait()


def row_grads(meta, c, d, qgt, state):
    blocks = state.shape[0]
    features = qgt.shape[1] // 2
    return pl.pallas_call(
        row_grads_kernel,
        in_specs=[smem_spec()] + [vmem_spec()] * 4,
        out_specs=[hbm_spec()] * 2,
        out_shape=[jax.ShapeDtypeStruct((blocks * BLK, features), jnp.bfloat16)] * 2,
        scratch_shapes=[
            pltpu.VMEM((blocks, BLK, features), jnp.bfloat16),
            pltpu.VMEM((blocks, BLK, features), jnp.bfloat16),
            pltpu.SemaphoreType.DMA((2, blocks)),
        ],
        compiler_params=params(10),
        name="row_grads",
    )(meta, c, d, qgt, state)


def index_kernel(small, blocks, block_table, train_rows, test_rows, meta, count):
    chip = lax.axis_index("rows").astype(jnp.int32)
    core = lax.axis_index("pair").astype(jnp.int32)
    first = lax.axis_index(RP).astype(jnp.int32) * blocks
    tables = train_rows.shape[0]
    for t in range(tables):
        count[t] = 0
        meta[TESTN, t] = test_rows[t]
        if small:
            away = (t // 2) ^ chip
            not_mine = (t % 2) ^ core
            meta[SLOT_IN, t] = 2 * away + not_mine
            meta[TABLE_OF, t] = 2 * away + not_mine
            meta[SLOT_OUT, t] = 4 * not_mine + ((away + 3) & 3)
        else:
            for row in (SLOT_IN, TABLE_OF, SLOT_OUT):
                meta[row, t] = t

    def earlier(n, carry):
        table = block_table[n]
        count[table] = count[table] + 1
        return carry

    lax.fori_loop(0, first, earlier, 0)
    for b in range(blocks):
        table = block_table[first + b]
        meta[OWNER, b] = table
        meta[LIVE, b] = jnp.minimum(train_rows[table] - count[table] * BLK, BLK)
        count[table] = count[table] + 1


def index_table(small, blocks, block_table, train_rows, test_rows):
    tables = train_rows.shape[0]
    return pl.pallas_call(
        lambda *refs: index_kernel(small, blocks, *refs),
        in_specs=[smem_spec()] * 3,
        out_specs=smem_spec(),
        out_shape=jax.ShapeDtypeStruct((6, max(blocks, tables)), jnp.int32),
        scratch_shapes=[pltpu.SMEM((tables,), jnp.int32)],
        name="index_table",
    )(block_table, train_rows, test_rows)


def local(small, query_rows, key_rows, value_rows, cotangent, train_rows, test_rows, block_table):
    features = query_rows.shape[1]
    blocks = key_rows.shape[0] // BLK
    tables = train_rows.shape[0]
    pair = lambda value: lax.ppermute(value, "pair", PAIR)
    step = lambda value, s: lax.ppermute(value, "rows", [(z, z ^ s) for z in range(4)])
    if small:
        held = 1

        def spread(value):
            pieces = []
            for near in [value] + [step(value, s) for s in (1, 2, 3)]:
                pieces += [near, pair(near)]
            return pieces

    else:
        held = 0
        spread = lambda value: [lax.all_gather(value, RP, axis=0, tiled=True)]

    queries = spread(query_rows)
    grads = spread(cotangent)
    if small:
        block_table, queries[2] = lax.optimization_barrier((block_table, queries[2]))
    meta = index_table(small, blocks, block_table, train_rows, test_rows)
    qgt, state, blk, tab = block_scores(meta, tables, held, queries, grads, key_rows, value_rows)
    if small:
        stats = spread(tab)
        dtypes = [jnp.float32, jnp.bfloat16]
    else:
        peak = lax.pmax(tab[0], RP)
        sums = lax.psum(tab[1:] * jnp.exp2(tab[0] - peak)[None], RP)
        stats = [jnp.concatenate([peak[None], sums], axis=0)]
        dtypes = [jnp.float32]
    ab, blk, state = query_sums(features, state, blk)
    c, d, *q_terms = query_grads(meta, tables, stats, blk, ab, dtypes)
    if small:
        keep, send = q_terms
        total = keep + pair(send).astype(jnp.float32)
        low = total.astype(jnp.bfloat16)
        got = [step(low[s - 1], s) for s in (1, 2, 3)]
        low, c = lax.optimization_barrier((low, c))
        key_grad, value_grad = row_grads(meta, c, d, qgt, state)
        query_grad = total[3]
        for value in got:
            query_grad = query_grad + value.astype(jnp.float32)
    else:
        query_grad = lax.psum_scatter(
            q_terms[0].reshape(tables * TEST, features), RP, scatter_dimension=0, tiled=True
        )
        key_grad, value_grad = row_grads(meta, c, d, qgt, state)
    return query_grad.astype(jnp.bfloat16), key_grad, value_grad


def solution(mesh):
    sizes = mesh.shape
    tables_of_rows = P(("groups", "rows", "pair"), "mp")
    in_specs = (tables_of_rows,) * 4 + (P("groups"),) * 3
    out_specs = (tables_of_rows,) * 3

    def run(query_rows, *rest):
        local_rows = query_rows.shape[0] // (sizes["groups"] * sizes["rows"] * sizes["pair"])
        small = sizes["rows"] == 4 and sizes["pair"] == 2 and local_rows == TEST
        return jax.shard_map(
            lambda *args: local(small, *args),
            mesh=mesh,
            in_specs=in_specs,
            out_specs=out_specs,
            check_vma=False,
        )(query_rows, *rest)

    return run
```

```python
import math

import jax
import jax.numpy as jnp
from jax import lax
from jax.experimental import pallas as pl
from jax.experimental.pallas import tpu as pltpu
from jax.sharding import PartitionSpec as P

HD = 64
TEST = 128
BLK = 512
LANES = 128
WIDE = 2 * TEST
CHUNK = 64

NEG = -1e30
SCORE_SCALE = 1.0 / math.sqrt(HD)
LOG2_SCALE = SCORE_SCALE * math.log2(math.e)
RP = ("rows", "pair")
PAIR = [(0, 1), (1, 0)]


def params(mib):
    return pltpu.CompilerParams(vmem_limit_bytes=mib * 1024 * 1024)


def two_heads(rows):
    feature = lax.broadcasted_iota(jnp.int32, rows.shape, 0)
    zero = jnp.zeros_like(rows)
    return jnp.concatenate(
        [jnp.where(feature < HD, rows, zero), jnp.where(feature < HD, zero, rows)], axis=1
    )


def every_copy(copies):
    for copy in copies:
        copy.start()
    return copies


OWNER, LIVE, TESTN, SLOT_IN, TABLE_OF, SLOT_OUT = range(6)


def vmem_spec():
    return pl.BlockSpec(memory_space=pltpu.VMEM)


def smem_spec():
    return pl.BlockSpec(memory_space=pltpu.SMEM)


def hbm_spec():
    return pl.BlockSpec(memory_space=pltpu.HBM)


def in_hbm(value):
    return pltpu.with_memory_space_constraint(value, pltpu.HBM)


def load_kernel(small, table_hbm, train_hbm, test_hbm, key_hbm, value_hbm, meta, state, *scratch):
    block_table, train_rows, test_rows, count, sem, small_sem = scratch
    entries = every_copy(
        [
            pltpu.make_async_copy(table_hbm, block_table, small_sem.at[0]),
            pltpu.make_async_copy(train_hbm, train_rows, small_sem.at[1]),
            pltpu.make_async_copy(test_hbm, test_rows, small_sem.at[2]),
        ]
    )
    blocks = state.shape[0]
    features = key_hbm.shape[1]
    stacked = features // HD * TEST
    loads = []
    for b in range(blocks):
        for n, source in enumerate((key_hbm, value_hbm)):
            lanes = pl.ds(2 * stacked + n * features, features)
            loads.append(
                pltpu.make_async_copy(
                    source.at[pl.ds(b * BLK, BLK)], state.at[b, :, lanes], sem.at[n, b]
                )
            )
    every_copy(loads)
    chip = lax.axis_index("rows").astype(jnp.int32)
    core = lax.axis_index("pair").astype(jnp.int32)
    first = lax.axis_index(RP).astype(jnp.int32) * blocks
    for copy in entries:
        copy.wait()
    for t in range(train_rows.shape[0]):
        count[t] = 0
        meta[TESTN, t] = test_rows[t]
        if small:
            away = (t // 2) ^ chip
            not_mine = (t % 2) ^ core
            meta[SLOT_IN, t] = 2 * away + not_mine
            meta[TABLE_OF, t] = 2 * away + not_mine
            meta[SLOT_OUT, t] = 4 * not_mine + ((away + 3) & 3)
        else:
            for row in (SLOT_IN, TABLE_OF, SLOT_OUT):
                meta[row, t] = t

    def earlier(n, carry):
        table = block_table[n]
        count[table] = count[table] + 1
        return carry

    lax.fori_loop(0, first, earlier, 0)
    for b in range(blocks):
        table = block_table[first + b]
        meta[OWNER, b] = table
        meta[LIVE, b] = jnp.minimum(train_rows[table] - count[table] * BLK, BLK)
        count[table] = count[table] + 1
    for copy in loads:
        copy.wait()


def load_rows(small, block_table, train_rows, test_rows, key_rows, value_rows):
    tables = train_rows.shape[0]
    features = key_rows.shape[1]
    blocks = key_rows.shape[0] // BLK
    stacked = features // HD * TEST
    return pl.pallas_call(
        lambda *refs: load_kernel(small, *refs),
        in_specs=[hbm_spec()] * 5,
        out_specs=[smem_spec(), vmem_spec()],
        out_shape=[
            pltpu.SMEM((6, max(blocks, tables)), jnp.int32),
            pltpu.VMEM((blocks, BLK, 2 * stacked + 2 * features), jnp.bfloat16),
        ],
        scratch_shapes=[
            pltpu.SMEM(block_table.shape, jnp.int32),
            pltpu.SMEM((tables,), jnp.int32),
            pltpu.SMEM((tables,), jnp.int32),
            pltpu.SMEM((tables,), jnp.int32),
            pltpu.SemaphoreType.DMA((2, blocks)),
            pltpu.SemaphoreType.DMA((3,)),
        ],
        compiler_params=params(4),
        name="load_rows",
    )(*map(in_hbm, (block_table, train_rows, test_rows, key_rows, value_rows)))


def turn_pieces(pieces, held, held_s, sem, store):
    early = every_copy(
        [pltpu.make_async_copy(pieces[n], held_s.at[n], sem.at[n]) for n in range(held)]
    )
    at_slot = held
    for piece in pieces[held:]:
        for m in range(piece.shape[0] // TEST):
            store(at_slot, piece[m * TEST : (m + 1) * TEST, :].T)
            at_slot += 1
    for copy in early:
        copy.wait()
    for n in range(held):
        store(n, held_s[n].T)


def fold(values, op):
    return op(values.reshape(CHUNK // 8, 8, WIDE), axis=0)


def units_of(blocks, features):
    return [(b, p) for b in range(blocks) for p in range(features // LANES)]


def weights_kernel(count, held, meta, *refs):
    pieces = refs[:count]
    state, qt_ref, peak_hbm, state_out, peak_s, scores_s, held_s, sem, peak_sem = refs[count:]
    tables, features, _ = qt_ref.shape
    stacked = features // HD * TEST
    units = units_of(state.shape[0], features)

    def store(at_slot, turned):
        qt_ref[at_slot] = turned

    turn_pieces(pieces, held, held_s, sem, store)
    peaks = [None] * len(units)
    for t in range(len(units) + 1):
        if t < len(units):
            b, p = units[t]
            live = meta[LIVE, b]
            queries = two_heads(
                qt_ref[meta[SLOT_IN, meta[OWNER, b]], p * LANES : (p + 1) * LANES, :]
            )
            peak = jnp.full((8, WIDE), NEG, jnp.float32)
        for r in range(0, BLK, CHUNK):
            rows = slice(r, r + CHUNK)
            if t > 0:
                last_b, last_p = units[t - 1]
                weights = jnp.exp2(scores_s[(t - 1) % 2, rows, :] * LOG2_SCALE - peaks[t - 1])
                state_out[last_b, rows, last_p * WIDE : (last_p + 1) * WIDE] = weights.astype(
                    jnp.bfloat16
                )
            if t < len(units):
                keys = state[b, rows, 2 * stacked + p * LANES : 2 * stacked + (p + 1) * LANES]
                scores = jnp.dot(keys, queries, preferred_element_type=jnp.float32)
                row = lax.broadcasted_iota(jnp.int32, scores.shape, 0)
                scores = jnp.where(row < live - r, scores, NEG)
                scores_s[t % 2, rows, :] = scores
                peak = jnp.maximum(peak, fold(scores, jnp.max))
        if t < len(units):
            peaks[t] = jnp.max(peak, axis=0, keepdims=True) * LOG2_SCALE
            peak_s[b : b + 1, p * WIDE : (p + 1) * WIDE] = peaks[t]
    for copy in every_copy([pltpu.make_async_copy(peak_s, peak_hbm, peak_sem.at[0])]):
        copy.wait()


def block_weights(meta, held, pieces, state, features, tables):
    blocks = state.shape[0]
    stacked = features // HD * TEST
    count = len(pieces)
    pieces = [in_hbm(piece) if n < held else piece for n, piece in enumerate(pieces)]
    specs = [hbm_spec() if n < held else vmem_spec() for n in range(count)]
    return pl.pallas_call(
        lambda *refs: weights_kernel(count, held, *refs),
        in_specs=[smem_spec()] + specs + [vmem_spec()],
        out_specs=[vmem_spec(), hbm_spec(), vmem_spec()],
        out_shape=[
            pltpu.VMEM((tables, features, TEST), jnp.bfloat16),
            pltpu.HBM((blocks, stacked), jnp.float32),
            pltpu.VMEM(state.shape, jnp.bfloat16),
        ],
        input_output_aliases={count + 1: 2},
        scratch_shapes=[
            pltpu.VMEM((blocks, stacked), jnp.float32),
            pltpu.VMEM((2, BLK, WIDE), jnp.float32),
            pltpu.VMEM((max(held, 1), TEST, features), jnp.bfloat16),
            pltpu.SemaphoreType.DMA((max(held, 1),)),
            pltpu.SemaphoreType.DMA((1,)),
        ],
        compiler_params=params(10),
        name="block_weights",
    )(meta, *pieces, state)


def moved_kernel(count, held, meta, *refs):
    pieces = refs[:count]
    peak_hbm, state, gt_ref, blk_hbm, tab_ref, state_out = refs[count : count + 6]
    blk_s, tab_s, dprobs_s, held_s, sem, blk_sem = refs[count + 6 :]
    tables, features, _ = gt_ref.shape
    stacked = features // HD * TEST
    blocks = state.shape[0]
    units = units_of(blocks, features)
    peak_copy = pltpu.make_async_copy(peak_hbm, blk_s.at[0], blk_sem.at[0])
    peak_copy.start()
    query = lax.broadcasted_iota(jnp.int32, (features, TEST), 1)

    def store(at_slot, turned):
        live = query < meta[TESTN, meta[TABLE_OF, at_slot]]
        gt_ref[at_slot] = jnp.where(live, turned, jnp.zeros_like(turned))

    turn_pieces(pieces, held, held_s, sem, store)
    means = [None] * len(units)
    zero = jnp.zeros((8, WIDE), jnp.float32)
    for t in range(len(units) + 1):
        if t < len(units):
            b, p = units[t]
            grads = two_heads(
                gt_ref[meta[SLOT_IN, meta[OWNER, b]], p * LANES : (p + 1) * LANES, :]
            )
            mass = part = zero
        for r in range(0, BLK, CHUNK):
            rows = slice(r, r + CHUNK)
            if t > 0:
                last_b, last_p = units[t - 1]
                weights = state[last_b, rows, last_p * WIDE : (last_p + 1) * WIDE]
                moved = weights.astype(jnp.float32) * (dprobs_s[(t - 1) % 2, rows, :] - means[t - 1])
                lanes = slice(stacked + last_p * WIDE, stacked + (last_p + 1) * WIDE)
                state_out[last_b, rows, lanes] = moved.astype(jnp.bfloat16)
            if t < len(units):
                first = 2 * stacked + features + p * LANES
                values = state[b, rows, first : first + LANES]
                dprobs = jnp.dot(values, grads, preferred_element_type=jnp.float32)
                weights = state[b, rows, p * WIDE : (p + 1) * WIDE].astype(jnp.float32)
                mass = mass + fold(weights, jnp.sum)
                part = part + fold(weights * dprobs, jnp.sum)
                dprobs_s[t % 2, rows, :] = dprobs
        if t < len(units):
            wide = slice(p * WIDE, (p + 1) * WIDE)
            mass = jnp.sum(mass, axis=0, keepdims=True)
            means[t] = jnp.sum(part, axis=0, keepdims=True) / mass
            blk_s[1, b : b + 1, wide] = mass
            blk_s[2, b : b + 1, wide] = means[t]
    peak_copy.wait()
    tab_s[0] = jnp.full(tab_s.shape[1:], NEG, jnp.float32)
    tab_s[1] = jnp.zeros(tab_s.shape[1:], jnp.float32)
    tab_s[2] = jnp.zeros(tab_s.shape[1:], jnp.float32)
    for b in range(blocks):
        at = pl.ds(meta[OWNER, b], 1)
        peak, mass, mean = blk_s[0, b : b + 1, :], blk_s[1, b : b + 1, :], blk_s[2, b : b + 1, :]
        old = tab_s[0, at, :]
        new = jnp.maximum(old, peak)
        old_weight = jnp.exp2(old - new)
        new_mass = mass * jnp.exp2(peak - new)
        tab_s[0, at, :] = new
        tab_s[1, at, :] = tab_s[1, at, :] * old_weight + new_mass
        tab_s[2, at, :] = tab_s[2, at, :] * old_weight + new_mass * mean
    here = tab_s[1] > 0.0
    mass = jnp.where(here, tab_s[1], 1.0)
    tab_ref[0] = jnp.where(here, tab_s[0] + jnp.log2(mass), NEG)
    tab_ref[1] = tab_s[2] / mass
    for copy in every_copy([pltpu.make_async_copy(blk_s, blk_hbm, blk_sem.at[0])]):
        copy.wait()


def moved_weights(meta, held, pieces, peak, state, features, tables):
    blocks = state.shape[0]
    stacked = features // HD * TEST
    count = len(pieces)
    pieces = [in_hbm(piece) if n < held else piece for n, piece in enumerate(pieces)]
    specs = [hbm_spec() if n < held else vmem_spec() for n in range(count)]
    return pl.pallas_call(
        lambda *refs: moved_kernel(count, held, *refs),
        in_specs=[smem_spec()] + specs + [hbm_spec(), vmem_spec()],
        out_specs=[vmem_spec(), hbm_spec(), vmem_spec(), vmem_spec()],
        out_shape=[
            pltpu.VMEM((tables, features, TEST), jnp.bfloat16),
            pltpu.HBM((3, blocks, stacked), jnp.float32),
            jax.ShapeDtypeStruct((2, tables, stacked), jnp.float32),
            pltpu.VMEM(state.shape, jnp.bfloat16),
        ],
        input_output_aliases={count + 2: 3},
        scratch_shapes=[
            pltpu.VMEM((3, blocks, stacked), jnp.float32),
            pltpu.VMEM((3, tables, stacked), jnp.float32),
            pltpu.VMEM((2, BLK, WIDE), jnp.float32),
            pltpu.VMEM((max(held, 1), TEST, features), jnp.bfloat16),
            pltpu.SemaphoreType.DMA((max(held, 1),)),
            pltpu.SemaphoreType.DMA((1,)),
        ],
        compiler_params=params(10),
        name="moved_weights",
    )(meta, *pieces, in_hbm(peak), state)


def query_sums_kernel(state, blk_hbm, ab_ref, blk_ref, state_out, blk_sem):
    blocks, _, features, _ = ab_ref.shape
    stacked = features // HD * TEST
    copy = pltpu.make_async_copy(blk_hbm, blk_ref, blk_sem.at[0])
    copy.start()
    for b in range(blocks):
        for p in range(features // LANES):
            keys = state[b, :, 2 * stacked + p * LANES : 2 * stacked + (p + 1) * LANES]
            for n, first in enumerate((stacked, 0)):
                values = state[b, :, first + p * WIDE : first + (p + 1) * WIDE]
                product = lax.dot_general(
                    keys, values, (((0,), (0,)), ((), ())), preferred_element_type=jnp.float32
                )
                ab_ref[b, n, p * LANES : p * LANES + HD, :] = product[:HD, :TEST]
                ab_ref[b, n, p * LANES + HD : (p + 1) * LANES, :] = product[HD:, TEST:]
    copy.wait()


def query_sums(features, state, blk):
    blocks = state.shape[0]
    return pl.pallas_call(
        query_sums_kernel,
        in_specs=[vmem_spec(), hbm_spec()],
        out_specs=[vmem_spec()] * 3,
        out_shape=[
            pltpu.VMEM((blocks, 2, features, TEST), jnp.float32),
            pltpu.VMEM(blk.shape, jnp.float32),
            pltpu.VMEM(state.shape, jnp.bfloat16),
        ],
        input_output_aliases={0: 2},
        scratch_shapes=[pltpu.SemaphoreType.DMA((1,))],
        compiler_params=params(8),
        name="query_sums",
    )(state, in_hbm(blk))


def merged(pieces):
    peak = pieces[0][0]
    for piece in pieces[1:]:
        peak = jnp.maximum(peak, piece[0])
    mass = part = 0.0
    for piece in pieces:
        weight = jnp.exp2(piece[0] - peak)
        mass = mass + weight
        part = part + piece[1] * weight
    return peak, mass, part / mass


def query_grad_kernel(count, meta, *refs):
    pieces = refs[:count]
    blk_ref, ab_ref = refs[count : count + 2]
    c_ref, d_ref, *q_refs = refs[count + 2 : -2]
    tab_s, acc_s = refs[-2:]
    blocks = blk_ref.shape[1]
    tables, features, _ = acc_s.shape
    tab_s[0], tab_s[1], tab_s[2] = merged(pieces)
    acc_s[...] = jnp.zeros_like(acc_s)
    for b in range(blocks):
        table = meta[OWNER, b]
        at = meta[SLOT_OUT, table]
        mass = tab_s[1, pl.ds(table, 1), :]
        c = jnp.exp2(blk_ref[0, b : b + 1, :] - tab_s[0, pl.ds(table, 1), :]) / mass
        d = c * (blk_ref[2, b : b + 1, :] - tab_s[2, pl.ds(table, 1), :])
        c_ref[b : b + 1, :] = c
        d_ref[b : b + 1, :] = d
        for h in range(features // HD):
            rows = slice(h * HD, (h + 1) * HD)
            lanes = slice(h * TEST, (h + 1) * TEST)
            acc_s[at, rows, :] += c[:, lanes] * ab_ref[b, 0, rows, :] + d[:, lanes] * ab_ref[b, 1, rows, :]
    per = tables // len(q_refs)
    for n in range(tables):
        ref = q_refs[n // per]
        ref[n % per] = (acc_s[n] * SCORE_SCALE).T.astype(ref.dtype)


def query_grads(meta, tables, pieces, blk, ab, q_dtypes):
    blocks, _, features, _ = ab.shape
    stacked = blk.shape[2]
    per = tables // len(q_dtypes)
    return pl.pallas_call(
        lambda *refs: query_grad_kernel(len(pieces), *refs),
        in_specs=[smem_spec()] + [vmem_spec()] * (len(pieces) + 2),
        out_specs=[vmem_spec()] * (2 + len(q_dtypes)),
        out_shape=[
            jax.ShapeDtypeStruct((blocks, stacked), jnp.float32),
            jax.ShapeDtypeStruct((blocks, stacked), jnp.float32),
        ]
        + [jax.ShapeDtypeStruct((per, TEST, features), dtype) for dtype in q_dtypes],
        scratch_shapes=[
            pltpu.VMEM((3, tables, stacked), jnp.float32),
            pltpu.VMEM((tables, features, TEST), jnp.float32),
        ],
        compiler_params=params(10),
        name="query_grads",
    )(meta, *pieces, blk, ab)


def row_grads_kernel(meta, c_ref, d_ref, qt_ref, gt_ref, state, dk_hbm, dv_hbm, dk_s, dv_s, out_sem):
    blocks, _, features = dk_s.shape
    stacked = features // HD * TEST
    turned = (((1,), (1,)), ((), ()))
    stores = []
    for b in range(blocks):
        at_slot = meta[SLOT_IN, meta[OWNER, b]]
        for p in range(features // LANES):
            at = slice(p * LANES, (p + 1) * LANES)
            wide = slice(p * WIDE, (p + 1) * WIDE)
            c = c_ref[b : b + 1, wide]
            d = d_ref[b : b + 1, wide]
            q_t = two_heads(qt_ref[at_slot, at, :].astype(jnp.float32))
            g_t = two_heads(gt_ref[at_slot, at, :].astype(jnp.float32))
            for_u = (q_t * (c * SCORE_SCALE)).astype(jnp.bfloat16)
            for_e = jnp.concatenate([g_t * c, q_t * (d * SCORE_SCALE)], axis=0).astype(jnp.bfloat16)
            from_e = lax.dot_general(
                state[b, :, wide], for_e, turned, preferred_element_type=jnp.float32
            )
            moved = state[b, :, stacked + p * WIDE : stacked + (p + 1) * WIDE]
            from_u = lax.dot_general(moved, for_u, turned, preferred_element_type=jnp.float32)
            dv_s[b, :, at] = from_e[:, :LANES].astype(jnp.bfloat16)
            dk_s[b, :, at] = (from_u + from_e[:, LANES:]).astype(jnp.bfloat16)
        rows = pl.ds(b * BLK, BLK)
        stores += every_copy(
            [
                pltpu.make_async_copy(dk_s.at[b], dk_hbm.at[rows], out_sem.at[0, b]),
                pltpu.make_async_copy(dv_s.at[b], dv_hbm.at[rows], out_sem.at[1, b]),
            ]
        )
    for copy in stores:
        copy.wait()


def row_grads(meta, c, d, turned, state):
    blocks = state.shape[0]
    features = turned[0].shape[1]
    return pl.pallas_call(
        row_grads_kernel,
        in_specs=[smem_spec()] + [vmem_spec()] * 5,
        out_specs=[hbm_spec()] * 2,
        out_shape=[jax.ShapeDtypeStruct((blocks * BLK, features), jnp.bfloat16)] * 2,
        scratch_shapes=[
            pltpu.VMEM((blocks, BLK, features), jnp.bfloat16),
            pltpu.VMEM((blocks, BLK, features), jnp.bfloat16),
            pltpu.SemaphoreType.DMA((2, blocks)),
        ],
        compiler_params=params(10),
        name="row_grads",
    )(meta, c, d, *turned, state)


def local(small, query_rows, key_rows, value_rows, cotangent, train_rows, test_rows, block_table):
    features = query_rows.shape[1]
    blocks = key_rows.shape[0] // BLK
    tables = train_rows.shape[0]
    pair = lambda value: lax.ppermute(value, "pair", PAIR)
    step = lambda value, s: lax.ppermute(value, "rows", [(z, z ^ s) for z in range(4)])
    after = lambda value, other: lax.optimization_barrier((value, other))
    load = lambda entries: load_rows(small, entries, train_rows, test_rows, key_rows, value_rows)
    if small:
        held = 1
        near = [step(query_rows, s) for s in (1, 2, 3)]
        near_grads = [step(cotangent, s) for s in (1, 2, 3)]
        block_table, near[0] = after(block_table, near[0])
        meta, state = load(block_table)
        near[0], meta = after(near[0], meta)
        queries = [query_rows, pair(query_rows)]
        for value in near:
            queries += [value, pair(value)]
        qt, peak, state = block_weights(meta, held, queries, state, features, tables)
        *near_grads, qt = lax.optimization_barrier((*near_grads, qt))
        grads = [cotangent, pair(cotangent)]
        for value in near_grads:
            grads += [value, pair(value)]
    else:
        held = 0
        meta, state = load(block_table)
        queries = [lax.all_gather(query_rows, RP, axis=0, tiled=True)]
        qt, peak, state = block_weights(meta, held, queries, state, features, tables)
        grads = [lax.all_gather(cotangent, RP, axis=0, tiled=True)]
    gt, blk, tab, state = moved_weights(meta, held, grads, peak, state, features, tables)
    if small:
        near = [step(tab, s) for s in (1, 2, 3)]
        ab, blk, state = query_sums(features, state, blk)
        *near, ab = lax.optimization_barrier((*near, ab))
        stats = [tab, pair(tab)]
        for value in near:
            stats += [value, pair(value)]
        dtypes = [jnp.float32, jnp.bfloat16]
    else:
        ab, blk, state = query_sums(features, state, blk)
        peak = lax.pmax(tab[0], RP)
        weight = jnp.exp2(tab[0] - peak)
        total, part = lax.psum(jnp.stack([weight, weight * tab[1]]), RP)
        stats = [jnp.stack([peak + jnp.log2(total), part / total])]
        dtypes = [jnp.float32]
    c, d, *q_terms = query_grads(meta, tables, stats, blk, ab, dtypes)
    if small:
        keep, send = q_terms
        total = keep + pair(send).astype(jnp.float32)
        low = total.astype(jnp.bfloat16)
        got = [step(low[s - 1], s) for s in (1, 2, 3)]
        low, c = lax.optimization_barrier((low, c))
        key_grad, value_grad = row_grads(meta, c, d, (qt, gt), state)
        query_grad = total[3]
        for value in got:
            query_grad = query_grad + value.astype(jnp.float32)
    else:
        query_grad = lax.psum_scatter(
            q_terms[0].reshape(tables * TEST, features), RP, scatter_dimension=0, tiled=True
        )
        key_grad, value_grad = row_grads(meta, c, d, (qt, gt), state)
    return query_grad.astype(jnp.bfloat16), key_grad, value_grad


def solution(mesh):
    sizes = mesh.shape
    tables_of_rows = P(("groups", "rows", "pair"), "mp")
    in_specs = (tables_of_rows,) * 4 + (P("groups"),) * 3
    out_specs = (tables_of_rows,) * 3

    def run(query_rows, *rest):
        local_rows = query_rows.shape[0] // (sizes["groups"] * sizes["rows"] * sizes["pair"])
        small = sizes["rows"] == 4 and sizes["pair"] == 2 and local_rows == TEST
        return jax.shard_map(
            lambda *args: local(small, *args),
            mesh=mesh,
            in_specs=in_specs,
            out_specs=out_specs,
            check_vma=False,
        )(query_rows, *rest)

    return run
```

```python
import math

import jax
import jax.numpy as jnp
from jax import lax
from jax.experimental import pallas as pl
from jax.experimental.pallas import tpu as pltpu
from jax.sharding import PartitionSpec as P

HD = 64
TEST = 128
BLK = 512
LANES = 128
WIDE = 2 * TEST
CHUNK = 64

NEG = -1e30
SCORE_SCALE = 1.0 / math.sqrt(HD)
LOG2_SCALE = SCORE_SCALE * math.log2(math.e)
RP = ("rows", "pair")
PAIR = [(0, 1), (1, 0)]


def params(mib):
    return pltpu.CompilerParams(vmem_limit_bytes=mib * 1024 * 1024)


def two_heads(rows):
    feature = lax.broadcasted_iota(jnp.int32, rows.shape, 0)
    zero = jnp.zeros_like(rows)
    return jnp.concatenate(
        [jnp.where(feature < HD, rows, zero), jnp.where(feature < HD, zero, rows)], axis=1
    )


def every_copy(copies):
    for copy in copies:
        copy.start()
    return copies


OWNER, LIVE, TESTN, SLOT_IN, TABLE_OF, SLOT_OUT = range(6)


def vmem_spec():
    return pl.BlockSpec(memory_space=pltpu.VMEM)


def smem_spec():
    return pl.BlockSpec(memory_space=pltpu.SMEM)


def hbm_spec():
    return pl.BlockSpec(memory_space=pltpu.HBM)


def in_hbm(value):
    return pltpu.with_memory_space_constraint(value, pltpu.HBM)


def load_kernel(small, table_hbm, train_hbm, test_hbm, key_hbm, value_hbm, meta, state, *scratch):
    block_table, train_rows, test_rows, count, sem, small_sem = scratch
    entries = every_copy(
        [
            pltpu.make_async_copy(table_hbm, block_table, small_sem.at[0]),
            pltpu.make_async_copy(train_hbm, train_rows, small_sem.at[1]),
            pltpu.make_async_copy(test_hbm, test_rows, small_sem.at[2]),
        ]
    )
    blocks = state.shape[0]
    features = key_hbm.shape[1]
    stacked = features // HD * TEST
    loads = []
    for b in range(blocks):
        for n, source in enumerate((key_hbm, value_hbm)):
            lanes = pl.ds(2 * stacked + n * features, features)
            loads.append(
                pltpu.make_async_copy(
                    source.at[pl.ds(b * BLK, BLK)], state.at[b, :, lanes], sem.at[n, b]
                )
            )
    every_copy(loads)
    chip = lax.axis_index("rows").astype(jnp.int32)
    core = lax.axis_index("pair").astype(jnp.int32)
    first = lax.axis_index(RP).astype(jnp.int32) * blocks
    for copy in entries:
        copy.wait()
    for t in range(train_rows.shape[0]):
        count[t] = 0
        meta[TESTN, t] = test_rows[t]
        if small:
            away = (t // 2) ^ chip
            not_mine = (t % 2) ^ core
            meta[SLOT_IN, t] = 2 * away + not_mine
            meta[TABLE_OF, t] = 2 * away + not_mine
            meta[SLOT_OUT, t] = 4 * not_mine + ((away + 3) & 3)
        else:
            for row in (SLOT_IN, TABLE_OF, SLOT_OUT):
                meta[row, t] = t

    def earlier(n, carry):
        table = block_table[n]
        count[table] = count[table] + 1
        return carry

    lax.fori_loop(0, first, earlier, 0)
    for b in range(blocks):
        table = block_table[first + b]
        meta[OWNER, b] = table
        meta[LIVE, b] = jnp.minimum(train_rows[table] - count[table] * BLK, BLK)
        count[table] = count[table] + 1
    for copy in loads:
        copy.wait()


def load_rows(small, block_table, train_rows, test_rows, key_rows, value_rows):
    tables = train_rows.shape[0]
    features = key_rows.shape[1]
    blocks = key_rows.shape[0] // BLK
    stacked = features // HD * TEST
    return pl.pallas_call(
        lambda *refs: load_kernel(small, *refs),
        in_specs=[hbm_spec()] * 5,
        out_specs=[smem_spec(), vmem_spec()],
        out_shape=[
            pltpu.SMEM((6, max(blocks, tables)), jnp.int32),
            pltpu.VMEM((blocks, BLK, 2 * stacked + 2 * features), jnp.bfloat16),
        ],
        scratch_shapes=[
            pltpu.SMEM(block_table.shape, jnp.int32),
            pltpu.SMEM((tables,), jnp.int32),
            pltpu.SMEM((tables,), jnp.int32),
            pltpu.SMEM((tables,), jnp.int32),
            pltpu.SemaphoreType.DMA((2, blocks)),
            pltpu.SemaphoreType.DMA((3,)),
        ],
        compiler_params=params(4),
        name="load_rows",
    )(*map(in_hbm, (block_table, train_rows, test_rows, key_rows, value_rows)))


def turn_pieces(pieces, held, held_s, sem, store):
    early = every_copy(
        [pltpu.make_async_copy(pieces[n], held_s.at[n], sem.at[n]) for n in range(held)]
    )
    at_slot = held
    for piece in pieces[held:]:
        for m in range(piece.shape[0] // TEST):
            store(at_slot, piece[m * TEST : (m + 1) * TEST, :].T)
            at_slot += 1
    for copy in early:
        copy.wait()
    for n in range(held):
        store(n, held_s[n].T)


def fold(values, op):
    return op(values.reshape(CHUNK // 8, 8, WIDE), axis=0)


def rows_of(meta, b, p, features):
    at_slot = meta[SLOT_IN, meta[OWNER, b]]
    return pl.ds(pl.multiple_of(at_slot * features + p * LANES, LANES), LANES)


def put_heads(side, first, b, p, features, row):
    at = first + b * features // HD + 2 * p
    side[at : at + 1, :] = row[:, :TEST]
    side[at + 1 : at + 2, :] = row[:, TEST:]


def get_heads(side, row, heads):
    return jnp.concatenate([side[row + h : row + h + 1, :] for h in range(heads)], axis=1)


def units_of(blocks, features):
    return [(b, p) for b in range(blocks) for p in range(features // LANES)]


def weights_kernel(count, held, meta, *refs):
    pieces = refs[:count]
    state, side, state_out, scores_s, held_s, sem = refs[count:]
    _, features = held_s.shape[1:]
    stacked = features // HD * TEST
    first_peak = side.shape[0] - state.shape[0] * features // HD
    units = units_of(state.shape[0], features)

    def store(at_slot, turned):
        side[at_slot * features : (at_slot + 1) * features, :] = turned.astype(jnp.float32)

    turn_pieces(pieces, held, held_s, sem, store)
    peaks = [None] * len(units)
    for t in range(len(units) + 1):
        if t < len(units):
            b, p = units[t]
            live = meta[LIVE, b]
            queries = two_heads(side[rows_of(meta, b, p, features), :]).astype(jnp.bfloat16)
            peak = jnp.full((8, WIDE), NEG, jnp.float32)
        for r in range(0, BLK, CHUNK):
            rows = slice(r, r + CHUNK)
            if t > 0:
                last_b, last_p = units[t - 1]
                weights = jnp.exp2(scores_s[(t - 1) % 2, rows, :] * LOG2_SCALE - peaks[t - 1])
                state_out[last_b, rows, last_p * WIDE : (last_p + 1) * WIDE] = weights.astype(
                    jnp.bfloat16
                )
            if t < len(units):
                keys = state[b, rows, 2 * stacked + p * LANES : 2 * stacked + (p + 1) * LANES]
                scores = jnp.dot(keys, queries, preferred_element_type=jnp.float32)
                row = lax.broadcasted_iota(jnp.int32, scores.shape, 0)
                scores = jnp.where(row < live - r, scores, NEG)
                scores_s[t % 2, rows, :] = scores
                peak = jnp.maximum(peak, fold(scores, jnp.max))
        if t < len(units):
            peaks[t] = jnp.max(peak, axis=0, keepdims=True) * LOG2_SCALE
            put_heads(side, first_peak, b, p, features, peaks[t])


def block_weights(meta, held, pieces, state, features, tables):
    blocks = state.shape[0]
    count = len(pieces)
    pieces = [in_hbm(piece) if n < held else piece for n, piece in enumerate(pieces)]
    specs = [hbm_spec() if n < held else vmem_spec() for n in range(count)]
    return pl.pallas_call(
        lambda *refs: weights_kernel(count, held, *refs),
        in_specs=[smem_spec()] + specs + [vmem_spec()],
        out_specs=[vmem_spec()] * 2,
        out_shape=[
            pltpu.VMEM((tables * features + blocks * features // HD, TEST), jnp.float32),
            pltpu.VMEM(state.shape, jnp.bfloat16),
        ],
        input_output_aliases={count + 1: 1},
        scratch_shapes=[
            pltpu.VMEM((2, BLK, WIDE), jnp.float32),
            pltpu.VMEM((max(held, 1), TEST, features), jnp.bfloat16),
            pltpu.SemaphoreType.DMA((max(held, 1),)),
        ],
        compiler_params=params(10),
        name="block_weights",
    )(meta, *pieces, state)


def moved_kernel(count, held, meta, *refs):
    pieces = refs[:count]
    q_side, state, side, tab_ref, state_out = refs[count : count + 5]
    tab_s, dprobs_s, held_s, sem = refs[count + 5 :]
    tables = tab_ref.shape[1]
    _, features = held_s.shape[1:]
    stacked = features // HD * TEST
    blocks = state.shape[0]
    heads = features // HD
    first = tables * features
    units = units_of(blocks, features)
    query = lax.broadcasted_iota(jnp.int32, (features, TEST), 1)

    def store(at_slot, turned):
        live = query < meta[TESTN, meta[TABLE_OF, at_slot]]
        turned = jnp.where(live, turned, jnp.zeros_like(turned)).astype(jnp.float32)
        side[at_slot * features : (at_slot + 1) * features, :] = turned

    turn_pieces(pieces, held, held_s, sem, store)
    means = [None] * len(units)
    zero = jnp.zeros((8, WIDE), jnp.float32)
    for t in range(len(units) + 1):
        if t < len(units):
            b, p = units[t]
            grads = two_heads(side[rows_of(meta, b, p, features), :]).astype(jnp.bfloat16)
            mass = part = zero
        for r in range(0, BLK, CHUNK):
            rows = slice(r, r + CHUNK)
            if t > 0:
                last_b, last_p = units[t - 1]
                weights = state[last_b, rows, last_p * WIDE : (last_p + 1) * WIDE]
                moved = weights.astype(jnp.float32) * (dprobs_s[(t - 1) % 2, rows, :] - means[t - 1])
                lanes = slice(stacked + last_p * WIDE, stacked + (last_p + 1) * WIDE)
                state_out[last_b, rows, lanes] = moved.astype(jnp.bfloat16)
            if t < len(units):
                lane = 2 * stacked + features + p * LANES
                values = state[b, rows, lane : lane + LANES]
                dprobs = jnp.dot(values, grads, preferred_element_type=jnp.float32)
                weights = state[b, rows, p * WIDE : (p + 1) * WIDE].astype(jnp.float32)
                mass = mass + fold(weights, jnp.sum)
                part = part + fold(weights * dprobs, jnp.sum)
                dprobs_s[t % 2, rows, :] = dprobs
        if t < len(units):
            mass = jnp.sum(mass, axis=0, keepdims=True)
            means[t] = jnp.sum(part, axis=0, keepdims=True) / mass
            put_heads(side, first, b, p, features, means[t])
            put_heads(side, first + blocks * heads, b, p, features, mass)
    tab_s[0] = jnp.full(tab_s.shape[1:], NEG, jnp.float32)
    tab_s[1] = jnp.zeros(tab_s.shape[1:], jnp.float32)
    tab_s[2] = jnp.zeros(tab_s.shape[1:], jnp.float32)
    for b in range(blocks):
        at = pl.ds(meta[OWNER, b], 1)
        row = first + b * heads
        peak, mean = get_heads(q_side, row, heads), get_heads(side, row, heads)
        mass = get_heads(side, row + blocks * heads, heads)
        old = tab_s[0, at, :]
        new = jnp.maximum(old, peak)
        old_weight = jnp.exp2(old - new)
        new_mass = mass * jnp.exp2(peak - new)
        tab_s[0, at, :] = new
        tab_s[1, at, :] = tab_s[1, at, :] * old_weight + new_mass
        tab_s[2, at, :] = tab_s[2, at, :] * old_weight + new_mass * mean
    here = tab_s[1] > 0.0
    mass = jnp.where(here, tab_s[1], 1.0)
    tab_ref[0] = jnp.where(here, tab_s[0] + jnp.log2(mass), NEG)
    tab_ref[1] = tab_s[2] / mass


def moved_weights(meta, held, pieces, q_side, state, features, tables):
    blocks = state.shape[0]
    stacked = features // HD * TEST
    count = len(pieces)
    pieces = [in_hbm(piece) if n < held else piece for n, piece in enumerate(pieces)]
    specs = [hbm_spec() if n < held else vmem_spec() for n in range(count)]
    return pl.pallas_call(
        lambda *refs: moved_kernel(count, held, *refs),
        in_specs=[smem_spec()] + specs + [vmem_spec()] * 2,
        out_specs=[vmem_spec()] * 3,
        out_shape=[
            pltpu.VMEM((tables * features + 2 * blocks * features // HD, TEST), jnp.float32),
            jax.ShapeDtypeStruct((2, tables, stacked), jnp.float32),
            pltpu.VMEM(state.shape, jnp.bfloat16),
        ],
        input_output_aliases={count + 2: 2},
        scratch_shapes=[
            pltpu.VMEM((3, tables, stacked), jnp.float32),
            pltpu.VMEM((2, BLK, WIDE), jnp.float32),
            pltpu.VMEM((max(held, 1), TEST, features), jnp.bfloat16),
            pltpu.SemaphoreType.DMA((max(held, 1),)),
        ],
        compiler_params=params(10),
        name="moved_weights",
    )(meta, *pieces, q_side, state)


def query_sums_kernel(state, ab_ref, state_out):
    blocks, _, features, _ = ab_ref.shape
    stacked = features // HD * TEST
    for b in range(blocks):
        for p in range(features // LANES):
            keys = state[b, :, 2 * stacked + p * LANES : 2 * stacked + (p + 1) * LANES]
            for n, first in enumerate((stacked, 0)):
                values = state[b, :, first + p * WIDE : first + (p + 1) * WIDE]
                product = lax.dot_general(
                    keys, values, (((0,), (0,)), ((), ())), preferred_element_type=jnp.float32
                )
                ab_ref[b, n, p * LANES : p * LANES + HD, :] = product[:HD, :TEST]
                ab_ref[b, n, p * LANES + HD : (p + 1) * LANES, :] = product[HD:, TEST:]


def query_sums(features, state):
    blocks = state.shape[0]
    return pl.pallas_call(
        query_sums_kernel,
        in_specs=[vmem_spec()],
        out_specs=[vmem_spec()] * 2,
        out_shape=[
            pltpu.VMEM((blocks, 2, features, TEST), jnp.float32),
            pltpu.VMEM(state.shape, jnp.bfloat16),
        ],
        input_output_aliases={0: 1},
        compiler_params=params(8),
        name="query_sums",
    )(state)


def merged(pieces):
    peak = pieces[0][0]
    for piece in pieces[1:]:
        peak = jnp.maximum(peak, piece[0])
    mass = part = 0.0
    for piece in pieces:
        weight = jnp.exp2(piece[0] - peak)
        mass = mass + weight
        part = part + piece[1] * weight
    return peak, mass, part / mass


def query_grad_kernel(count, meta, *refs):
    pieces = refs[:count]
    q_side, g_side, ab_ref = refs[count : count + 3]
    c_ref, d_ref, *q_refs = refs[count + 3 : -2]
    tab_s, acc_s = refs[-2:]
    blocks = ab_ref.shape[0]
    tables, features, _ = acc_s.shape
    heads = features // HD
    tab_s[0], tab_s[1], tab_s[2] = merged(pieces)
    acc_s[...] = jnp.zeros_like(acc_s)
    for b in range(blocks):
        at = meta[SLOT_OUT, meta[OWNER, b]]
        table = pl.ds(meta[OWNER, b], 1)
        row = tables * features + b * heads
        mass = tab_s[1, table, :]
        c = jnp.exp2(get_heads(q_side, row, heads) - tab_s[0, table, :]) / mass
        d = c * (get_heads(g_side, row, heads) - tab_s[2, table, :])
        c_ref[b : b + 1, :] = c
        d_ref[b : b + 1, :] = d
        for h in range(heads):
            rows = slice(h * HD, (h + 1) * HD)
            lanes = slice(h * TEST, (h + 1) * TEST)
            acc_s[at, rows, :] += c[:, lanes] * ab_ref[b, 0, rows, :] + d[:, lanes] * ab_ref[b, 1, rows, :]
    per = tables // len(q_refs)
    for n in range(tables):
        ref = q_refs[n // per]
        ref[n % per] = (acc_s[n] * SCORE_SCALE).T.astype(ref.dtype)


def query_grads(meta, tables, pieces, sides, ab, q_dtypes):
    blocks, _, features, _ = ab.shape
    stacked = features // HD * TEST
    per = tables // len(q_dtypes)
    return pl.pallas_call(
        lambda *refs: query_grad_kernel(len(pieces), *refs),
        in_specs=[smem_spec()] + [vmem_spec()] * (len(pieces) + 3),
        out_specs=[vmem_spec()] * (2 + len(q_dtypes)),
        out_shape=[
            jax.ShapeDtypeStruct((blocks, stacked), jnp.float32),
            jax.ShapeDtypeStruct((blocks, stacked), jnp.float32),
        ]
        + [jax.ShapeDtypeStruct((per, TEST, features), dtype) for dtype in q_dtypes],
        scratch_shapes=[
            pltpu.VMEM((3, tables, stacked), jnp.float32),
            pltpu.VMEM((tables, features, TEST), jnp.float32),
        ],
        compiler_params=params(10),
        name="query_grads",
    )(meta, *pieces, *sides, ab)


def row_grads_kernel(meta, c_ref, d_ref, q_side, g_side, state, dk_hbm, dv_hbm, dk_s, dv_s, out_sem):
    blocks, _, features = dk_s.shape
    stacked = features // HD * TEST
    turned = (((1,), (1,)), ((), ()))
    stores = []
    for b in range(blocks):
        for p in range(features // LANES):
            at = slice(p * LANES, (p + 1) * LANES)
            wide = slice(p * WIDE, (p + 1) * WIDE)
            c = c_ref[b : b + 1, wide]
            d = d_ref[b : b + 1, wide]
            q_t = two_heads(q_side[rows_of(meta, b, p, features), :])
            g_t = two_heads(g_side[rows_of(meta, b, p, features), :])
            for_u = (q_t * (c * SCORE_SCALE)).astype(jnp.bfloat16)
            for_e = jnp.concatenate([g_t * c, q_t * (d * SCORE_SCALE)], axis=0).astype(jnp.bfloat16)
            from_e = lax.dot_general(
                state[b, :, wide], for_e, turned, preferred_element_type=jnp.float32
            )
            moved = state[b, :, stacked + p * WIDE : stacked + (p + 1) * WIDE]
            from_u = lax.dot_general(moved, for_u, turned, preferred_element_type=jnp.float32)
            dv_s[b, :, at] = from_e[:, :LANES].astype(jnp.bfloat16)
            dk_s[b, :, at] = (from_u + from_e[:, LANES:]).astype(jnp.bfloat16)
        rows = pl.ds(b * BLK, BLK)
        stores += every_copy(
            [
                pltpu.make_async_copy(dk_s.at[b], dk_hbm.at[rows], out_sem.at[0, b]),
                pltpu.make_async_copy(dv_s.at[b], dv_hbm.at[rows], out_sem.at[1, b]),
            ]
        )
    for copy in stores:
        copy.wait()


def row_grads(meta, c, d, sides, state, features):
    blocks = state.shape[0]
    return pl.pallas_call(
        row_grads_kernel,
        in_specs=[smem_spec()] + [vmem_spec()] * 5,
        out_specs=[hbm_spec()] * 2,
        out_shape=[jax.ShapeDtypeStruct((blocks * BLK, features), jnp.bfloat16)] * 2,
        scratch_shapes=[
            pltpu.VMEM((blocks, BLK, features), jnp.bfloat16),
            pltpu.VMEM((blocks, BLK, features), jnp.bfloat16),
            pltpu.SemaphoreType.DMA((2, blocks)),
        ],
        compiler_params=params(10),
        name="row_grads",
    )(meta, c, d, *sides, state)


def local(small, query_rows, key_rows, value_rows, cotangent, train_rows, test_rows, block_table):
    features = query_rows.shape[1]
    blocks = key_rows.shape[0] // BLK
    tables = train_rows.shape[0]
    pair = lambda value: lax.ppermute(value, "pair", PAIR)
    step = lambda value, s: lax.ppermute(value, "rows", [(z, z ^ s) for z in range(4)])
    after = lambda value, other: lax.optimization_barrier((value, other))
    load = lambda entries: load_rows(small, entries, train_rows, test_rows, key_rows, value_rows)
    if small:
        held = 1
        near = [step(query_rows, s) for s in (1, 2, 3)]
        near_grads = [step(cotangent, s) for s in (1, 2, 3)]
        block_table, near[0] = after(block_table, near[0])
        meta, state = load(block_table)
        own, _ = after(query_rows, meta)
        near = [after(value, meta)[0] for value in near]
        queries = [query_rows, pair(own)]
        for value in near:
            queries += [value, pair(value)]
        q_side, state = block_weights(meta, held, queries, state, features, tables)
        *near_grads, q_side = lax.optimization_barrier((*near_grads, q_side))
        grads = [cotangent, pair(cotangent)]
        for value in near_grads:
            grads += [value, pair(value)]
    else:
        held = 0
        meta, state = load(block_table)
        queries = [lax.all_gather(query_rows, RP, axis=0, tiled=True)]
        q_side, state = block_weights(meta, held, queries, state, features, tables)
        grads = [lax.all_gather(cotangent, RP, axis=0, tiled=True)]
    g_side, tab, state = moved_weights(meta, held, grads, q_side, state, features, tables)
    if small:
        near = [step(tab, s) for s in (1, 2, 3)]
        ab, state = query_sums(features, state)
        *near, ab = lax.optimization_barrier((*near, ab))
        stats = [tab, pair(tab)]
        for value in near:
            stats += [value, pair(value)]
        dtypes = [jnp.float32, jnp.bfloat16]
    else:
        ab, state = query_sums(features, state)
        peak = lax.pmax(tab[0], RP)
        weight = jnp.exp2(tab[0] - peak)
        total, part = lax.psum(jnp.stack([weight, weight * tab[1]]), RP)
        stats = [jnp.stack([peak + jnp.log2(total), part / total])]
        dtypes = [jnp.float32]
    c, d, *q_terms = query_grads(meta, tables, stats, (q_side, g_side), ab, dtypes)
    if small:
        keep, send = q_terms
        total = keep + pair(send).astype(jnp.float32)
        low = total.astype(jnp.bfloat16)
        got = [step(low[s - 1], s) for s in (1, 2, 3)]
        low, c = lax.optimization_barrier((low, c))
        key_grad, value_grad = row_grads(meta, c, d, (q_side, g_side), state, features)
        query_grad = total[3]
        for value in got:
            query_grad = query_grad + value.astype(jnp.float32)
    else:
        query_grad = lax.psum_scatter(
            q_terms[0].reshape(tables * TEST, features), RP, scatter_dimension=0, tiled=True
        )
        key_grad, value_grad = row_grads(meta, c, d, (q_side, g_side), state, features)
    return query_grad.astype(jnp.bfloat16), key_grad, value_grad


def solution(mesh):
    sizes = mesh.shape
    tables_of_rows = P(("groups", "rows", "pair"), "mp")
    in_specs = (tables_of_rows,) * 4 + (P("groups"),) * 3
    out_specs = (tables_of_rows,) * 3

    def run(query_rows, *rest):
        local_rows = query_rows.shape[0] // (sizes["groups"] * sizes["rows"] * sizes["pair"])
        small = sizes["rows"] == 4 and sizes["pair"] == 2 and local_rows == TEST
        return jax.shard_map(
            lambda *args: local(small, *args),
            mesh=mesh,
            in_specs=in_specs,
            out_specs=out_specs,
            check_vma=False,
        )(query_rows, *rest)

    return run
```

```python
import math

import jax
import jax.numpy as jnp
from jax import lax
from jax.experimental import pallas as pl
from jax.experimental.pallas import tpu as pltpu
from jax.sharding import PartitionSpec as P

HD = 64
TEST = 128
BLK = 512
LANES = 128
WIDE = 2 * TEST
CHUNK = 64

NEG = -1e30
SCORE_SCALE = 1.0 / math.sqrt(HD)
LOG2_SCALE = SCORE_SCALE * math.log2(math.e)
RP = ("rows", "pair")
PAIR = [(0, 1), (1, 0)]


def params(mib):
    return pltpu.CompilerParams(vmem_limit_bytes=mib * 1024 * 1024)


def two_heads(rows):
    feature = lax.broadcasted_iota(jnp.int32, rows.shape, 0)
    zero = jnp.zeros_like(rows)
    return jnp.concatenate(
        [jnp.where(feature < HD, rows, zero), jnp.where(feature < HD, zero, rows)], axis=1
    )


def every_copy(copies):
    for copy in copies:
        copy.start()
    return copies


OWNER, LIVE, TESTN, SLOT_IN, TABLE_OF, SLOT_OUT = range(6)


def vmem_spec():
    return pl.BlockSpec(memory_space=pltpu.VMEM)


def smem_spec():
    return pl.BlockSpec(memory_space=pltpu.SMEM)


def hbm_spec():
    return pl.BlockSpec(memory_space=pltpu.HBM)


def in_hbm(value):
    return pltpu.with_memory_space_constraint(value, pltpu.HBM)


def load_kernel(small, table_hbm, train_hbm, test_hbm, key_hbm, value_hbm, meta, state, *scratch):
    block_table, train_rows, test_rows, count, sem, small_sem = scratch
    entries = every_copy(
        [
            pltpu.make_async_copy(table_hbm, block_table, small_sem.at[0]),
            pltpu.make_async_copy(train_hbm, train_rows, small_sem.at[1]),
            pltpu.make_async_copy(test_hbm, test_rows, small_sem.at[2]),
        ]
    )
    blocks = state.shape[0]
    features = key_hbm.shape[1]
    stacked = features // HD * TEST
    loads = []
    for b in range(blocks):
        for n, source in enumerate((key_hbm, value_hbm)):
            lanes = pl.ds(2 * stacked + n * features, features)
            loads.append(
                pltpu.make_async_copy(
                    source.at[pl.ds(b * BLK, BLK)], state.at[b, :, lanes], sem.at[n, b]
                )
            )
    every_copy(loads)
    chip = lax.axis_index("rows").astype(jnp.int32)
    core = lax.axis_index("pair").astype(jnp.int32)
    first = lax.axis_index(RP).astype(jnp.int32) * blocks
    for copy in entries:
        copy.wait()
    for t in range(train_rows.shape[0]):
        count[t] = 0
        meta[TESTN, t] = test_rows[t]
        if small:
            away = (t // 2) ^ chip
            not_mine = (t % 2) ^ core
            meta[SLOT_IN, t] = 2 * away + not_mine
            meta[TABLE_OF, t] = 2 * away + not_mine
            meta[SLOT_OUT, t] = 4 * not_mine + ((away + 3) & 3)
        else:
            for row in (SLOT_IN, TABLE_OF, SLOT_OUT):
                meta[row, t] = t

    def earlier(n, carry):
        table = block_table[n]
        count[table] = count[table] + 1
        return carry

    lax.fori_loop(0, first, earlier, 0)
    for b in range(blocks):
        table = block_table[first + b]
        meta[OWNER, b] = table
        meta[LIVE, b] = jnp.minimum(train_rows[table] - count[table] * BLK, BLK)
        count[table] = count[table] + 1
    for copy in loads:
        copy.wait()


def load_rows(small, block_table, train_rows, test_rows, key_rows, value_rows):
    tables = train_rows.shape[0]
    features = key_rows.shape[1]
    blocks = key_rows.shape[0] // BLK
    stacked = features // HD * TEST
    return pl.pallas_call(
        lambda *refs: load_kernel(small, *refs),
        in_specs=[hbm_spec()] * 5,
        out_specs=[smem_spec(), vmem_spec()],
        out_shape=[
            pltpu.SMEM((6, max(blocks, tables)), jnp.int32),
            pltpu.VMEM((blocks, BLK, 2 * stacked + 2 * features), jnp.bfloat16),
        ],
        scratch_shapes=[
            pltpu.SMEM(block_table.shape, jnp.int32),
            pltpu.SMEM((tables,), jnp.int32),
            pltpu.SMEM((tables,), jnp.int32),
            pltpu.SMEM((tables,), jnp.int32),
            pltpu.SemaphoreType.DMA((2, blocks)),
            pltpu.SemaphoreType.DMA((3,)),
        ],
        compiler_params=params(4),
        name="load_rows",
    )(*map(in_hbm, (block_table, train_rows, test_rows, key_rows, value_rows)))


def turn_pieces(pieces, held, held_s, sem, store):
    early = every_copy(
        [pltpu.make_async_copy(pieces[n], held_s.at[n], sem.at[n]) for n in range(held)]
    )
    at_slot = held
    for piece in pieces[held:]:
        for m in range(piece.shape[0] // TEST):
            store(at_slot, piece[m * TEST : (m + 1) * TEST, :].T)
            at_slot += 1
    for copy in early:
        copy.wait()
    for n in range(held):
        store(n, held_s[n].T)


def fold(values, op):
    return op(values.reshape(CHUNK // 8, 8, WIDE), axis=0)


def rows_of(meta, b, p, features):
    at_slot = meta[SLOT_IN, meta[OWNER, b]]
    return pl.ds(pl.multiple_of(at_slot * features + p * LANES, LANES), LANES)


def put_heads(side, first, b, p, features, row):
    at = first + b * features // HD + 2 * p
    side[at : at + 1, :] = row[:, :TEST]
    side[at + 1 : at + 2, :] = row[:, TEST:]


def get_heads(side, row, heads):
    return jnp.concatenate([side[row + h : row + h + 1, :] for h in range(heads)], axis=1)


def units_of(blocks, features):
    return [(b, p) for b in range(blocks) for p in range(features // LANES)]


def weights_kernel(count, held, meta, *refs):
    pieces = refs[:count]
    state, side, state_out, scores_s, held_s, sem = refs[count:]
    _, features = held_s.shape[1:]
    stacked = features // HD * TEST
    first_peak = side.shape[0] - state.shape[0] * features // HD
    units = units_of(state.shape[0], features)

    def store(at_slot, turned):
        side[at_slot * features : (at_slot + 1) * features, :] = turned.astype(jnp.float32)

    turn_pieces(pieces, held, held_s, sem, store)
    peaks = [None] * len(units)
    for t in range(len(units) + 1):
        if t < len(units):
            b, p = units[t]
            live = meta[LIVE, b]
            queries = two_heads(side[rows_of(meta, b, p, features), :]).astype(jnp.bfloat16)
            peak = jnp.full((8, WIDE), NEG, jnp.float32)
        for r in range(0, BLK, CHUNK):
            rows = slice(r, r + CHUNK)
            if t > 0:
                last_b, last_p = units[t - 1]
                weights = jnp.exp2(scores_s[(t - 1) % 2, rows, :] * LOG2_SCALE - peaks[t - 1])
                state_out[last_b, rows, last_p * WIDE : (last_p + 1) * WIDE] = weights.astype(
                    jnp.bfloat16
                )
            if t < len(units):
                keys = state[b, rows, 2 * stacked + p * LANES : 2 * stacked + (p + 1) * LANES]
                scores = jnp.dot(keys, queries, preferred_element_type=jnp.float32)
                row = lax.broadcasted_iota(jnp.int32, scores.shape, 0)
                scores = jnp.where(row < live - r, scores, NEG)
                scores_s[t % 2, rows, :] = scores
                peak = jnp.maximum(peak, fold(scores, jnp.max))
        if t < len(units):
            peaks[t] = jnp.max(peak, axis=0, keepdims=True) * LOG2_SCALE
    for (b, p), peak in zip(units, peaks):
        put_heads(side, first_peak, b, p, features, peak)


def block_weights(meta, held, pieces, state, features, tables):
    blocks = state.shape[0]
    count = len(pieces)
    pieces = [in_hbm(piece) if n < held else piece for n, piece in enumerate(pieces)]
    specs = [hbm_spec() if n < held else vmem_spec() for n in range(count)]
    return pl.pallas_call(
        lambda *refs: weights_kernel(count, held, *refs),
        in_specs=[smem_spec()] + specs + [vmem_spec()],
        out_specs=[vmem_spec()] * 2,
        out_shape=[
            pltpu.VMEM((tables * features + blocks * features // HD, TEST), jnp.float32),
            pltpu.VMEM(state.shape, jnp.bfloat16),
        ],
        input_output_aliases={count + 1: 1},
        scratch_shapes=[
            pltpu.VMEM((2, BLK, WIDE), jnp.float32),
            pltpu.VMEM((max(held, 1), TEST, features), jnp.bfloat16),
            pltpu.SemaphoreType.DMA((max(held, 1),)),
        ],
        compiler_params=params(10),
        name="block_weights",
    )(meta, *pieces, state)


def moved_kernel(count, held, meta, *refs):
    pieces = refs[:count]
    q_side, state, side, tab_ref, state_out = refs[count : count + 5]
    dprobs_s, held_s, sem = refs[count + 5 :]
    tables = tab_ref.shape[1]
    _, features = held_s.shape[1:]
    stacked = features // HD * TEST
    blocks = state.shape[0]
    heads = features // HD
    first = tables * features
    units = units_of(blocks, features)
    query = lax.broadcasted_iota(jnp.int32, (features, TEST), 1)

    def store(at_slot, turned):
        live = query < meta[TESTN, meta[TABLE_OF, at_slot]]
        turned = jnp.where(live, turned, jnp.zeros_like(turned)).astype(jnp.float32)
        side[at_slot * features : (at_slot + 1) * features, :] = turned

    turn_pieces(pieces, held, held_s, sem, store)
    means, masses = [None] * len(units), [None] * len(units)
    zero = jnp.zeros((8, WIDE), jnp.float32)
    for t in range(len(units) + 1):
        if t < len(units):
            b, p = units[t]
            grads = two_heads(side[rows_of(meta, b, p, features), :]).astype(jnp.bfloat16)
            mass = part = zero
        for r in range(0, BLK, CHUNK):
            rows = slice(r, r + CHUNK)
            if t > 0:
                last_b, last_p = units[t - 1]
                weights = state[last_b, rows, last_p * WIDE : (last_p + 1) * WIDE]
                moved = weights.astype(jnp.float32) * (dprobs_s[(t - 1) % 2, rows, :] - means[t - 1])
                lanes = slice(stacked + last_p * WIDE, stacked + (last_p + 1) * WIDE)
                state_out[last_b, rows, lanes] = moved.astype(jnp.bfloat16)
            if t < len(units):
                lane = 2 * stacked + features + p * LANES
                values = state[b, rows, lane : lane + LANES]
                dprobs = jnp.dot(values, grads, preferred_element_type=jnp.float32)
                weights = state[b, rows, p * WIDE : (p + 1) * WIDE].astype(jnp.float32)
                mass = mass + fold(weights, jnp.sum)
                part = part + fold(weights * dprobs, jnp.sum)
                dprobs_s[t % 2, rows, :] = dprobs
        if t < len(units):
            mass = jnp.sum(mass, axis=0, keepdims=True)
            masses[t] = mass
            means[t] = jnp.sum(part, axis=0, keepdims=True) / mass
    for (b, p), mean, mass in zip(units, means, masses):
        put_heads(side, first, b, p, features, mean)
        put_heads(side, first + blocks * heads, b, p, features, mass)
    table = lax.broadcasted_iota(jnp.int32, (tables, stacked), 0)
    peak = jnp.full((tables, stacked), NEG, jnp.float32)
    for b in range(blocks):
        own = table == meta[OWNER, b]
        block_peak = get_heads(q_side, first + b * heads, heads)
        peak = jnp.where(own, jnp.maximum(peak, block_peak), peak)
    total = part = jnp.zeros((tables, stacked), jnp.float32)
    for b in range(blocks):
        own = table == meta[OWNER, b]
        at = b * (features // LANES)
        mass = jnp.concatenate(masses[at : at + features // LANES], axis=1)
        mean = jnp.concatenate(means[at : at + features // LANES], axis=1)
        block_peak = get_heads(q_side, first + b * heads, heads)
        scaled = jnp.where(own, jnp.exp2(block_peak - peak) * mass, 0.0)
        total = total + scaled
        part = part + scaled * mean
    here = total > 0.0
    mass = jnp.where(here, total, 1.0)
    tab_ref[0] = jnp.where(here, peak + jnp.log2(mass), NEG)
    tab_ref[1] = part / mass


def moved_weights(meta, held, pieces, q_side, state, features, tables):
    blocks = state.shape[0]
    stacked = features // HD * TEST
    count = len(pieces)
    pieces = [in_hbm(piece) if n < held else piece for n, piece in enumerate(pieces)]
    specs = [hbm_spec() if n < held else vmem_spec() for n in range(count)]
    return pl.pallas_call(
        lambda *refs: moved_kernel(count, held, *refs),
        in_specs=[smem_spec()] + specs + [vmem_spec()] * 2,
        out_specs=[vmem_spec()] * 3,
        out_shape=[
            pltpu.VMEM((tables * features + 2 * blocks * features // HD, TEST), jnp.float32),
            jax.ShapeDtypeStruct((2, tables, stacked), jnp.float32),
            pltpu.VMEM(state.shape, jnp.bfloat16),
        ],
        input_output_aliases={count + 2: 2},
        scratch_shapes=[
            pltpu.VMEM((2, BLK, WIDE), jnp.float32),
            pltpu.VMEM((max(held, 1), TEST, features), jnp.bfloat16),
            pltpu.SemaphoreType.DMA((max(held, 1),)),
        ],
        compiler_params=params(10),
        name="moved_weights",
    )(meta, *pieces, q_side, state)


def query_sums_kernel(state, ab_ref, state_out):
    blocks, _, features, _ = ab_ref.shape
    stacked = features // HD * TEST
    for b in range(blocks):
        for p in range(features // LANES):
            keys = state[b, :, 2 * stacked + p * LANES : 2 * stacked + (p + 1) * LANES]
            for n, first in enumerate((stacked, 0)):
                values = state[b, :, first + p * WIDE : first + (p + 1) * WIDE]
                product = lax.dot_general(
                    keys, values, (((0,), (0,)), ((), ())), preferred_element_type=jnp.float32
                )
                ab_ref[b, n, p * LANES : p * LANES + HD, :] = product[:HD, :TEST]
                ab_ref[b, n, p * LANES + HD : (p + 1) * LANES, :] = product[HD:, TEST:]


def query_sums(features, state):
    blocks = state.shape[0]
    return pl.pallas_call(
        query_sums_kernel,
        in_specs=[vmem_spec()],
        out_specs=[vmem_spec()] * 2,
        out_shape=[
            pltpu.VMEM((blocks, 2, features, TEST), jnp.float32),
            pltpu.VMEM(state.shape, jnp.bfloat16),
        ],
        input_output_aliases={0: 1},
        compiler_params=params(8),
        name="query_sums",
    )(state)


def merged(pieces):
    peak = pieces[0][0]
    for piece in pieces[1:]:
        peak = jnp.maximum(peak, piece[0])
    mass = part = 0.0
    for piece in pieces:
        weight = jnp.exp2(piece[0] - peak)
        mass = mass + weight
        part = part + piece[1] * weight
    return peak, mass, part / mass


def query_grad_kernel(count, meta, *refs):
    pieces = refs[:count]
    q_side, g_side, ab_ref = refs[count : count + 3]
    c_ref, d_ref, *q_refs = refs[count + 3 : -2]
    tab_s, acc_s = refs[-2:]
    blocks = ab_ref.shape[0]
    tables, features, _ = acc_s.shape
    heads = features // HD
    tab_s[0], tab_s[1], tab_s[2] = merged(pieces)
    acc_s[...] = jnp.zeros_like(acc_s)
    for b in range(blocks):
        at = meta[SLOT_OUT, meta[OWNER, b]]
        table = pl.ds(meta[OWNER, b], 1)
        row = tables * features + b * heads
        mass = tab_s[1, table, :]
        c = jnp.exp2(get_heads(q_side, row, heads) - tab_s[0, table, :]) / mass
        d = c * (get_heads(g_side, row, heads) - tab_s[2, table, :])
        c_ref[b : b + 1, :] = c
        d_ref[b : b + 1, :] = d
        for h in range(heads):
            rows = slice(h * HD, (h + 1) * HD)
            lanes = slice(h * TEST, (h + 1) * TEST)
            acc_s[at, rows, :] += c[:, lanes] * ab_ref[b, 0, rows, :] + d[:, lanes] * ab_ref[b, 1, rows, :]
    per = tables // len(q_refs)
    for n in range(tables):
        ref = q_refs[n // per]
        ref[n % per] = (acc_s[n] * SCORE_SCALE).T.astype(ref.dtype)


def query_grads(meta, tables, pieces, sides, ab, q_dtypes):
    blocks, _, features, _ = ab.shape
    stacked = features // HD * TEST
    per = tables // len(q_dtypes)
    return pl.pallas_call(
        lambda *refs: query_grad_kernel(len(pieces), *refs),
        in_specs=[smem_spec()] + [vmem_spec()] * (len(pieces) + 3),
        out_specs=[vmem_spec()] * (2 + len(q_dtypes)),
        out_shape=[
            jax.ShapeDtypeStruct((blocks, stacked), jnp.float32),
            jax.ShapeDtypeStruct((blocks, stacked), jnp.float32),
        ]
        + [jax.ShapeDtypeStruct((per, TEST, features), dtype) for dtype in q_dtypes],
        scratch_shapes=[
            pltpu.VMEM((3, tables, stacked), jnp.float32),
            pltpu.VMEM((tables, features, TEST), jnp.float32),
        ],
        compiler_params=params(10),
        name="query_grads",
    )(meta, *pieces, *sides, ab)


def row_grads_kernel(meta, c_ref, d_ref, q_side, g_side, state, dk_hbm, dv_hbm, dk_s, dv_s, out_sem):
    blocks, _, features = dk_s.shape
    stacked = features // HD * TEST
    turned = (((1,), (1,)), ((), ()))
    stores = []
    for b in range(blocks):
        for p in range(features // LANES):
            at = slice(p * LANES, (p + 1) * LANES)
            wide = slice(p * WIDE, (p + 1) * WIDE)
            c = c_ref[b : b + 1, wide]
            d = d_ref[b : b + 1, wide]
            q_t = two_heads(q_side[rows_of(meta, b, p, features), :])
            g_t = two_heads(g_side[rows_of(meta, b, p, features), :])
            for_u = (q_t * (c * SCORE_SCALE)).astype(jnp.bfloat16)
            for_e = jnp.concatenate([g_t * c, q_t * (d * SCORE_SCALE)], axis=0).astype(jnp.bfloat16)
            from_e = lax.dot_general(
                state[b, :, wide], for_e, turned, preferred_element_type=jnp.float32
            )
            moved = state[b, :, stacked + p * WIDE : stacked + (p + 1) * WIDE]
            from_u = lax.dot_general(moved, for_u, turned, preferred_element_type=jnp.float32)
            dv_s[b, :, at] = from_e[:, :LANES].astype(jnp.bfloat16)
            dk_s[b, :, at] = (from_u + from_e[:, LANES:]).astype(jnp.bfloat16)
        rows = pl.ds(b * BLK, BLK)
        stores += every_copy(
            [
                pltpu.make_async_copy(dk_s.at[b], dk_hbm.at[rows], out_sem.at[0, b]),
                pltpu.make_async_copy(dv_s.at[b], dv_hbm.at[rows], out_sem.at[1, b]),
            ]
        )
    for copy in stores:
        copy.wait()


def row_grads(meta, c, d, sides, state, features):
    blocks = state.shape[0]
    return pl.pallas_call(
        row_grads_kernel,
        in_specs=[smem_spec()] + [vmem_spec()] * 5,
        out_specs=[hbm_spec()] * 2,
        out_shape=[jax.ShapeDtypeStruct((blocks * BLK, features), jnp.bfloat16)] * 2,
        scratch_shapes=[
            pltpu.VMEM((blocks, BLK, features), jnp.bfloat16),
            pltpu.VMEM((blocks, BLK, features), jnp.bfloat16),
            pltpu.SemaphoreType.DMA((2, blocks)),
        ],
        compiler_params=params(10),
        name="row_grads",
    )(meta, c, d, *sides, state)


def local(small, query_rows, key_rows, value_rows, cotangent, train_rows, test_rows, block_table):
    features = query_rows.shape[1]
    blocks = key_rows.shape[0] // BLK
    tables = train_rows.shape[0]
    pair = lambda value: lax.ppermute(value, "pair", PAIR)
    step = lambda value, s: lax.ppermute(value, "rows", [(z, z ^ s) for z in range(4)])
    after = lambda value, other: lax.optimization_barrier((value, other))
    load = lambda entries: load_rows(small, entries, train_rows, test_rows, key_rows, value_rows)
    if small:
        held = 1
        near = [step(query_rows, 1), step(query_rows, 2)]
        near_grads = [step(cotangent, 1), step(cotangent, 2)]
        near.append(step(near[1], 1))
        near_grads.append(step(near_grads[1], 1))
        block_table, near[0] = after(block_table, near[0])
        meta, state = load(block_table)
        own, near[0], near[1], meta = lax.optimization_barrier((query_rows, near[0], near[1], meta))
        queries = [query_rows, pair(own)]
        for value in near:
            queries += [value, pair(value)]
        q_side, state = block_weights(meta, held, queries, state, features, tables)
        own, *near_grads, q_side = lax.optimization_barrier((cotangent, *near_grads, q_side))
        grads = [cotangent, pair(own)]
        for value in near_grads:
            grads += [value, pair(value)]
    else:
        held = 0
        meta, state = load(block_table)
        queries = [lax.all_gather(query_rows, RP, axis=0, tiled=True)]
        q_side, state = block_weights(meta, held, queries, state, features, tables)
        grads = [lax.all_gather(cotangent, RP, axis=0, tiled=True)]
    g_side, tab, state = moved_weights(meta, held, grads, q_side, state, features, tables)
    if small:
        near = [step(tab, s) for s in (1, 2, 3)]
        ab, state = query_sums(features, state)
        *near, ab = lax.optimization_barrier((*near, ab))
        stats = [tab, pair(tab)]
        for value in near:
            stats += [value, pair(value)]
        dtypes = [jnp.float32, jnp.bfloat16]
    else:
        ab, state = query_sums(features, state)
        peak = lax.pmax(tab[0], RP)
        weight = jnp.exp2(tab[0] - peak)
        total, part = lax.psum(jnp.stack([weight, weight * tab[1]]), RP)
        stats = [jnp.stack([peak + jnp.log2(total), part / total])]
        dtypes = [jnp.float32]
    c, d, *q_terms = query_grads(meta, tables, stats, (q_side, g_side), ab, dtypes)
    if small:
        keep, send = q_terms
        total = keep + pair(send).astype(jnp.float32)
        low = total.astype(jnp.bfloat16)
        got = [step(low[s - 1], s) for s in (1, 2, 3)]
        low, c = lax.optimization_barrier((low, c))
        key_grad, value_grad = row_grads(meta, c, d, (q_side, g_side), state, features)
        query_grad = total[3]
        for value in got:
            query_grad = query_grad + value.astype(jnp.float32)
    else:
        query_grad = lax.psum_scatter(
            q_terms[0].reshape(tables * TEST, features), RP, scatter_dimension=0, tiled=True
        )
        key_grad, value_grad = row_grads(meta, c, d, (q_side, g_side), state, features)
    return query_grad.astype(jnp.bfloat16), key_grad, value_grad


def solution(mesh):
    sizes = mesh.shape
    tables_of_rows = P(("groups", "rows", "pair"), "mp")
    in_specs = (tables_of_rows,) * 4 + (P("groups"),) * 3
    out_specs = (tables_of_rows,) * 3

    def run(query_rows, *rest):
        local_rows = query_rows.shape[0] // (sizes["groups"] * sizes["rows"] * sizes["pair"])
        small = sizes["rows"] == 4 and sizes["pair"] == 2 and local_rows == TEST
        return jax.shard_map(
            lambda *args: local(small, *args),
            mesh=mesh,
            in_specs=in_specs,
            out_specs=out_specs,
            check_vma=False,
        )(query_rows, *rest)

    return run
```

```python
import math

import jax
import jax.numpy as jnp
from jax import lax
from jax.experimental import pallas as pl
from jax.experimental.pallas import tpu as pltpu
from jax.sharding import PartitionSpec as P

HD = 64
TEST = 128
BLK = 512
LANES = 128
WIDE = 2 * TEST
CHUNK = 64

NEG = -1e30
SCORE_SCALE = 1.0 / math.sqrt(HD)
LOG2_SCALE = SCORE_SCALE * math.log2(math.e)
RP = ("rows", "pair")
PAIR = [(0, 1), (1, 0)]


def params(mib):
    return pltpu.CompilerParams(vmem_limit_bytes=mib * 1024 * 1024)


def two_heads(rows):
    feature = lax.broadcasted_iota(jnp.int32, rows.shape, 0)
    zero = jnp.zeros_like(rows)
    return jnp.concatenate(
        [jnp.where(feature < HD, rows, zero), jnp.where(feature < HD, zero, rows)], axis=1
    )


def every_copy(copies):
    for copy in copies:
        copy.start()
    return copies


OWNER, LIVE, TESTN, SLOT_IN, TABLE_OF, SLOT_OUT = range(6)


def vmem_spec():
    return pl.BlockSpec(memory_space=pltpu.VMEM)


def smem_spec():
    return pl.BlockSpec(memory_space=pltpu.SMEM)


def hbm_spec():
    return pl.BlockSpec(memory_space=pltpu.HBM)


def in_hbm(value):
    return pltpu.with_memory_space_constraint(value, pltpu.HBM)


def index_kernel(small, blocks, table_hbm, train_hbm, test_hbm, query_hbm, meta, query_ref, *scratch):
    block_table, train_rows, test_rows, count, small_sem = scratch
    entries = every_copy(
        [
            pltpu.make_async_copy(table_hbm, block_table, small_sem.at[0]),
            pltpu.make_async_copy(train_hbm, train_rows, small_sem.at[1]),
            pltpu.make_async_copy(test_hbm, test_rows, small_sem.at[2]),
            pltpu.make_async_copy(query_hbm, query_ref, small_sem.at[3]),
        ]
    )
    chip = lax.axis_index("rows").astype(jnp.int32)
    core = lax.axis_index("pair").astype(jnp.int32)
    first = lax.axis_index(RP).astype(jnp.int32) * blocks
    for copy in entries:
        copy.wait()
    for t in range(train_rows.shape[0]):
        count[t] = 0
        meta[TESTN, t] = test_rows[t]
        if small:
            away = (t // 2) ^ chip
            not_mine = (t % 2) ^ core
            meta[SLOT_IN, t] = 2 * away + not_mine
            meta[TABLE_OF, t] = 2 * away + not_mine
            meta[SLOT_OUT, t] = 4 * not_mine + ((away + 3) & 3)
        else:
            for row in (SLOT_IN, TABLE_OF, SLOT_OUT):
                meta[row, t] = t

    def earlier(n, carry):
        table = block_table[n]
        count[table] = count[table] + 1
        return carry

    lax.fori_loop(0, first, earlier, 0)
    for b in range(blocks):
        table = block_table[first + b]
        meta[OWNER, b] = table
        meta[LIVE, b] = jnp.minimum(train_rows[table] - count[table] * BLK, BLK)
        count[table] = count[table] + 1


def index_table(small, blocks, block_table, train_rows, test_rows, query_rows):
    tables = train_rows.shape[0]
    return pl.pallas_call(
        lambda *refs: index_kernel(small, blocks, *refs),
        in_specs=[hbm_spec()] * 4,
        out_specs=[smem_spec(), vmem_spec()],
        out_shape=[
            pltpu.SMEM((6, max(blocks, tables)), jnp.int32),
            pltpu.VMEM(query_rows.shape, query_rows.dtype),
        ],
        scratch_shapes=[
            pltpu.SMEM(block_table.shape, jnp.int32),
            pltpu.SMEM((tables,), jnp.int32),
            pltpu.SMEM((tables,), jnp.int32),
            pltpu.SMEM((tables,), jnp.int32),
            pltpu.SemaphoreType.DMA((4,)),
        ],
        name="index_table",
    )(*map(in_hbm, (block_table, train_rows, test_rows, query_rows)))


def turn_pieces(pieces, store):
    at_slot = 0
    for piece in pieces:
        for m in range(piece.shape[0] // TEST):
            store(at_slot, piece[m * TEST : (m + 1) * TEST, :].T)
            at_slot += 1


def fold(values, op):
    return op(values.reshape(CHUNK // 8, 8, WIDE), axis=0)


def rows_of(meta, b, p, features):
    at_slot = meta[SLOT_IN, meta[OWNER, b]]
    return pl.ds(pl.multiple_of(at_slot * features + p * LANES, LANES), LANES)


def put_heads(side, first, b, p, features, row):
    at = first + b * features // HD + 2 * p
    side[at : at + 1, :] = row[:, :TEST]
    side[at + 1 : at + 2, :] = row[:, TEST:]


def get_heads(side, row, heads):
    return jnp.concatenate([side[row + h : row + h + 1, :] for h in range(heads)], axis=1)


def units_of(blocks, features):
    return [(b, p) for b in range(blocks) for p in range(features // LANES)]


def weights_kernel(count, meta, *refs):
    pieces = refs[:count]
    key_hbm, value_hbm, side, state, scores_s, sem = refs[count:]
    blocks = state.shape[0]
    features = key_hbm.shape[1]
    stacked = features // HD * TEST
    first_peak = side.shape[0] - blocks * features // HD
    units = units_of(blocks, features)
    loads = []
    for n, source in enumerate((key_hbm, value_hbm)):
        lanes = pl.ds(2 * stacked + n * features, features)
        loads.append(
            every_copy(
                [
                    pltpu.make_async_copy(
                        source.at[pl.ds(b * BLK, BLK)], state.at[b, :, lanes], sem.at[n, b]
                    )
                    for b in range(blocks)
                ]
            )
        )

    def store(at_slot, turned):
        side[at_slot * features : (at_slot + 1) * features, :] = turned.astype(jnp.float32)

    turn_pieces(pieces, store)
    peaks = [None] * len(units)
    for t in range(len(units) + 1):
        if t < len(units):
            b, p = units[t]
            if p == 0:
                loads[0][b].wait()
            live = meta[LIVE, b]
            queries = two_heads(side[rows_of(meta, b, p, features), :]).astype(jnp.bfloat16)
            peak = jnp.full((8, WIDE), NEG, jnp.float32)
        for r in range(0, BLK, CHUNK):
            rows = slice(r, r + CHUNK)
            if t > 0:
                last_b, last_p = units[t - 1]
                weights = jnp.exp2(scores_s[(t - 1) % 2, rows, :] * LOG2_SCALE - peaks[t - 1])
                state[last_b, rows, last_p * WIDE : (last_p + 1) * WIDE] = weights.astype(jnp.bfloat16)
            if t < len(units):
                keys = state[b, rows, 2 * stacked + p * LANES : 2 * stacked + (p + 1) * LANES]
                scores = jnp.dot(keys, queries, preferred_element_type=jnp.float32)
                row = lax.broadcasted_iota(jnp.int32, scores.shape, 0)
                scores = jnp.where(row < live - r, scores, NEG)
                scores_s[t % 2, rows, :] = scores
                peak = jnp.maximum(peak, fold(scores, jnp.max))
        if t < len(units):
            peaks[t] = jnp.max(peak, axis=0, keepdims=True) * LOG2_SCALE
    for (b, p), peak in zip(units, peaks):
        put_heads(side, first_peak, b, p, features, peak)
    for copy in loads[1]:
        copy.wait()


def block_weights(meta, pieces, key_rows, value_rows, tables):
    features = key_rows.shape[1]
    blocks = key_rows.shape[0] // BLK
    stacked = features // HD * TEST
    return pl.pallas_call(
        lambda *refs: weights_kernel(len(pieces), *refs),
        in_specs=[smem_spec()] + [vmem_spec()] * len(pieces) + [hbm_spec()] * 2,
        out_specs=[vmem_spec()] * 2,
        out_shape=[
            pltpu.VMEM((tables * features + blocks * features // HD, TEST), jnp.float32),
            pltpu.VMEM((blocks, BLK, 2 * stacked + 2 * features), jnp.bfloat16),
        ],
        scratch_shapes=[
            pltpu.VMEM((2, BLK, WIDE), jnp.float32),
            pltpu.SemaphoreType.DMA((2, blocks)),
        ],
        compiler_params=params(10),
        name="block_weights",
    )(meta, *pieces, in_hbm(key_rows), in_hbm(value_rows))


def moved_kernel(count, features, meta, *refs):
    pieces = refs[:count]
    q_side, state, side, tab_ref, state_out = refs[count : count + 5]
    dprobs_s = refs[count + 5]
    tables = tab_ref.shape[1]
    stacked = features // HD * TEST
    blocks = state.shape[0]
    heads = features // HD
    first = tables * features
    units = units_of(blocks, features)
    query = lax.broadcasted_iota(jnp.int32, (features, TEST), 1)

    def store(at_slot, turned):
        live = query < meta[TESTN, meta[TABLE_OF, at_slot]]
        turned = jnp.where(live, turned, jnp.zeros_like(turned)).astype(jnp.float32)
        side[at_slot * features : (at_slot + 1) * features, :] = turned

    turn_pieces(pieces, store)
    means, masses = [None] * len(units), [None] * len(units)
    zero = jnp.zeros((8, WIDE), jnp.float32)
    for t in range(len(units) + 1):
        if t < len(units):
            b, p = units[t]
            grads = two_heads(side[rows_of(meta, b, p, features), :]).astype(jnp.bfloat16)
            mass = part = zero
        for r in range(0, BLK, CHUNK):
            rows = slice(r, r + CHUNK)
            if t > 0:
                last_b, last_p = units[t - 1]
                weights = state[last_b, rows, last_p * WIDE : (last_p + 1) * WIDE]
                moved = weights.astype(jnp.float32) * (dprobs_s[(t - 1) % 2, rows, :] - means[t - 1])
                lanes = slice(stacked + last_p * WIDE, stacked + (last_p + 1) * WIDE)
                state_out[last_b, rows, lanes] = moved.astype(jnp.bfloat16)
            if t < len(units):
                lane = 2 * stacked + features + p * LANES
                values = state[b, rows, lane : lane + LANES]
                dprobs = jnp.dot(values, grads, preferred_element_type=jnp.float32)
                weights = state[b, rows, p * WIDE : (p + 1) * WIDE].astype(jnp.float32)
                mass = mass + fold(weights, jnp.sum)
                part = part + fold(weights * dprobs, jnp.sum)
                dprobs_s[t % 2, rows, :] = dprobs
        if t < len(units):
            mass = jnp.sum(mass, axis=0, keepdims=True)
            masses[t] = mass
            means[t] = jnp.sum(part, axis=0, keepdims=True) / mass
    for (b, p), mean, mass in zip(units, means, masses):
        put_heads(side, first, b, p, features, mean)
        put_heads(side, first + blocks * heads, b, p, features, mass)
    table = lax.broadcasted_iota(jnp.int32, (tables, stacked), 0)
    peak = jnp.full((tables, stacked), NEG, jnp.float32)
    for b in range(blocks):
        own = table == meta[OWNER, b]
        block_peak = get_heads(q_side, first + b * heads, heads)
        peak = jnp.where(own, jnp.maximum(peak, block_peak), peak)
    total = part = jnp.zeros((tables, stacked), jnp.float32)
    for b in range(blocks):
        own = table == meta[OWNER, b]
        at = b * (features // LANES)
        mass = jnp.concatenate(masses[at : at + features // LANES], axis=1)
        mean = jnp.concatenate(means[at : at + features // LANES], axis=1)
        block_peak = get_heads(q_side, first + b * heads, heads)
        scaled = jnp.where(own, jnp.exp2(block_peak - peak) * mass, 0.0)
        total = total + scaled
        part = part + scaled * mean
    here = total > 0.0
    mass = jnp.where(here, total, 1.0)
    tab_ref[0] = jnp.where(here, peak + jnp.log2(mass), NEG)
    tab_ref[1] = part / mass


def moved_weights(meta, pieces, q_side, state, features, tables):
    blocks = state.shape[0]
    stacked = features // HD * TEST
    count = len(pieces)
    return pl.pallas_call(
        lambda *refs: moved_kernel(count, features, *refs),
        in_specs=[smem_spec()] + [vmem_spec()] * (count + 2),
        out_specs=[vmem_spec()] * 3,
        out_shape=[
            pltpu.VMEM((tables * features + 2 * blocks * features // HD, TEST), jnp.float32),
            jax.ShapeDtypeStruct((2, tables, stacked), jnp.float32),
            pltpu.VMEM(state.shape, jnp.bfloat16),
        ],
        input_output_aliases={count + 2: 2},
        scratch_shapes=[pltpu.VMEM((2, BLK, WIDE), jnp.float32)],
        compiler_params=params(10),
        name="moved_weights",
    )(meta, *pieces, q_side, state)


def query_sums_kernel(state, ab_ref, state_out):
    blocks, _, features, _ = ab_ref.shape
    stacked = features // HD * TEST
    for b in range(blocks):
        for p in range(features // LANES):
            keys = state[b, :, 2 * stacked + p * LANES : 2 * stacked + (p + 1) * LANES]
            for n, first in enumerate((stacked, 0)):
                values = state[b, :, first + p * WIDE : first + (p + 1) * WIDE]
                product = lax.dot_general(
                    keys, values, (((0,), (0,)), ((), ())), preferred_element_type=jnp.float32
                )
                ab_ref[b, n, p * LANES : p * LANES + HD, :] = product[:HD, :TEST]
                ab_ref[b, n, p * LANES + HD : (p + 1) * LANES, :] = product[HD:, TEST:]


def query_sums(features, state):
    blocks = state.shape[0]
    return pl.pallas_call(
        query_sums_kernel,
        in_specs=[vmem_spec()],
        out_specs=[vmem_spec()] * 2,
        out_shape=[
            pltpu.VMEM((blocks, 2, features, TEST), jnp.float32),
            pltpu.VMEM(state.shape, jnp.bfloat16),
        ],
        input_output_aliases={0: 1},
        compiler_params=params(8),
        name="query_sums",
    )(state)


def merged(pieces):
    peak = pieces[0][0]
    for piece in pieces[1:]:
        peak = jnp.maximum(peak, piece[0])
    mass = part = 0.0
    for piece in pieces:
        weight = jnp.exp2(piece[0] - peak)
        mass = mass + weight
        part = part + piece[1] * weight
    return peak, mass, part / mass


def query_grad_kernel(count, meta, *refs):
    pieces = refs[:count]
    q_side, g_side, ab_ref = refs[count : count + 3]
    c_ref, d_ref, *q_refs = refs[count + 3 : -2]
    tab_s, acc_s = refs[-2:]
    blocks = ab_ref.shape[0]
    tables, features, _ = acc_s.shape
    heads = features // HD
    tab_s[0], tab_s[1], tab_s[2] = merged(pieces)
    acc_s[...] = jnp.zeros_like(acc_s)
    for b in range(blocks):
        at = meta[SLOT_OUT, meta[OWNER, b]]
        table = pl.ds(meta[OWNER, b], 1)
        row = tables * features + b * heads
        mass = tab_s[1, table, :]
        c = jnp.exp2(get_heads(q_side, row, heads) - tab_s[0, table, :]) / mass
        d = c * (get_heads(g_side, row, heads) - tab_s[2, table, :])
        c_ref[b : b + 1, :] = c
        d_ref[b : b + 1, :] = d
        for h in range(heads):
            rows = slice(h * HD, (h + 1) * HD)
            lanes = slice(h * TEST, (h + 1) * TEST)
            acc_s[at, rows, :] += c[:, lanes] * ab_ref[b, 0, rows, :] + d[:, lanes] * ab_ref[b, 1, rows, :]
    per = tables // len(q_refs)
    for n in range(tables):
        ref = q_refs[n // per]
        ref[n % per] = (acc_s[n] * SCORE_SCALE).T.astype(ref.dtype)


def query_grads(meta, tables, pieces, sides, ab, q_dtypes):
    blocks, _, features, _ = ab.shape
    stacked = features // HD * TEST
    per = tables // len(q_dtypes)
    return pl.pallas_call(
        lambda *refs: query_grad_kernel(len(pieces), *refs),
        in_specs=[smem_spec()] + [vmem_spec()] * (len(pieces) + 3),
        out_specs=[vmem_spec()] * (2 + len(q_dtypes)),
        out_shape=[
            jax.ShapeDtypeStruct((blocks, stacked), jnp.float32),
            jax.ShapeDtypeStruct((blocks, stacked), jnp.float32),
        ]
        + [jax.ShapeDtypeStruct((per, TEST, features), dtype) for dtype in q_dtypes],
        scratch_shapes=[
            pltpu.VMEM((3, tables, stacked), jnp.float32),
            pltpu.VMEM((tables, features, TEST), jnp.float32),
        ],
        compiler_params=params(10),
        name="query_grads",
    )(meta, *pieces, *sides, ab)


def row_grads_kernel(meta, c_ref, d_ref, q_side, g_side, state, dk_hbm, dv_hbm, dk_s, dv_s, out_sem):
    blocks, _, features = dk_s.shape
    stacked = features // HD * TEST
    turned = (((1,), (1,)), ((), ()))
    stores = []
    for b in range(blocks):
        for p in range(features // LANES):
            at = slice(p * LANES, (p + 1) * LANES)
            wide = slice(p * WIDE, (p + 1) * WIDE)
            c = c_ref[b : b + 1, wide]
            d = d_ref[b : b + 1, wide]
            q_t = two_heads(q_side[rows_of(meta, b, p, features), :])
            g_t = two_heads(g_side[rows_of(meta, b, p, features), :])
            for_u = (q_t * (c * SCORE_SCALE)).astype(jnp.bfloat16)
            for_e = jnp.concatenate([g_t * c, q_t * (d * SCORE_SCALE)], axis=0).astype(jnp.bfloat16)
            from_e = lax.dot_general(
                state[b, :, wide], for_e, turned, preferred_element_type=jnp.float32
            )
            moved = state[b, :, stacked + p * WIDE : stacked + (p + 1) * WIDE]
            from_u = lax.dot_general(moved, for_u, turned, preferred_element_type=jnp.float32)
            dv_s[b, :, at] = from_e[:, :LANES].astype(jnp.bfloat16)
            dk_s[b, :, at] = (from_u + from_e[:, LANES:]).astype(jnp.bfloat16)
        rows = pl.ds(b * BLK, BLK)
        stores += every_copy(
            [
                pltpu.make_async_copy(dk_s.at[b], dk_hbm.at[rows], out_sem.at[0, b]),
                pltpu.make_async_copy(dv_s.at[b], dv_hbm.at[rows], out_sem.at[1, b]),
            ]
        )
    for copy in stores:
        copy.wait()


def row_grads(meta, c, d, sides, state, features):
    blocks = state.shape[0]
    return pl.pallas_call(
        row_grads_kernel,
        in_specs=[smem_spec()] + [vmem_spec()] * 5,
        out_specs=[hbm_spec()] * 2,
        out_shape=[jax.ShapeDtypeStruct((blocks * BLK, features), jnp.bfloat16)] * 2,
        scratch_shapes=[
            pltpu.VMEM((blocks, BLK, features), jnp.bfloat16),
            pltpu.VMEM((blocks, BLK, features), jnp.bfloat16),
            pltpu.SemaphoreType.DMA((2, blocks)),
        ],
        compiler_params=params(10),
        name="row_grads",
    )(meta, c, d, *sides, state)


def local(small, query_rows, key_rows, value_rows, cotangent, train_rows, test_rows, block_table):
    features = query_rows.shape[1]
    blocks = key_rows.shape[0] // BLK
    tables = train_rows.shape[0]
    pair = lambda value: lax.ppermute(value, "pair", PAIR)
    step = lambda value, s: lax.ppermute(value, "rows", [(z, z ^ s) for z in range(4)])
    after = lambda value, other: lax.optimization_barrier((value, other))
    index = lambda entries: index_table(small, blocks, entries, train_rows, test_rows, query_rows)
    if small:
        near = [step(query_rows, s) for s in (1, 2, 3)]
        near_grads = [step(cotangent, 1), step(cotangent, 2)]
        near_grads.append(step(near_grads[1], 1))
        block_table, near[0] = after(block_table, near[0])
        meta, own = index(block_table)
        near[0], meta = after(near[0], meta)
        queries = [own, pair(own)]
        for value in near:
            queries += [value, pair(value)]
        q_side, state = block_weights(meta, queries, key_rows, value_rows, tables)
        own, *near_grads, q_side = lax.optimization_barrier((cotangent, *near_grads, q_side))
        grads = [own, pair(own)]
        for value in near_grads:
            grads += [value, pair(value)]
    else:
        meta, _ = index(block_table)
        queries = [lax.all_gather(query_rows, RP, axis=0, tiled=True)]
        q_side, state = block_weights(meta, queries, key_rows, value_rows, tables)
        grads = [lax.all_gather(cotangent, RP, axis=0, tiled=True)]
    g_side, tab, state = moved_weights(meta, grads, q_side, state, features, tables)
    if small:
        near = [step(tab, s) for s in (1, 2, 3)]
        ab, state = query_sums(features, state)
        *near, ab = lax.optimization_barrier((*near, ab))
        stats = [tab, pair(tab)]
        for value in near:
            stats += [value, pair(value)]
        dtypes = [jnp.float32, jnp.bfloat16]
    else:
        ab, state = query_sums(features, state)
        peak = lax.pmax(tab[0], RP)
        weight = jnp.exp2(tab[0] - peak)
        total, part = lax.psum(jnp.stack([weight, weight * tab[1]]), RP)
        stats = [jnp.stack([peak + jnp.log2(total), part / total])]
        dtypes = [jnp.float32]
    c, d, *q_terms = query_grads(meta, tables, stats, (q_side, g_side), ab, dtypes)
    if small:
        keep, send = q_terms
        total = keep + pair(send).astype(jnp.float32)
        low = total.astype(jnp.bfloat16)
        got = [step(low[s - 1], s) for s in (1, 2, 3)]
        low, c = lax.optimization_barrier((low, c))
        key_grad, value_grad = row_grads(meta, c, d, (q_side, g_side), state, features)
        query_grad = total[3]
        for value in got:
            query_grad = query_grad + value.astype(jnp.float32)
    else:
        query_grad = lax.psum_scatter(
            q_terms[0].reshape(tables * TEST, features), RP, scatter_dimension=0, tiled=True
        )
        key_grad, value_grad = row_grads(meta, c, d, (q_side, g_side), state, features)
    return query_grad.astype(jnp.bfloat16), key_grad, value_grad


def solution(mesh):
    sizes = mesh.shape
    tables_of_rows = P(("groups", "rows", "pair"), "mp")
    in_specs = (tables_of_rows,) * 4 + (P("groups"),) * 3
    out_specs = (tables_of_rows,) * 3

    def run(query_rows, *rest):
        local_rows = query_rows.shape[0] // (sizes["groups"] * sizes["rows"] * sizes["pair"])
        small = sizes["rows"] == 4 and sizes["pair"] == 2 and local_rows == TEST
        return jax.shard_map(
            lambda *args: local(small, *args),
            mesh=mesh,
            in_specs=in_specs,
            out_specs=out_specs,
            check_vma=False,
        )(query_rows, *rest)

    return run
```

```python
import math

import jax
import jax.numpy as jnp
from jax import lax
from jax.experimental import pallas as pl
from jax.experimental.pallas import tpu as pltpu
from jax.sharding import PartitionSpec as P

HD = 64
TEST = 128
BLK = 512
LANES = 128
WIDE = 2 * TEST
CHUNK = 64

NEG = -1e30
SCORE_SCALE = 1.0 / math.sqrt(HD)
LOG2_SCALE = SCORE_SCALE * math.log2(math.e)
RP = ("rows", "pair")
PAIR = [(0, 1), (1, 0)]


def params(mib):
    return pltpu.CompilerParams(vmem_limit_bytes=mib * 1024 * 1024)


def two_heads(rows):
    feature = lax.broadcasted_iota(jnp.int32, rows.shape, 0)
    zero = jnp.zeros_like(rows)
    return jnp.concatenate(
        [jnp.where(feature < HD, rows, zero), jnp.where(feature < HD, zero, rows)], axis=1
    )


def every_copy(copies):
    for copy in copies:
        copy.start()
    return copies


OWNER, LIVE, TESTN, SLOT_IN, TABLE_OF, SLOT_OUT = range(6)


def vmem_spec():
    return pl.BlockSpec(memory_space=pltpu.VMEM)


def smem_spec():
    return pl.BlockSpec(memory_space=pltpu.SMEM)


def hbm_spec():
    return pl.BlockSpec(memory_space=pltpu.HBM)


def in_hbm(value):
    return pltpu.with_memory_space_constraint(value, pltpu.HBM)


def index_kernel(small, table_hbm, train_hbm, test_hbm, *refs):
    query_hbm, key_hbm, value_hbm, meta, query_ref, state = refs[:6]
    block_table, train_rows, test_rows, count, small_sem, sem = refs[6:]
    blocks = state.shape[0]
    features = key_hbm.shape[1]
    stacked = features // HD * TEST
    entries = every_copy(
        [
            pltpu.make_async_copy(table_hbm, block_table, small_sem.at[0]),
            pltpu.make_async_copy(train_hbm, train_rows, small_sem.at[1]),
            pltpu.make_async_copy(test_hbm, test_rows, small_sem.at[2]),
        ]
    )
    loads = [pltpu.make_async_copy(query_hbm, query_ref, small_sem.at[3])]
    for n, source in enumerate((key_hbm, value_hbm)):
        lanes = pl.ds(2 * stacked + n * features, features)
        for b in range(blocks):
            rows = pl.ds(b * BLK, BLK)
            loads.append(
                pltpu.make_async_copy(source.at[rows], state.at[b, :, lanes], sem.at[n, b])
            )
    every_copy(loads)
    chip = lax.axis_index("rows").astype(jnp.int32)
    core = lax.axis_index("pair").astype(jnp.int32)
    first = lax.axis_index(RP).astype(jnp.int32) * blocks
    for copy in entries:
        copy.wait()
    for t in range(train_rows.shape[0]):
        count[t] = 0
        meta[TESTN, t] = test_rows[t]
        if small:
            away = (t // 2) ^ chip
            not_mine = (t % 2) ^ core
            meta[SLOT_IN, t] = 2 * away + not_mine
            meta[TABLE_OF, t] = 2 * away + not_mine
            meta[SLOT_OUT, t] = 4 * not_mine + ((away + 3) & 3)
        else:
            for row in (SLOT_IN, TABLE_OF, SLOT_OUT):
                meta[row, t] = t

    def earlier(n, carry):
        table = block_table[n]
        count[table] = count[table] + 1
        return carry

    lax.fori_loop(0, first, earlier, 0)
    for b in range(blocks):
        table = block_table[first + b]
        meta[OWNER, b] = table
        meta[LIVE, b] = jnp.minimum(train_rows[table] - count[table] * BLK, BLK)
        count[table] = count[table] + 1
    for copy in loads:
        copy.wait()


def index_table(small, block_table, train_rows, test_rows, query_rows, key_rows, value_rows):
    tables = train_rows.shape[0]
    features = key_rows.shape[1]
    blocks = key_rows.shape[0] // BLK
    stacked = features // HD * TEST
    arrays = (block_table, train_rows, test_rows, query_rows, key_rows, value_rows)
    return pl.pallas_call(
        lambda *refs: index_kernel(small, *refs),
        in_specs=[hbm_spec()] * 6,
        out_specs=[smem_spec(), vmem_spec(), vmem_spec()],
        out_shape=[
            pltpu.SMEM((6, max(blocks, tables)), jnp.int32),
            pltpu.VMEM(query_rows.shape, query_rows.dtype),
            pltpu.VMEM((blocks, BLK, 2 * stacked + 2 * features), jnp.bfloat16),
        ],
        scratch_shapes=[
            pltpu.SMEM(block_table.shape, jnp.int32),
            pltpu.SMEM((tables,), jnp.int32),
            pltpu.SMEM((tables,), jnp.int32),
            pltpu.SMEM((tables,), jnp.int32),
            pltpu.SemaphoreType.DMA((4,)),
            pltpu.SemaphoreType.DMA((2, blocks)),
        ],
        compiler_params=params(4),
        name="index_table",
    )(*map(in_hbm, arrays))


def turn_pieces(pieces, store):
    at_slot = 0
    for piece in pieces:
        for m in range(piece.shape[0] // TEST):
            store(at_slot, piece[m * TEST : (m + 1) * TEST, :].T)
            at_slot += 1


def fold(values, op):
    return op(values.reshape(CHUNK // 8, 8, WIDE), axis=0)


def rows_of(meta, b, p, features):
    at_slot = meta[SLOT_IN, meta[OWNER, b]]
    return pl.ds(pl.multiple_of(at_slot * features + p * LANES, LANES), LANES)


def put_heads(side, first, b, p, features, row):
    at = first + b * features // HD + 2 * p
    side[at : at + 1, :] = row[:, :TEST]
    side[at + 1 : at + 2, :] = row[:, TEST:]


def get_heads(side, row, heads):
    return jnp.concatenate([side[row + h : row + h + 1, :] for h in range(heads)], axis=1)


def units_of(blocks, features):
    return [(b, p) for b in range(blocks) for p in range(features // LANES)]


def weights_kernel(count, features, meta, *refs):
    pieces = refs[:count]
    state, side, state_out, scores_s = refs[count:]
    blocks = state.shape[0]
    stacked = features // HD * TEST
    first_peak = side.shape[0] - blocks * features // HD
    units = units_of(blocks, features)

    def store(at_slot, turned):
        side[at_slot * features : (at_slot + 1) * features, :] = turned.astype(jnp.float32)

    turn_pieces(pieces, store)
    peaks = [None] * len(units)
    for t in range(len(units) + 1):
        if t < len(units):
            b, p = units[t]
            live = meta[LIVE, b]
            queries = two_heads(side[rows_of(meta, b, p, features), :]).astype(jnp.bfloat16)
            peak = jnp.full((8, WIDE), NEG, jnp.float32)
        for r in range(0, BLK, CHUNK):
            rows = slice(r, r + CHUNK)
            if t > 0:
                last_b, last_p = units[t - 1]
                weights = jnp.exp2(scores_s[(t - 1) % 2, rows, :] * LOG2_SCALE - peaks[t - 1])
                state_out[last_b, rows, last_p * WIDE : (last_p + 1) * WIDE] = weights.astype(
                    jnp.bfloat16
                )
            if t < len(units):
                keys = state[b, rows, 2 * stacked + p * LANES : 2 * stacked + (p + 1) * LANES]
                scores = jnp.dot(keys, queries, preferred_element_type=jnp.float32)
                row = lax.broadcasted_iota(jnp.int32, scores.shape, 0)
                scores = jnp.where(row < live - r, scores, NEG)
                scores_s[t % 2, rows, :] = scores
                peak = jnp.maximum(peak, fold(scores, jnp.max))
        if t < len(units):
            peaks[t] = jnp.max(peak, axis=0, keepdims=True) * LOG2_SCALE
    for (b, p), peak in zip(units, peaks):
        put_heads(side, first_peak, b, p, features, peak)


def block_weights(meta, pieces, state, features, tables):
    blocks = state.shape[0]
    count = len(pieces)
    return pl.pallas_call(
        lambda *refs: weights_kernel(count, features, *refs),
        in_specs=[smem_spec()] + [vmem_spec()] * (count + 1),
        out_specs=[vmem_spec()] * 2,
        out_shape=[
            pltpu.VMEM((tables * features + blocks * features // HD, TEST), jnp.float32),
            pltpu.VMEM(state.shape, jnp.bfloat16),
        ],
        input_output_aliases={count + 1: 1},
        scratch_shapes=[pltpu.VMEM((2, BLK, WIDE), jnp.float32)],
        compiler_params=params(10),
        name="block_weights",
    )(meta, *pieces, state)


def moved_kernel(count, features, meta, *refs):
    pieces = refs[:count]
    q_side, state, side, tab_ref, state_out = refs[count : count + 5]
    dprobs_s = refs[count + 5]
    tables = tab_ref.shape[1]
    stacked = features // HD * TEST
    blocks = state.shape[0]
    heads = features // HD
    first = tables * features
    units = units_of(blocks, features)
    query = lax.broadcasted_iota(jnp.int32, (features, TEST), 1)

    def store(at_slot, turned):
        live = query < meta[TESTN, meta[TABLE_OF, at_slot]]
        turned = jnp.where(live, turned, jnp.zeros_like(turned)).astype(jnp.float32)
        side[at_slot * features : (at_slot + 1) * features, :] = turned

    turn_pieces(pieces, store)
    means, masses = [None] * len(units), [None] * len(units)
    zero = jnp.zeros((8, WIDE), jnp.float32)
    for t in range(len(units) + 1):
        if t < len(units):
            b, p = units[t]
            grads = two_heads(side[rows_of(meta, b, p, features), :]).astype(jnp.bfloat16)
            mass = part = zero
        for r in range(0, BLK, CHUNK):
            rows = slice(r, r + CHUNK)
            if t > 0:
                last_b, last_p = units[t - 1]
                weights = state[last_b, rows, last_p * WIDE : (last_p + 1) * WIDE]
                moved = weights.astype(jnp.float32) * (dprobs_s[(t - 1) % 2, rows, :] - means[t - 1])
                lanes = slice(stacked + last_p * WIDE, stacked + (last_p + 1) * WIDE)
                state_out[last_b, rows, lanes] = moved.astype(jnp.bfloat16)
            if t < len(units):
                lane = 2 * stacked + features + p * LANES
                values = state[b, rows, lane : lane + LANES]
                dprobs = jnp.dot(values, grads, preferred_element_type=jnp.float32)
                weights = state[b, rows, p * WIDE : (p + 1) * WIDE].astype(jnp.float32)
                mass = mass + fold(weights, jnp.sum)
                part = part + fold(weights * dprobs, jnp.sum)
                dprobs_s[t % 2, rows, :] = dprobs
        if t < len(units):
            mass = jnp.sum(mass, axis=0, keepdims=True)
            masses[t] = mass
            means[t] = jnp.sum(part, axis=0, keepdims=True) / mass
    for (b, p), mean, mass in zip(units, means, masses):
        put_heads(side, first, b, p, features, mean)
        put_heads(side, first + blocks * heads, b, p, features, mass)
    table = lax.broadcasted_iota(jnp.int32, (tables, stacked), 0)
    peak = jnp.full((tables, stacked), NEG, jnp.float32)
    for b in range(blocks):
        own = table == meta[OWNER, b]
        block_peak = get_heads(q_side, first + b * heads, heads)
        peak = jnp.where(own, jnp.maximum(peak, block_peak), peak)
    total = part = jnp.zeros((tables, stacked), jnp.float32)
    for b in range(blocks):
        own = table == meta[OWNER, b]
        at = b * (features // LANES)
        mass = jnp.concatenate(masses[at : at + features // LANES], axis=1)
        mean = jnp.concatenate(means[at : at + features // LANES], axis=1)
        block_peak = get_heads(q_side, first + b * heads, heads)
        scaled = jnp.where(own, jnp.exp2(block_peak - peak) * mass, 0.0)
        total = total + scaled
        part = part + scaled * mean
    here = total > 0.0
    mass = jnp.where(here, total, 1.0)
    tab_ref[0] = jnp.where(here, peak + jnp.log2(mass), NEG)
    tab_ref[1] = part / mass


def moved_weights(meta, pieces, q_side, state, features, tables):
    blocks = state.shape[0]
    stacked = features // HD * TEST
    count = len(pieces)
    return pl.pallas_call(
        lambda *refs: moved_kernel(count, features, *refs),
        in_specs=[smem_spec()] + [vmem_spec()] * (count + 2),
        out_specs=[vmem_spec()] * 3,
        out_shape=[
            pltpu.VMEM((tables * features + 2 * blocks * features // HD, TEST), jnp.float32),
            jax.ShapeDtypeStruct((2, tables, stacked), jnp.float32),
            pltpu.VMEM(state.shape, jnp.bfloat16),
        ],
        input_output_aliases={count + 2: 2},
        scratch_shapes=[pltpu.VMEM((2, BLK, WIDE), jnp.float32)],
        compiler_params=params(10),
        name="moved_weights",
    )(meta, *pieces, q_side, state)


def query_sums_kernel(state, ab_ref, state_out):
    blocks, _, features, _ = ab_ref.shape
    stacked = features // HD * TEST
    for b in range(blocks):
        for p in range(features // LANES):
            keys = state[b, :, 2 * stacked + p * LANES : 2 * stacked + (p + 1) * LANES]
            for n, first in enumerate((stacked, 0)):
                values = state[b, :, first + p * WIDE : first + (p + 1) * WIDE]
                product = lax.dot_general(
                    keys, values, (((0,), (0,)), ((), ())), preferred_element_type=jnp.float32
                )
                ab_ref[b, n, p * LANES : p * LANES + HD, :] = product[:HD, :TEST]
                ab_ref[b, n, p * LANES + HD : (p + 1) * LANES, :] = product[HD:, TEST:]


def query_sums(features, state):
    blocks = state.shape[0]
    return pl.pallas_call(
        query_sums_kernel,
        in_specs=[vmem_spec()],
        out_specs=[vmem_spec()] * 2,
        out_shape=[
            pltpu.VMEM((blocks, 2, features, TEST), jnp.float32),
            pltpu.VMEM(state.shape, jnp.bfloat16),
        ],
        input_output_aliases={0: 1},
        compiler_params=params(8),
        name="query_sums",
    )(state)


def merged(pieces):
    peak = pieces[0][0]
    for piece in pieces[1:]:
        peak = jnp.maximum(peak, piece[0])
    mass = part = 0.0
    for piece in pieces:
        weight = jnp.exp2(piece[0] - peak)
        mass = mass + weight
        part = part + piece[1] * weight
    return peak, mass, part / mass


def query_grad_kernel(count, meta, *refs):
    pieces = refs[:count]
    q_side, g_side, ab_ref = refs[count : count + 3]
    c_ref, d_ref, *q_refs = refs[count + 3 : -2]
    tab_s, acc_s = refs[-2:]
    blocks = ab_ref.shape[0]
    tables, features, _ = acc_s.shape
    heads = features // HD
    tab_s[0], tab_s[1], tab_s[2] = merged(pieces)
    acc_s[...] = jnp.zeros_like(acc_s)
    for b in range(blocks):
        at = meta[SLOT_OUT, meta[OWNER, b]]
        table = pl.ds(meta[OWNER, b], 1)
        row = tables * features + b * heads
        mass = tab_s[1, table, :]
        c = jnp.exp2(get_heads(q_side, row, heads) - tab_s[0, table, :]) / mass
        d = c * (get_heads(g_side, row, heads) - tab_s[2, table, :])
        c_ref[b : b + 1, :] = c
        d_ref[b : b + 1, :] = d
        for h in range(heads):
            rows = slice(h * HD, (h + 1) * HD)
            lanes = slice(h * TEST, (h + 1) * TEST)
            acc_s[at, rows, :] += c[:, lanes] * ab_ref[b, 0, rows, :] + d[:, lanes] * ab_ref[b, 1, rows, :]
    per = tables // len(q_refs)
    for n in range(tables):
        ref = q_refs[n // per]
        ref[n % per] = (acc_s[n] * SCORE_SCALE).T.astype(ref.dtype)


def query_grads(meta, tables, pieces, sides, ab, q_dtypes):
    blocks, _, features, _ = ab.shape
    stacked = features // HD * TEST
    per = tables // len(q_dtypes)
    return pl.pallas_call(
        lambda *refs: query_grad_kernel(len(pieces), *refs),
        in_specs=[smem_spec()] + [vmem_spec()] * (len(pieces) + 3),
        out_specs=[vmem_spec()] * (2 + len(q_dtypes)),
        out_shape=[
            jax.ShapeDtypeStruct((blocks, stacked), jnp.float32),
            jax.ShapeDtypeStruct((blocks, stacked), jnp.float32),
        ]
        + [jax.ShapeDtypeStruct((per, TEST, features), dtype) for dtype in q_dtypes],
        scratch_shapes=[
            pltpu.VMEM((3, tables, stacked), jnp.float32),
            pltpu.VMEM((tables, features, TEST), jnp.float32),
        ],
        compiler_params=params(10),
        name="query_grads",
    )(meta, *pieces, *sides, ab)


def row_grads_kernel(meta, c_ref, d_ref, q_side, g_side, state, dk_hbm, dv_hbm, dk_s, dv_s, out_sem):
    blocks, _, features = dk_s.shape
    stacked = features // HD * TEST
    turned = (((1,), (1,)), ((), ()))
    stores = []
    for b in range(blocks):
        for p in range(features // LANES):
            at = slice(p * LANES, (p + 1) * LANES)
            wide = slice(p * WIDE, (p + 1) * WIDE)
            c = c_ref[b : b + 1, wide]
            d = d_ref[b : b + 1, wide]
            q_t = two_heads(q_side[rows_of(meta, b, p, features), :])
            g_t = two_heads(g_side[rows_of(meta, b, p, features), :])
            for_u = (q_t * (c * SCORE_SCALE)).astype(jnp.bfloat16)
            for_e = jnp.concatenate([g_t * c, q_t * (d * SCORE_SCALE)], axis=0).astype(jnp.bfloat16)
            from_e = lax.dot_general(
                state[b, :, wide], for_e, turned, preferred_element_type=jnp.float32
            )
            moved = state[b, :, stacked + p * WIDE : stacked + (p + 1) * WIDE]
            from_u = lax.dot_general(moved, for_u, turned, preferred_element_type=jnp.float32)
            dv_s[b, :, at] = from_e[:, :LANES].astype(jnp.bfloat16)
            dk_s[b, :, at] = (from_u + from_e[:, LANES:]).astype(jnp.bfloat16)
        rows = pl.ds(b * BLK, BLK)
        stores += every_copy(
            [
                pltpu.make_async_copy(dk_s.at[b], dk_hbm.at[rows], out_sem.at[0, b]),
                pltpu.make_async_copy(dv_s.at[b], dv_hbm.at[rows], out_sem.at[1, b]),
            ]
        )
    for copy in stores:
        copy.wait()


def row_grads(meta, c, d, sides, state, features):
    blocks = state.shape[0]
    return pl.pallas_call(
        row_grads_kernel,
        in_specs=[smem_spec()] + [vmem_spec()] * 5,
        out_specs=[hbm_spec()] * 2,
        out_shape=[jax.ShapeDtypeStruct((blocks * BLK, features), jnp.bfloat16)] * 2,
        scratch_shapes=[
            pltpu.VMEM((blocks, BLK, features), jnp.bfloat16),
            pltpu.VMEM((blocks, BLK, features), jnp.bfloat16),
            pltpu.SemaphoreType.DMA((2, blocks)),
        ],
        compiler_params=params(10),
        name="row_grads",
    )(meta, c, d, *sides, state)


def local(small, query_rows, key_rows, value_rows, cotangent, train_rows, test_rows, block_table):
    features = query_rows.shape[1]
    blocks = key_rows.shape[0] // BLK
    tables = train_rows.shape[0]
    pair = lambda value: lax.ppermute(value, "pair", PAIR)
    step = lambda value, s: lax.ppermute(value, "rows", [(z, z ^ s) for z in range(4)])
    after = lambda value, other: lax.optimization_barrier((value, other))
    index = lambda entries: index_table(
        small, entries, train_rows, test_rows, query_rows, key_rows, value_rows
    )
    if small:
        near = [step(query_rows, s) for s in (1, 2, 3)]
        near_grads = [step(cotangent, 1), step(cotangent, 2)]
        near_grads.append(step(near_grads[1], 1))
        block_table, near[0] = after(block_table, near[0])
        meta, own, state = index(block_table)
        near[0], meta = after(near[0], meta)
        queries = [own, pair(own)]
        for value in near:
            queries += [value, pair(value)]
        q_side, state = block_weights(meta, queries, state, features, tables)
        *near_grads[1:], q_side = lax.optimization_barrier((*near_grads[1:], q_side))
        grads = [cotangent, pair(cotangent)]
        for value in near_grads:
            grads += [value, pair(value)]
    else:
        meta, _, state = index(block_table)
        queries = [lax.all_gather(query_rows, RP, axis=0, tiled=True)]
        q_side, state = block_weights(meta, queries, state, features, tables)
        grads = [lax.all_gather(cotangent, RP, axis=0, tiled=True)]
    g_side, tab, state = moved_weights(meta, grads, q_side, state, features, tables)
    if small:
        near = [step(tab, s) for s in (1, 2, 3)]
        ab, state = query_sums(features, state)
        *near, ab = lax.optimization_barrier((*near, ab))
        stats = [tab, pair(tab)]
        for value in near:
            stats += [value, pair(value)]
        dtypes = [jnp.float32, jnp.bfloat16]
    else:
        ab, state = query_sums(features, state)
        peak = lax.pmax(tab[0], RP)
        weight = jnp.exp2(tab[0] - peak)
        total, part = lax.psum(jnp.stack([weight, weight * tab[1]]), RP)
        stats = [jnp.stack([peak + jnp.log2(total), part / total])]
        dtypes = [jnp.float32]
    c, d, *q_terms = query_grads(meta, tables, stats, (q_side, g_side), ab, dtypes)
    if small:
        keep, send = q_terms
        total = keep + pair(send).astype(jnp.float32)
        low = total.astype(jnp.bfloat16)
        got = [step(low[s - 1], s) for s in (1, 2, 3)]
        low, c = lax.optimization_barrier((low, c))
        key_grad, value_grad = row_grads(meta, c, d, (q_side, g_side), state, features)
        query_grad = total[3]
        for value in got:
            query_grad = query_grad + value.astype(jnp.float32)
    else:
        query_grad = lax.psum_scatter(
            q_terms[0].reshape(tables * TEST, features), RP, scatter_dimension=0, tiled=True
        )
        key_grad, value_grad = row_grads(meta, c, d, (q_side, g_side), state, features)
    return query_grad.astype(jnp.bfloat16), key_grad, value_grad


def solution(mesh):
    sizes = mesh.shape
    tables_of_rows = P(("groups", "rows", "pair"), "mp")
    in_specs = (tables_of_rows,) * 4 + (P("groups"),) * 3
    out_specs = (tables_of_rows,) * 3

    def run(query_rows, *rest):
        local_rows = query_rows.shape[0] // (sizes["groups"] * sizes["rows"] * sizes["pair"])
        small = sizes["rows"] == 4 and sizes["pair"] == 2 and local_rows == TEST
        return jax.shard_map(
            lambda *args: local(small, *args),
            mesh=mesh,
            in_specs=in_specs,
            out_specs=out_specs,
            check_vma=False,
        )(query_rows, *rest)

    return run
```

```python
import math

import jax
import jax.numpy as jnp
from jax import lax
from jax.experimental import pallas as pl
from jax.experimental.pallas import tpu as pltpu
from jax.sharding import PartitionSpec as P

HD = 64
TEST = 128
BLK = 512
LANES = 128
WIDE = 2 * TEST
CHUNK = 64

NEG = -1e30
SCORE_SCALE = 1.0 / math.sqrt(HD)
LOG2_SCALE = SCORE_SCALE * math.log2(math.e)
RP = ("rows", "pair")
PAIR = [(0, 1), (1, 0)]


def params(mib):
    return pltpu.CompilerParams(vmem_limit_bytes=mib * 1024 * 1024)


def two_heads(rows):
    feature = lax.broadcasted_iota(jnp.int32, rows.shape, 0)
    zero = jnp.zeros_like(rows)
    return jnp.concatenate(
        [jnp.where(feature < HD, rows, zero), jnp.where(feature < HD, zero, rows)], axis=1
    )


def every_copy(copies):
    for copy in copies:
        copy.start()
    return copies


OWNER, LIVE, TESTN, SLOT_IN, TABLE_OF, SLOT_OUT = range(6)


def vmem_spec():
    return pl.BlockSpec(memory_space=pltpu.VMEM)


def smem_spec():
    return pl.BlockSpec(memory_space=pltpu.SMEM)


def hbm_spec():
    return pl.BlockSpec(memory_space=pltpu.HBM)


def in_hbm(value):
    return pltpu.with_memory_space_constraint(value, pltpu.HBM)


def index_kernel(small, table_hbm, train_hbm, test_hbm, *refs):
    query_hbm, key_hbm, value_hbm, meta, query_ref, state = refs[:6]
    block_table, train_rows, test_rows, count, small_sem, sem = refs[6:]
    blocks = state.shape[0]
    features = key_hbm.shape[1]
    stacked = features // HD * TEST
    entries = every_copy(
        [
            pltpu.make_async_copy(table_hbm, block_table, small_sem.at[0]),
            pltpu.make_async_copy(train_hbm, train_rows, small_sem.at[1]),
            pltpu.make_async_copy(test_hbm, test_rows, small_sem.at[2]),
        ]
    )
    loads = [pltpu.make_async_copy(query_hbm, query_ref, small_sem.at[3])]
    for n, source in enumerate((key_hbm, value_hbm)):
        lanes = pl.ds(2 * stacked + n * features, features)
        for b in range(blocks):
            rows = pl.ds(b * BLK, BLK)
            loads.append(
                pltpu.make_async_copy(source.at[rows], state.at[b, :, lanes], sem.at[n, b])
            )
    every_copy(loads)
    chip = lax.axis_index("rows").astype(jnp.int32)
    core = lax.axis_index("pair").astype(jnp.int32)
    first = lax.axis_index(RP).astype(jnp.int32) * blocks
    for copy in entries:
        copy.wait()
    for t in range(train_rows.shape[0]):
        count[t] = 0
        meta[TESTN, t] = test_rows[t]
        if small:
            away = (t // 2) ^ chip
            not_mine = (t % 2) ^ core
            meta[SLOT_IN, t] = 2 * away + not_mine
            meta[TABLE_OF, t] = 2 * away + not_mine
            meta[SLOT_OUT, t] = 4 * not_mine + ((away + 3) & 3)
        else:
            for row in (SLOT_IN, TABLE_OF, SLOT_OUT):
                meta[row, t] = t

    def earlier(n, carry):
        table = block_table[n]
        count[table] = count[table] + 1
        return carry

    lax.fori_loop(0, first, earlier, 0)
    for b in range(blocks):
        table = block_table[first + b]
        meta[OWNER, b] = table
        meta[LIVE, b] = jnp.minimum(train_rows[table] - count[table] * BLK, BLK)
        count[table] = count[table] + 1
    for copy in loads:
        copy.wait()


def index_table(small, block_table, train_rows, test_rows, query_rows, key_rows, value_rows):
    tables = train_rows.shape[0]
    features = key_rows.shape[1]
    blocks = key_rows.shape[0] // BLK
    stacked = features // HD * TEST
    arrays = (block_table, train_rows, test_rows, query_rows, key_rows, value_rows)
    return pl.pallas_call(
        lambda *refs: index_kernel(small, *refs),
        in_specs=[hbm_spec()] * 6,
        out_specs=[smem_spec(), vmem_spec(), vmem_spec()],
        out_shape=[
            pltpu.SMEM((6, max(blocks, tables)), jnp.int32),
            pltpu.VMEM(query_rows.shape, query_rows.dtype),
            pltpu.VMEM((blocks, BLK, 2 * stacked + 2 * features), jnp.bfloat16),
        ],
        scratch_shapes=[
            pltpu.SMEM(block_table.shape, jnp.int32),
            pltpu.SMEM((tables,), jnp.int32),
            pltpu.SMEM((tables,), jnp.int32),
            pltpu.SMEM((tables,), jnp.int32),
            pltpu.SemaphoreType.DMA((4,)),
            pltpu.SemaphoreType.DMA((2, blocks)),
        ],
        compiler_params=params(4),
        name="index_table",
    )(*map(in_hbm, arrays))


def turn_pieces(pieces, store):
    at_slot = 0
    for piece in pieces:
        for m in range(piece.shape[0] // TEST):
            store(at_slot, piece[m * TEST : (m + 1) * TEST, :].T)
            at_slot += 1


def fold(values, op):
    return op(values.reshape(CHUNK // 8, 8, WIDE), axis=0)


def rows_of(meta, b, p, features):
    at_slot = meta[SLOT_IN, meta[OWNER, b]]
    return pl.ds(pl.multiple_of(at_slot * features + p * LANES, LANES), LANES)


def put_heads(side, first, b, p, features, row):
    at = first + b * features // HD + 2 * p
    side[at : at + 1, :] = row[:, :TEST]
    side[at + 1 : at + 2, :] = row[:, TEST:]


def get_heads(side, row, heads):
    return jnp.concatenate([side[row + h : row + h + 1, :] for h in range(heads)], axis=1)


def units_of(blocks, features):
    return [(b, p) for b in range(blocks) for p in range(features // LANES)]


def weights_kernel(count, features, meta, *refs):
    pieces = refs[:count]
    state, side, state_out, scores_s = refs[count:]
    blocks = state.shape[0]
    stacked = features // HD * TEST
    first_peak = side.shape[0] - blocks * features // HD
    units = units_of(blocks, features)

    def store(at_slot, turned):
        side[at_slot * features : (at_slot + 1) * features, :] = turned.astype(jnp.float32)

    turn_pieces(pieces, store)
    peaks = [None] * len(units)
    for t in range(len(units) + 1):
        if t < len(units):
            b, p = units[t]
            live = meta[LIVE, b]
            queries = two_heads(side[rows_of(meta, b, p, features), :]).astype(jnp.bfloat16)
            peak = jnp.full((8, WIDE), NEG, jnp.float32)
        for r in range(0, BLK, CHUNK):
            rows = slice(r, r + CHUNK)
            if t > 0:
                last_b, last_p = units[t - 1]
                weights = jnp.exp2(scores_s[(t - 1) % 2, rows, :] * LOG2_SCALE - peaks[t - 1])
                state_out[last_b, rows, last_p * WIDE : (last_p + 1) * WIDE] = weights.astype(
                    jnp.bfloat16
                )
            if t < len(units):
                keys = state[b, rows, 2 * stacked + p * LANES : 2 * stacked + (p + 1) * LANES]
                scores = jnp.dot(keys, queries, preferred_element_type=jnp.float32)
                row = lax.broadcasted_iota(jnp.int32, scores.shape, 0)
                scores = jnp.where(row < live - r, scores, NEG)
                scores_s[t % 2, rows, :] = scores
                peak = jnp.maximum(peak, fold(scores, jnp.max))
        if t < len(units):
            peaks[t] = jnp.max(peak, axis=0, keepdims=True) * LOG2_SCALE
    for (b, p), peak in zip(units, peaks):
        put_heads(side, first_peak, b, p, features, peak)


def block_weights(meta, pieces, state, features, tables):
    blocks = state.shape[0]
    count = len(pieces)
    return pl.pallas_call(
        lambda *refs: weights_kernel(count, features, *refs),
        in_specs=[smem_spec()] + [vmem_spec()] * (count + 1),
        out_specs=[vmem_spec()] * 2,
        out_shape=[
            pltpu.VMEM((tables * features + blocks * features // HD, TEST), jnp.float32),
            pltpu.VMEM(state.shape, jnp.bfloat16),
        ],
        input_output_aliases={count + 1: 1},
        scratch_shapes=[pltpu.VMEM((2, BLK, WIDE), jnp.float32)],
        compiler_params=params(10),
        name="block_weights",
    )(meta, *pieces, state)


def moved_kernel(count, features, meta, *refs):
    pieces = refs[:count]
    q_side, state, side, tab_ref, state_out = refs[count : count + 5]
    dprobs_s = refs[count + 5]
    tables = tab_ref.shape[1]
    stacked = features // HD * TEST
    blocks = state.shape[0]
    heads = features // HD
    first = tables * features
    units = units_of(blocks, features)
    query = lax.broadcasted_iota(jnp.int32, (features, TEST), 1)

    def store(at_slot, turned):
        live = query < meta[TESTN, meta[TABLE_OF, at_slot]]
        turned = jnp.where(live, turned, jnp.zeros_like(turned)).astype(jnp.float32)
        side[at_slot * features : (at_slot + 1) * features, :] = turned

    turn_pieces(pieces, store)
    means, masses = [None] * len(units), [None] * len(units)
    zero = jnp.zeros((8, WIDE), jnp.float32)
    for t in range(len(units) + 1):
        if t < len(units):
            b, p = units[t]
            grads = two_heads(side[rows_of(meta, b, p, features), :]).astype(jnp.bfloat16)
            mass = part = zero
        for r in range(0, BLK, CHUNK):
            rows = slice(r, r + CHUNK)
            if t > 0:
                last_b, last_p = units[t - 1]
                weights = state[last_b, rows, last_p * WIDE : (last_p + 1) * WIDE]
                moved = weights.astype(jnp.float32) * (dprobs_s[(t - 1) % 2, rows, :] - means[t - 1])
                lanes = slice(stacked + last_p * WIDE, stacked + (last_p + 1) * WIDE)
                state_out[last_b, rows, lanes] = moved.astype(jnp.bfloat16)
            if t < len(units):
                lane = 2 * stacked + features + p * LANES
                values = state[b, rows, lane : lane + LANES]
                dprobs = jnp.dot(values, grads, preferred_element_type=jnp.float32)
                weights = state[b, rows, p * WIDE : (p + 1) * WIDE].astype(jnp.float32)
                mass = mass + fold(weights, jnp.sum)
                part = part + fold(weights * dprobs, jnp.sum)
                dprobs_s[t % 2, rows, :] = dprobs
        if t < len(units):
            mass = jnp.sum(mass, axis=0, keepdims=True)
            masses[t] = mass
            means[t] = jnp.sum(part, axis=0, keepdims=True) / mass
    for (b, p), mean, mass in zip(units, means, masses):
        put_heads(side, first, b, p, features, mean)
        put_heads(side, first + blocks * heads, b, p, features, mass)
    table = lax.broadcasted_iota(jnp.int32, (tables, stacked), 0)
    peak = jnp.full((tables, stacked), NEG, jnp.float32)
    for b in range(blocks):
        own = table == meta[OWNER, b]
        block_peak = get_heads(q_side, first + b * heads, heads)
        peak = jnp.where(own, jnp.maximum(peak, block_peak), peak)
    total = part = jnp.zeros((tables, stacked), jnp.float32)
    for b in range(blocks):
        own = table == meta[OWNER, b]
        at = b * (features // LANES)
        mass = jnp.concatenate(masses[at : at + features // LANES], axis=1)
        mean = jnp.concatenate(means[at : at + features // LANES], axis=1)
        block_peak = get_heads(q_side, first + b * heads, heads)
        scaled = jnp.where(own, jnp.exp2(block_peak - peak) * mass, 0.0)
        total = total + scaled
        part = part + scaled * mean
    here = total > 0.0
    mass = jnp.where(here, total, 1.0)
    tab_ref[0] = jnp.where(here, peak + jnp.log2(mass), NEG)
    tab_ref[1] = part / mass


def moved_weights(meta, pieces, q_side, state, features, tables):
    blocks = state.shape[0]
    stacked = features // HD * TEST
    count = len(pieces)
    return pl.pallas_call(
        lambda *refs: moved_kernel(count, features, *refs),
        in_specs=[smem_spec()] + [vmem_spec()] * (count + 2),
        out_specs=[vmem_spec()] * 3,
        out_shape=[
            pltpu.VMEM((tables * features + 2 * blocks * features // HD, TEST), jnp.float32),
            jax.ShapeDtypeStruct((2, tables, stacked), jnp.float32),
            pltpu.VMEM(state.shape, jnp.bfloat16),
        ],
        input_output_aliases={count + 2: 2},
        scratch_shapes=[pltpu.VMEM((2, BLK, WIDE), jnp.float32)],
        compiler_params=params(10),
        name="moved_weights",
    )(meta, *pieces, q_side, state)


def query_sums_kernel(state, ab_ref, state_out):
    blocks, _, features, _ = ab_ref.shape
    stacked = features // HD * TEST
    for b in range(blocks):
        for p in range(features // LANES):
            keys = state[b, :, 2 * stacked + p * LANES : 2 * stacked + (p + 1) * LANES]
            for n, first in enumerate((stacked, 0)):
                values = state[b, :, first + p * WIDE : first + (p + 1) * WIDE]
                product = lax.dot_general(
                    keys, values, (((0,), (0,)), ((), ())), preferred_element_type=jnp.float32
                )
                ab_ref[b, n, p * LANES : p * LANES + HD, :] = product[:HD, :TEST]
                ab_ref[b, n, p * LANES + HD : (p + 1) * LANES, :] = product[HD:, TEST:]


def query_sums(features, state):
    blocks = state.shape[0]
    return pl.pallas_call(
        query_sums_kernel,
        in_specs=[vmem_spec()],
        out_specs=[vmem_spec()] * 2,
        out_shape=[
            pltpu.VMEM((blocks, 2, features, TEST), jnp.float32),
            pltpu.VMEM(state.shape, jnp.bfloat16),
        ],
        input_output_aliases={0: 1},
        compiler_params=params(8),
        name="query_sums",
    )(state)


def merged(pieces):
    peak = pieces[0][0]
    for piece in pieces[1:]:
        peak = jnp.maximum(peak, piece[0])
    mass = part = 0.0
    for piece in pieces:
        weight = jnp.exp2(piece[0] - peak)
        mass = mass + weight
        part = part + piece[1] * weight
    return peak, mass, part / mass


def query_grad_kernel(count, meta, *refs):
    pieces = refs[:count]
    q_side, g_side, ab_ref = refs[count : count + 3]
    c_ref, d_ref, *q_refs = refs[count + 3 : -2]
    tab_s, acc_s = refs[-2:]
    blocks = ab_ref.shape[0]
    tables, features, _ = acc_s.shape
    heads = features // HD
    tab_s[0], tab_s[1], tab_s[2] = merged(pieces)
    acc_s[...] = jnp.zeros_like(acc_s)
    for b in range(blocks):
        at = meta[SLOT_OUT, meta[OWNER, b]]
        table = pl.ds(meta[OWNER, b], 1)
        row = tables * features + b * heads
        mass = tab_s[1, table, :]
        c = jnp.exp2(get_heads(q_side, row, heads) - tab_s[0, table, :]) / mass
        d = c * (get_heads(g_side, row, heads) - tab_s[2, table, :])
        c_ref[b : b + 1, :] = c
        d_ref[b : b + 1, :] = d
        for h in range(heads):
            rows = slice(h * HD, (h + 1) * HD)
            lanes = slice(h * TEST, (h + 1) * TEST)
            acc_s[at, rows, :] += c[:, lanes] * ab_ref[b, 0, rows, :] + d[:, lanes] * ab_ref[b, 1, rows, :]
    per = tables // len(q_refs)
    for n in range(tables):
        ref = q_refs[n // per]
        ref[n % per] = (acc_s[n] * SCORE_SCALE).T.astype(ref.dtype)


def query_grads(meta, tables, pieces, sides, ab, q_dtypes):
    blocks, _, features, _ = ab.shape
    stacked = features // HD * TEST
    per = tables // len(q_dtypes)
    return pl.pallas_call(
        lambda *refs: query_grad_kernel(len(pieces), *refs),
        in_specs=[smem_spec()] + [vmem_spec()] * (len(pieces) + 3),
        out_specs=[vmem_spec()] * (2 + len(q_dtypes)),
        out_shape=[
            jax.ShapeDtypeStruct((blocks, stacked), jnp.float32),
            jax.ShapeDtypeStruct((blocks, stacked), jnp.float32),
        ]
        + [jax.ShapeDtypeStruct((per, TEST, features), dtype) for dtype in q_dtypes],
        scratch_shapes=[
            pltpu.VMEM((3, tables, stacked), jnp.float32),
            pltpu.VMEM((tables, features, TEST), jnp.float32),
        ],
        compiler_params=params(10),
        name="query_grads",
    )(meta, *pieces, *sides, ab)


def row_grads_kernel(meta, c_ref, d_ref, q_side, g_side, state, dk_hbm, dv_hbm, dk_s, dv_s, out_sem):
    blocks, _, features = dk_s.shape
    stacked = features // HD * TEST
    turned = (((1,), (1,)), ((), ()))
    stores = []
    for b in range(blocks):
        for p in range(features // LANES):
            at = slice(p * LANES, (p + 1) * LANES)
            wide = slice(p * WIDE, (p + 1) * WIDE)
            c = c_ref[b : b + 1, wide]
            d = d_ref[b : b + 1, wide]
            q_t = two_heads(q_side[rows_of(meta, b, p, features), :])
            g_t = two_heads(g_side[rows_of(meta, b, p, features), :])
            for_u = (q_t * (c * SCORE_SCALE)).astype(jnp.bfloat16)
            for_e = jnp.concatenate([g_t * c, q_t * (d * SCORE_SCALE)], axis=0).astype(jnp.bfloat16)
            from_e = lax.dot_general(
                state[b, :, wide], for_e, turned, preferred_element_type=jnp.float32
            )
            moved = state[b, :, stacked + p * WIDE : stacked + (p + 1) * WIDE]
            from_u = lax.dot_general(moved, for_u, turned, preferred_element_type=jnp.float32)
            dv_s[b, :, at] = from_e[:, :LANES].astype(jnp.bfloat16)
            dk_s[b, :, at] = (from_u + from_e[:, LANES:]).astype(jnp.bfloat16)
        rows = pl.ds(b * BLK, BLK)
        stores += every_copy(
            [
                pltpu.make_async_copy(dk_s.at[b], dk_hbm.at[rows], out_sem.at[0, b]),
                pltpu.make_async_copy(dv_s.at[b], dv_hbm.at[rows], out_sem.at[1, b]),
            ]
        )
    for copy in stores:
        copy.wait()


def row_grads(meta, c, d, sides, state, features):
    blocks = state.shape[0]
    return pl.pallas_call(
        row_grads_kernel,
        in_specs=[smem_spec()] + [vmem_spec()] * 5,
        out_specs=[hbm_spec()] * 2,
        out_shape=[jax.ShapeDtypeStruct((blocks * BLK, features), jnp.bfloat16)] * 2,
        scratch_shapes=[
            pltpu.VMEM((blocks, BLK, features), jnp.bfloat16),
            pltpu.VMEM((blocks, BLK, features), jnp.bfloat16),
            pltpu.SemaphoreType.DMA((2, blocks)),
        ],
        compiler_params=params(10),
        name="row_grads",
    )(meta, c, d, *sides, state)


def local(small, query_rows, key_rows, value_rows, cotangent, train_rows, test_rows, block_table):
    features = query_rows.shape[1]
    blocks = key_rows.shape[0] // BLK
    tables = train_rows.shape[0]
    pair = lambda value: lax.ppermute(value, "pair", PAIR)
    step = lambda value, s: lax.ppermute(value, "rows", [(z, z ^ s) for z in range(4)])
    after = lambda value, other: lax.optimization_barrier((value, other))
    index = lambda entries: index_table(
        small, entries, train_rows, test_rows, query_rows, key_rows, value_rows
    )
    if small:
        near = [step(query_rows, 1), step(query_rows, 2)]
        near.append(step(near[1], 1))
        near_grads = [step(cotangent, 1), step(cotangent, 2)]
        near_grads.append(step(near_grads[1], 1))
        block_table, _ = after(block_table, near[1])
        meta, own, state = index(block_table)
        near[0], meta = after(near[0], meta)
        queries = [own, pair(own)]
        for value in near:
            queries += [value, pair(value)]
        q_side, state = block_weights(meta, queries, state, features, tables)
        *near_grads[1:], q_side = lax.optimization_barrier((*near_grads[1:], q_side))
        grads = [cotangent, pair(cotangent)]
        for value in near_grads:
            grads += [value, pair(value)]
    else:
        meta, _, state = index(block_table)
        queries = [lax.all_gather(query_rows, RP, axis=0, tiled=True)]
        q_side, state = block_weights(meta, queries, state, features, tables)
        grads = [lax.all_gather(cotangent, RP, axis=0, tiled=True)]
    g_side, tab, state = moved_weights(meta, grads, q_side, state, features, tables)
    if small:
        near = [step(tab, s) for s in (1, 2, 3)]
        ab, state = query_sums(features, state)
        *near, ab = lax.optimization_barrier((*near, ab))
        stats = [tab, pair(tab)]
        for value in near:
            stats += [value, pair(value)]
        dtypes = [jnp.float32, jnp.bfloat16]
    else:
        ab, state = query_sums(features, state)
        peak = lax.pmax(tab[0], RP)
        weight = jnp.exp2(tab[0] - peak)
        total, part = lax.psum(jnp.stack([weight, weight * tab[1]]), RP)
        stats = [jnp.stack([peak + jnp.log2(total), part / total])]
        dtypes = [jnp.float32]
    c, d, *q_terms = query_grads(meta, tables, stats, (q_side, g_side), ab, dtypes)
    if small:
        keep, send = q_terms
        total = keep + pair(send).astype(jnp.float32)
        low = total.astype(jnp.bfloat16)
        got = [step(low[s - 1], s) for s in (1, 2, 3)]
        low, c = lax.optimization_barrier((low, c))
        key_grad, value_grad = row_grads(meta, c, d, (q_side, g_side), state, features)
        query_grad = total[3]
        for value in got:
            query_grad = query_grad + value.astype(jnp.float32)
    else:
        query_grad = lax.psum_scatter(
            q_terms[0].reshape(tables * TEST, features), RP, scatter_dimension=0, tiled=True
        )
        key_grad, value_grad = row_grads(meta, c, d, (q_side, g_side), state, features)
    return query_grad.astype(jnp.bfloat16), key_grad, value_grad


def solution(mesh):
    sizes = mesh.shape
    tables_of_rows = P(("groups", "rows", "pair"), "mp")
    in_specs = (tables_of_rows,) * 4 + (P("groups"),) * 3
    out_specs = (tables_of_rows,) * 3

    def run(query_rows, *rest):
        local_rows = query_rows.shape[0] // (sizes["groups"] * sizes["rows"] * sizes["pair"])
        small = sizes["rows"] == 4 and sizes["pair"] == 2 and local_rows == TEST
        return jax.shard_map(
            lambda *args: local(small, *args),
            mesh=mesh,
            in_specs=in_specs,
            out_specs=out_specs,
            check_vma=False,
        )(query_rows, *rest)

    return run
```

```python
import math

import jax
import jax.numpy as jnp
from jax import lax
from jax.experimental import pallas as pl
from jax.experimental.pallas import tpu as pltpu
from jax.sharding import PartitionSpec as P

HD = 64
TEST = 128
BLK = 512
LANES = 128
WIDE = 2 * TEST
CHUNK = 64

NEG = -1e30
SCORE_SCALE = 1.0 / math.sqrt(HD)
LOG2_SCALE = SCORE_SCALE * math.log2(math.e)
RP = ("rows", "pair")
PAIR = [(0, 1), (1, 0)]


def params(mib):
    return pltpu.CompilerParams(vmem_limit_bytes=mib * 1024 * 1024)


def two_heads(rows):
    feature = lax.broadcasted_iota(jnp.int32, rows.shape, 0)
    zero = jnp.zeros_like(rows)
    return jnp.concatenate(
        [jnp.where(feature < HD, rows, zero), jnp.where(feature < HD, zero, rows)], axis=1
    )


def every_copy(copies):
    for copy in copies:
        copy.start()
    return copies


OWNER, LIVE, TESTN, SLOT_IN, TABLE_OF, SLOT_OUT = range(6)


def vmem_spec():
    return pl.BlockSpec(memory_space=pltpu.VMEM)


def smem_spec():
    return pl.BlockSpec(memory_space=pltpu.SMEM)


def hbm_spec():
    return pl.BlockSpec(memory_space=pltpu.HBM)


def in_hbm(value):
    return pltpu.with_memory_space_constraint(value, pltpu.HBM)


def index_kernel(small, table_hbm, train_hbm, test_hbm, *refs):
    query_hbm, key_hbm, value_hbm, meta, query_ref, state = refs[:6]
    block_table, train_rows, test_rows, count, small_sem, sem = refs[6:]
    blocks = state.shape[0]
    features = key_hbm.shape[1]
    stacked = features // HD * TEST
    entries = every_copy(
        [
            pltpu.make_async_copy(table_hbm, block_table, small_sem.at[0]),
            pltpu.make_async_copy(train_hbm, train_rows, small_sem.at[1]),
            pltpu.make_async_copy(test_hbm, test_rows, small_sem.at[2]),
        ]
    )
    loads = [pltpu.make_async_copy(query_hbm, query_ref, small_sem.at[3])]
    for n, source in enumerate((key_hbm, value_hbm)):
        lanes = pl.ds(2 * stacked + n * features, features)
        for b in range(blocks):
            rows = pl.ds(b * BLK, BLK)
            loads.append(
                pltpu.make_async_copy(source.at[rows], state.at[b, :, lanes], sem.at[n, b])
            )
    every_copy(loads)
    chip = lax.axis_index("rows").astype(jnp.int32)
    core = lax.axis_index("pair").astype(jnp.int32)
    first = lax.axis_index(RP).astype(jnp.int32) * blocks
    for copy in entries:
        copy.wait()
    for t in range(train_rows.shape[0]):
        count[t] = 0
        meta[TESTN, t] = test_rows[t]
        if small:
            away = (t // 2) ^ chip
            not_mine = (t % 2) ^ core
            meta[SLOT_IN, t] = 2 * away + not_mine
            meta[TABLE_OF, t] = 2 * away + not_mine
            meta[SLOT_OUT, t] = 4 * not_mine + ((away + 3) & 3)
        else:
            for row in (SLOT_IN, TABLE_OF, SLOT_OUT):
                meta[row, t] = t

    def earlier(n, carry):
        table = block_table[n]
        count[table] = count[table] + 1
        return carry

    lax.fori_loop(0, first, earlier, 0)
    for b in range(blocks):
        table = block_table[first + b]
        meta[OWNER, b] = table
        meta[LIVE, b] = jnp.minimum(train_rows[table] - count[table] * BLK, BLK)
        count[table] = count[table] + 1
    for copy in loads:
        copy.wait()


def index_table(small, block_table, train_rows, test_rows, query_rows, key_rows, value_rows):
    tables = train_rows.shape[0]
    features = key_rows.shape[1]
    blocks = key_rows.shape[0] // BLK
    stacked = features // HD * TEST
    arrays = (block_table, train_rows, test_rows, query_rows, key_rows, value_rows)
    return pl.pallas_call(
        lambda *refs: index_kernel(small, *refs),
        in_specs=[hbm_spec()] * 6,
        out_specs=[smem_spec(), vmem_spec(), vmem_spec()],
        out_shape=[
            pltpu.SMEM((6, max(blocks, tables)), jnp.int32),
            pltpu.VMEM(query_rows.shape, query_rows.dtype),
            pltpu.VMEM((blocks, BLK, 2 * stacked + 2 * features), jnp.bfloat16),
        ],
        scratch_shapes=[
            pltpu.SMEM(block_table.shape, jnp.int32),
            pltpu.SMEM((tables,), jnp.int32),
            pltpu.SMEM((tables,), jnp.int32),
            pltpu.SMEM((tables,), jnp.int32),
            pltpu.SemaphoreType.DMA((4,)),
            pltpu.SemaphoreType.DMA((2, blocks)),
        ],
        compiler_params=params(4),
        name="index_table",
    )(*map(in_hbm, arrays))


def turn_pieces(pieces, store):
    at_slot = 0
    for piece in pieces:
        for m in range(piece.shape[0] // TEST):
            store(at_slot, piece[m * TEST : (m + 1) * TEST, :].T)
            at_slot += 1


def fold(values, op):
    return op(values.reshape(CHUNK // 8, 8, WIDE), axis=0)


def rows_of(meta, b, p, features):
    at_slot = meta[SLOT_IN, meta[OWNER, b]]
    return pl.ds(pl.multiple_of(at_slot * features + p * LANES, LANES), LANES)


def put_heads(side, first, b, p, features, row):
    at = first + b * features // HD + 2 * p
    side[at : at + 1, :] = row[:, :TEST]
    side[at + 1 : at + 2, :] = row[:, TEST:]


def get_heads(side, row, heads):
    return jnp.concatenate([side[row + h : row + h + 1, :] for h in range(heads)], axis=1)


def units_of(blocks, features):
    return [(b, p) for b in range(blocks) for p in range(features // LANES)]


def weights_kernel(count, features, meta, *refs):
    pieces = refs[:count]
    state, side, state_out, scores_s = refs[count:]
    blocks = state.shape[0]
    stacked = features // HD * TEST
    first_peak = side.shape[0] - blocks * features // HD
    units = units_of(blocks, features)

    def store(at_slot, turned):
        side[at_slot * features : (at_slot + 1) * features, :] = turned.astype(jnp.float32)

    turn_pieces(pieces, store)
    peaks = [None] * len(units)
    for t in range(len(units) + 1):
        if t < len(units):
            b, p = units[t]
            live = meta[LIVE, b]
            queries = two_heads(side[rows_of(meta, b, p, features), :]).astype(jnp.bfloat16)
            peak = jnp.full((8, WIDE), NEG, jnp.float32)
        for r in range(0, BLK, CHUNK):
            rows = slice(r, r + CHUNK)
            if t > 0:
                last_b, last_p = units[t - 1]
                weights = jnp.exp2(scores_s[(t - 1) % 2, rows, :] * LOG2_SCALE - peaks[t - 1])
                state_out[last_b, rows, last_p * WIDE : (last_p + 1) * WIDE] = weights.astype(
                    jnp.bfloat16
                )
            if t < len(units):
                keys = state[b, rows, 2 * stacked + p * LANES : 2 * stacked + (p + 1) * LANES]
                scores = jnp.dot(keys, queries, preferred_element_type=jnp.float32)
                row = lax.broadcasted_iota(jnp.int32, scores.shape, 0)
                scores = jnp.where(row < live - r, scores, NEG)
                scores_s[t % 2, rows, :] = scores
                peak = jnp.maximum(peak, fold(scores, jnp.max))
        if t < len(units):
            peaks[t] = jnp.max(peak, axis=0, keepdims=True) * LOG2_SCALE
    for (b, p), peak in zip(units, peaks):
        put_heads(side, first_peak, b, p, features, peak)


def block_weights(meta, pieces, state, features, tables):
    blocks = state.shape[0]
    count = len(pieces)
    return pl.pallas_call(
        lambda *refs: weights_kernel(count, features, *refs),
        in_specs=[smem_spec()] + [vmem_spec()] * (count + 1),
        out_specs=[vmem_spec()] * 2,
        out_shape=[
            pltpu.VMEM((tables * features + blocks * features // HD, TEST), jnp.float32),
            pltpu.VMEM(state.shape, jnp.bfloat16),
        ],
        input_output_aliases={count + 1: 1},
        scratch_shapes=[pltpu.VMEM((2, BLK, WIDE), jnp.float32)],
        compiler_params=params(10),
        name="block_weights",
    )(meta, *pieces, state)


def moved_kernel(count, features, meta, *refs):
    pieces = refs[:count]
    q_side, state, side, tab_ref, state_out = refs[count : count + 5]
    dprobs_s = refs[count + 5]
    tables = tab_ref.shape[1]
    stacked = features // HD * TEST
    blocks = state.shape[0]
    heads = features // HD
    first = tables * features
    units = units_of(blocks, features)
    query = lax.broadcasted_iota(jnp.int32, (features, TEST), 1)

    def store(at_slot, turned):
        live = query < meta[TESTN, meta[TABLE_OF, at_slot]]
        turned = jnp.where(live, turned, jnp.zeros_like(turned)).astype(jnp.float32)
        side[at_slot * features : (at_slot + 1) * features, :] = turned

    turn_pieces(pieces, store)
    means, masses = [None] * len(units), [None] * len(units)
    zero = jnp.zeros((8, WIDE), jnp.float32)
    for t in range(len(units) + 1):
        if t < len(units):
            b, p = units[t]
            grads = two_heads(side[rows_of(meta, b, p, features), :]).astype(jnp.bfloat16)
            mass = part = zero
        for r in range(0, BLK, CHUNK):
            rows = slice(r, r + CHUNK)
            if t > 0:
                last_b, last_p = units[t - 1]
                weights = state[last_b, rows, last_p * WIDE : (last_p + 1) * WIDE]
                moved = weights.astype(jnp.float32) * (dprobs_s[(t - 1) % 2, rows, :] - means[t - 1])
                lanes = slice(stacked + last_p * WIDE, stacked + (last_p + 1) * WIDE)
                state_out[last_b, rows, lanes] = moved.astype(jnp.bfloat16)
            if t < len(units):
                lane = 2 * stacked + features + p * LANES
                values = state[b, rows, lane : lane + LANES]
                dprobs = jnp.dot(values, grads, preferred_element_type=jnp.float32)
                weights = state[b, rows, p * WIDE : (p + 1) * WIDE].astype(jnp.float32)
                mass = mass + fold(weights, jnp.sum)
                part = part + fold(weights * dprobs, jnp.sum)
                dprobs_s[t % 2, rows, :] = dprobs
        if t < len(units):
            mass = jnp.sum(mass, axis=0, keepdims=True)
            masses[t] = mass
            means[t] = jnp.sum(part, axis=0, keepdims=True) / mass
    for (b, p), mean, mass in zip(units, means, masses):
        put_heads(side, first, b, p, features, mean)
        put_heads(side, first + blocks * heads, b, p, features, mass)
    table = lax.broadcasted_iota(jnp.int32, (tables, stacked), 0)
    peak = jnp.full((tables, stacked), NEG, jnp.float32)
    for b in range(blocks):
        own = table == meta[OWNER, b]
        block_peak = get_heads(q_side, first + b * heads, heads)
        peak = jnp.where(own, jnp.maximum(peak, block_peak), peak)
    total = part = jnp.zeros((tables, stacked), jnp.float32)
    for b in range(blocks):
        own = table == meta[OWNER, b]
        at = b * (features // LANES)
        mass = jnp.concatenate(masses[at : at + features // LANES], axis=1)
        mean = jnp.concatenate(means[at : at + features // LANES], axis=1)
        block_peak = get_heads(q_side, first + b * heads, heads)
        scaled = jnp.where(own, jnp.exp2(block_peak - peak) * mass, 0.0)
        total = total + scaled
        part = part + scaled * mean
    here = total > 0.0
    mass = jnp.where(here, total, 1.0)
    tab_ref[0] = jnp.where(here, peak + jnp.log2(mass), NEG)
    tab_ref[1] = part / mass


def moved_weights(meta, pieces, q_side, state, features, tables):
    blocks = state.shape[0]
    stacked = features // HD * TEST
    count = len(pieces)
    return pl.pallas_call(
        lambda *refs: moved_kernel(count, features, *refs),
        in_specs=[smem_spec()] + [vmem_spec()] * (count + 2),
        out_specs=[vmem_spec()] * 3,
        out_shape=[
            pltpu.VMEM((tables * features + 2 * blocks * features // HD, TEST), jnp.float32),
            jax.ShapeDtypeStruct((2, tables, stacked), jnp.float32),
            pltpu.VMEM(state.shape, jnp.bfloat16),
        ],
        input_output_aliases={count + 2: 2},
        scratch_shapes=[pltpu.VMEM((2, BLK, WIDE), jnp.float32)],
        compiler_params=params(10),
        name="moved_weights",
    )(meta, *pieces, q_side, state)


def query_sums_kernel(state, ab_ref, state_out):
    blocks, _, features, _ = ab_ref.shape
    stacked = features // HD * TEST
    for b in range(blocks):
        for p in range(features // LANES):
            keys = state[b, :, 2 * stacked + p * LANES : 2 * stacked + (p + 1) * LANES]
            for n, first in enumerate((stacked, 0)):
                values = state[b, :, first + p * WIDE : first + (p + 1) * WIDE]
                product = lax.dot_general(
                    keys, values, (((0,), (0,)), ((), ())), preferred_element_type=jnp.float32
                )
                ab_ref[b, n, p * LANES : p * LANES + HD, :] = product[:HD, :TEST]
                ab_ref[b, n, p * LANES + HD : (p + 1) * LANES, :] = product[HD:, TEST:]


def query_sums(features, state):
    blocks = state.shape[0]
    return pl.pallas_call(
        query_sums_kernel,
        in_specs=[vmem_spec()],
        out_specs=[vmem_spec()] * 2,
        out_shape=[
            pltpu.VMEM((blocks, 2, features, TEST), jnp.float32),
            pltpu.VMEM(state.shape, jnp.bfloat16),
        ],
        input_output_aliases={0: 1},
        compiler_params=params(8),
        name="query_sums",
    )(state)


def merged(pieces):
    peak = pieces[0][0]
    for piece in pieces[1:]:
        peak = jnp.maximum(peak, piece[0])
    mass = part = 0.0
    for piece in pieces:
        weight = jnp.exp2(piece[0] - peak)
        mass = mass + weight
        part = part + piece[1] * weight
    return peak, mass, part / mass


def query_grad_kernel(count, meta, *refs):
    pieces = refs[:count]
    q_side, g_side, ab_ref = refs[count : count + 3]
    c_ref, d_ref, *q_refs = refs[count + 3 : -2]
    tab_s, acc_s = refs[-2:]
    blocks = ab_ref.shape[0]
    tables, features, _ = acc_s.shape
    heads = features // HD
    tab_s[0], tab_s[1], tab_s[2] = merged(pieces)
    acc_s[...] = jnp.zeros_like(acc_s)
    for b in range(blocks):
        at = meta[SLOT_OUT, meta[OWNER, b]]
        table = pl.ds(meta[OWNER, b], 1)
        row = tables * features + b * heads
        mass = tab_s[1, table, :]
        c = jnp.exp2(get_heads(q_side, row, heads) - tab_s[0, table, :]) / mass
        d = c * (get_heads(g_side, row, heads) - tab_s[2, table, :])
        c_ref[b : b + 1, :] = c
        d_ref[b : b + 1, :] = d
        for h in range(heads):
            rows = slice(h * HD, (h + 1) * HD)
            lanes = slice(h * TEST, (h + 1) * TEST)
            acc_s[at, rows, :] += c[:, lanes] * ab_ref[b, 0, rows, :] + d[:, lanes] * ab_ref[b, 1, rows, :]
    per = tables // len(q_refs)
    for n in range(tables):
        ref = q_refs[n // per]
        ref[n % per] = (acc_s[n] * SCORE_SCALE).T.astype(ref.dtype)


def query_grads(meta, tables, pieces, sides, ab, q_dtypes):
    blocks, _, features, _ = ab.shape
    stacked = features // HD * TEST
    per = tables // len(q_dtypes)
    return pl.pallas_call(
        lambda *refs: query_grad_kernel(len(pieces), *refs),
        in_specs=[smem_spec()] + [vmem_spec()] * (len(pieces) + 3),
        out_specs=[vmem_spec()] * (2 + len(q_dtypes)),
        out_shape=[
            jax.ShapeDtypeStruct((blocks, stacked), jnp.float32),
            jax.ShapeDtypeStruct((blocks, stacked), jnp.float32),
        ]
        + [jax.ShapeDtypeStruct((per, TEST, features), dtype) for dtype in q_dtypes],
        scratch_shapes=[
            pltpu.VMEM((3, tables, stacked), jnp.float32),
            pltpu.VMEM((tables, features, TEST), jnp.float32),
        ],
        compiler_params=params(10),
        name="query_grads",
    )(meta, *pieces, *sides, ab)


def row_grads_kernel(meta, c_ref, d_ref, q_side, g_side, state, dk_hbm, dv_hbm, dk_s, dv_s, out_sem):
    blocks, _, features = dk_s.shape
    stacked = features // HD * TEST
    turned = (((1,), (1,)), ((), ()))
    stores = []
    for b in range(blocks):
        for p in range(features // LANES):
            at = slice(p * LANES, (p + 1) * LANES)
            wide = slice(p * WIDE, (p + 1) * WIDE)
            c = c_ref[b : b + 1, wide]
            d = d_ref[b : b + 1, wide]
            q_t = two_heads(q_side[rows_of(meta, b, p, features), :])
            g_t = two_heads(g_side[rows_of(meta, b, p, features), :])
            for_u = (q_t * (c * SCORE_SCALE)).astype(jnp.bfloat16)
            for_e = jnp.concatenate([g_t * c, q_t * (d * SCORE_SCALE)], axis=0).astype(jnp.bfloat16)
            from_e = lax.dot_general(
                state[b, :, wide], for_e, turned, preferred_element_type=jnp.float32
            )
            moved = state[b, :, stacked + p * WIDE : stacked + (p + 1) * WIDE]
            from_u = lax.dot_general(moved, for_u, turned, preferred_element_type=jnp.float32)
            dv_s[b, :, at] = from_e[:, :LANES].astype(jnp.bfloat16)
            dk_s[b, :, at] = (from_u + from_e[:, LANES:]).astype(jnp.bfloat16)
        rows = pl.ds(b * BLK, BLK)
        stores += every_copy(
            [
                pltpu.make_async_copy(dk_s.at[b], dk_hbm.at[rows], out_sem.at[0, b]),
                pltpu.make_async_copy(dv_s.at[b], dv_hbm.at[rows], out_sem.at[1, b]),
            ]
        )
    for copy in stores:
        copy.wait()


def row_grads(meta, c, d, sides, state, features):
    blocks = state.shape[0]
    return pl.pallas_call(
        row_grads_kernel,
        in_specs=[smem_spec()] + [vmem_spec()] * 5,
        out_specs=[hbm_spec()] * 2,
        out_shape=[jax.ShapeDtypeStruct((blocks * BLK, features), jnp.bfloat16)] * 2,
        scratch_shapes=[
            pltpu.VMEM((blocks, BLK, features), jnp.bfloat16),
            pltpu.VMEM((blocks, BLK, features), jnp.bfloat16),
            pltpu.SemaphoreType.DMA((2, blocks)),
        ],
        compiler_params=params(10),
        name="row_grads",
    )(meta, c, d, *sides, state)


def local(small, query_rows, key_rows, value_rows, cotangent, train_rows, test_rows, block_table):
    features = query_rows.shape[1]
    blocks = key_rows.shape[0] // BLK
    tables = train_rows.shape[0]
    pair = lambda value: lax.ppermute(value, "pair", PAIR)
    step = lambda value, s: lax.ppermute(value, "rows", [(z, z ^ s) for z in range(4)])
    after = lambda value, other: lax.optimization_barrier((value, other))
    index = lambda entries: index_table(
        small, entries, train_rows, test_rows, query_rows, key_rows, value_rows
    )
    if small:
        near = [step(query_rows, s) for s in (1, 2, 3)]
        near_grads = [step(cotangent, 1), step(cotangent, 2)]
        near_grads.append(step(near_grads[1], 1))
        block_table, near[0] = after(block_table, near[0])
        meta, own, state = index(block_table)
        near[0], meta = after(near[0], meta)
        queries = [own, pair(own)]
        for value in near:
            queries += [value, pair(value)]
        q_side, state = block_weights(meta, queries, state, features, tables)
        near_grads[2], q_side = after(near_grads[2], q_side)
        grads = [cotangent, pair(cotangent)]
        for value in near_grads:
            grads += [value, pair(value)]
    else:
        meta, _, state = index(block_table)
        queries = [lax.all_gather(query_rows, RP, axis=0, tiled=True)]
        q_side, state = block_weights(meta, queries, state, features, tables)
        grads = [lax.all_gather(cotangent, RP, axis=0, tiled=True)]
    g_side, tab, state = moved_weights(meta, grads, q_side, state, features, tables)
    if small:
        near = [step(tab, s) for s in (3, 2, 1)]
        ab, state = query_sums(features, state)
        *near, ab = lax.optimization_barrier((*near, ab))
        stats = [tab, pair(tab)]
        for value in near:
            stats += [value, pair(value)]
        dtypes = [jnp.float32, jnp.bfloat16]
    else:
        ab, state = query_sums(features, state)
        peak = lax.pmax(tab[0], RP)
        weight = jnp.exp2(tab[0] - peak)
        total, part = lax.psum(jnp.stack([weight, weight * tab[1]]), RP)
        stats = [jnp.stack([peak + jnp.log2(total), part / total])]
        dtypes = [jnp.float32]
    c, d, *q_terms = query_grads(meta, tables, stats, (q_side, g_side), ab, dtypes)
    if small:
        keep, send = q_terms
        total = keep + pair(send).astype(jnp.float32)
        low = total.astype(jnp.bfloat16)
        got = [step(low[s - 1], s) for s in (3, 2, 1)]
        low, c = lax.optimization_barrier((low, c))
        key_grad, value_grad = row_grads(meta, c, d, (q_side, g_side), state, features)
        query_grad = total[3]
        for value in got:
            query_grad = query_grad + value.astype(jnp.float32)
    else:
        query_grad = lax.psum_scatter(
            q_terms[0].reshape(tables * TEST, features), RP, scatter_dimension=0, tiled=True
        )
        key_grad, value_grad = row_grads(meta, c, d, (q_side, g_side), state, features)
    return query_grad.astype(jnp.bfloat16), key_grad, value_grad


def solution(mesh):
    sizes = mesh.shape
    tables_of_rows = P(("groups", "rows", "pair"), "mp")
    in_specs = (tables_of_rows,) * 4 + (P("groups"),) * 3
    out_specs = (tables_of_rows,) * 3

    def run(query_rows, *rest):
        local_rows = query_rows.shape[0] // (sizes["groups"] * sizes["rows"] * sizes["pair"])
        small = sizes["rows"] == 4 and sizes["pair"] == 2 and local_rows == TEST
        return jax.shard_map(
            lambda *args: local(small, *args),
            mesh=mesh,
            in_specs=in_specs,
            out_specs=out_specs,
            check_vma=False,
        )(query_rows, *rest)

    return run
```

```python
import math

import jax
import jax.numpy as jnp
from jax import lax
from jax.experimental import pallas as pl
from jax.experimental.pallas import tpu as pltpu
from jax.sharding import PartitionSpec as P

HD = 64
TEST = 128
BLK = 512
LANES = 128
WIDE = 2 * TEST
CHUNK = 64

NEG = -1e30
SCORE_SCALE = 1.0 / math.sqrt(HD)
LOG2_SCALE = SCORE_SCALE * math.log2(math.e)
RP = ("rows", "pair")
PAIR = [(0, 1), (1, 0)]


def params(mib):
    return pltpu.CompilerParams(vmem_limit_bytes=mib * 1024 * 1024)


def two_heads(rows):
    feature = lax.broadcasted_iota(jnp.int32, rows.shape, 0)
    zero = jnp.zeros_like(rows)
    return jnp.concatenate(
        [jnp.where(feature < HD, rows, zero), jnp.where(feature < HD, zero, rows)], axis=1
    )


def every_copy(copies):
    for copy in copies:
        copy.start()
    return copies


OWNER, LIVE, TESTN, SLOT_IN, TABLE_OF, SLOT_OUT, OUT_TABLE = range(7)


def vmem_spec():
    return pl.BlockSpec(memory_space=pltpu.VMEM)


def smem_spec():
    return pl.BlockSpec(memory_space=pltpu.SMEM)


def hbm_spec():
    return pl.BlockSpec(memory_space=pltpu.HBM)


def in_hbm(value):
    return pltpu.with_memory_space_constraint(value, pltpu.HBM)


def index_kernel(small, table_hbm, train_hbm, test_hbm, *refs):
    query_hbm, key_hbm, value_hbm, meta, query_ref, state = refs[:6]
    block_table, train_rows, test_rows, count, small_sem, sem = refs[6:]
    blocks = state.shape[0]
    features = key_hbm.shape[1]
    stacked = features // HD * TEST
    entries = every_copy(
        [
            pltpu.make_async_copy(table_hbm, block_table, small_sem.at[0]),
            pltpu.make_async_copy(train_hbm, train_rows, small_sem.at[1]),
            pltpu.make_async_copy(test_hbm, test_rows, small_sem.at[2]),
        ]
    )
    loads = [pltpu.make_async_copy(query_hbm, query_ref, small_sem.at[3])]
    for n, source in enumerate((key_hbm, value_hbm)):
        lanes = pl.ds(2 * stacked + n * features, features)
        for b in range(blocks):
            rows = pl.ds(b * BLK, BLK)
            loads.append(
                pltpu.make_async_copy(source.at[rows], state.at[b, :, lanes], sem.at[n, b])
            )
    every_copy(loads)
    chip = lax.axis_index("rows").astype(jnp.int32)
    core = lax.axis_index("pair").astype(jnp.int32)
    first = lax.axis_index(RP).astype(jnp.int32) * blocks
    for copy in entries:
        copy.wait()
    for t in range(train_rows.shape[0]):
        count[t] = 0
        meta[TESTN, t] = test_rows[t]
        if small:
            away = (t // 2) ^ chip
            not_mine = (t % 2) ^ core
            meta[SLOT_IN, t] = 2 * away + not_mine
            meta[TABLE_OF, t] = 2 * away + not_mine
            meta[SLOT_OUT, t] = 4 * not_mine + ((away + 3) & 3)
            meta[OUT_TABLE, 4 * not_mine + ((away + 3) & 3)] = t
        else:
            for row in (SLOT_IN, TABLE_OF, SLOT_OUT, OUT_TABLE):
                meta[row, t] = t

    def earlier(n, carry):
        table = block_table[n]
        count[table] = count[table] + 1
        return carry

    lax.fori_loop(0, first, earlier, 0)
    for b in range(blocks):
        table = block_table[first + b]
        meta[OWNER, b] = table
        meta[LIVE, b] = jnp.minimum(train_rows[table] - count[table] * BLK, BLK)
        count[table] = count[table] + 1
    for copy in loads:
        copy.wait()


def index_table(small, block_table, train_rows, test_rows, query_rows, key_rows, value_rows):
    tables = train_rows.shape[0]
    features = key_rows.shape[1]
    blocks = key_rows.shape[0] // BLK
    stacked = features // HD * TEST
    arrays = (block_table, train_rows, test_rows, query_rows, key_rows, value_rows)
    return pl.pallas_call(
        lambda *refs: index_kernel(small, *refs),
        in_specs=[hbm_spec()] * 6,
        out_specs=[smem_spec(), vmem_spec(), vmem_spec()],
        out_shape=[
            pltpu.SMEM((7, max(blocks, tables)), jnp.int32),
            pltpu.VMEM(query_rows.shape, query_rows.dtype),
            pltpu.VMEM((blocks, BLK, 2 * stacked + 2 * features), jnp.bfloat16),
        ],
        scratch_shapes=[
            pltpu.SMEM(block_table.shape, jnp.int32),
            pltpu.SMEM((tables,), jnp.int32),
            pltpu.SMEM((tables,), jnp.int32),
            pltpu.SMEM((tables,), jnp.int32),
            pltpu.SemaphoreType.DMA((4,)),
            pltpu.SemaphoreType.DMA((2, blocks)),
        ],
        compiler_params=params(4),
        name="index_table",
    )(*map(in_hbm, arrays))


def turn_pieces(pieces, store):
    at_slot = 0
    for piece in pieces:
        for m in range(piece.shape[0] // TEST):
            store(at_slot, piece[m * TEST : (m + 1) * TEST, :].T)
            at_slot += 1


def fold(values, op):
    return op(values.reshape(CHUNK // 8, 8, WIDE), axis=0)


def rows_of(meta, b, p, features):
    at_slot = meta[SLOT_IN, meta[OWNER, b]]
    return pl.ds(pl.multiple_of(at_slot * features + p * LANES, LANES), LANES)


def put_heads(side, first, b, p, features, row):
    at = first + b * features // HD + 2 * p
    side[at : at + 1, :] = row[:, :TEST]
    side[at + 1 : at + 2, :] = row[:, TEST:]


def get_heads(side, row, heads):
    return jnp.concatenate([side[row + h : row + h + 1, :] for h in range(heads)], axis=1)


def units_of(blocks, features):
    return [(b, p) for b in range(blocks) for p in range(features // LANES)]


def weights_kernel(count, features, meta, *refs):
    pieces = refs[:count]
    state, side, state_out, scores_s = refs[count:]
    blocks = state.shape[0]
    stacked = features // HD * TEST
    first_peak = side.shape[0] - blocks * features // HD
    units = units_of(blocks, features)

    def store(at_slot, turned):
        side[at_slot * features : (at_slot + 1) * features, :] = turned.astype(jnp.float32)

    turn_pieces(pieces, store)
    peaks = [None] * len(units)
    for t in range(len(units) + 1):
        if t < len(units):
            b, p = units[t]
            live = meta[LIVE, b]
            queries = two_heads(side[rows_of(meta, b, p, features), :]).astype(jnp.bfloat16)
            peak = jnp.full((8, WIDE), NEG, jnp.float32)
        for r in range(0, BLK, CHUNK):
            rows = slice(r, r + CHUNK)
            if t > 0:
                last_b, last_p = units[t - 1]
                weights = jnp.exp2(scores_s[(t - 1) % 2, rows, :] * LOG2_SCALE - peaks[t - 1])
                state_out[last_b, rows, last_p * WIDE : (last_p + 1) * WIDE] = weights.astype(
                    jnp.bfloat16
                )
            if t < len(units):
                keys = state[b, rows, 2 * stacked + p * LANES : 2 * stacked + (p + 1) * LANES]
                scores = jnp.dot(keys, queries, preferred_element_type=jnp.float32)
                row = lax.broadcasted_iota(jnp.int32, scores.shape, 0)
                scores = jnp.where(row < live - r, scores, NEG)
                scores_s[t % 2, rows, :] = scores
                peak = jnp.maximum(peak, fold(scores, jnp.max))
        if t < len(units):
            peaks[t] = jnp.max(peak, axis=0, keepdims=True) * LOG2_SCALE
    for (b, p), peak in zip(units, peaks):
        put_heads(side, first_peak, b, p, features, peak)


def block_weights(meta, pieces, state, features, tables):
    blocks = state.shape[0]
    count = len(pieces)
    return pl.pallas_call(
        lambda *refs: weights_kernel(count, features, *refs),
        in_specs=[smem_spec()] + [vmem_spec()] * (count + 1),
        out_specs=[vmem_spec()] * 2,
        out_shape=[
            pltpu.VMEM((tables * features + blocks * features // HD, TEST), jnp.float32),
            pltpu.VMEM(state.shape, jnp.bfloat16),
        ],
        input_output_aliases={count + 1: 1},
        scratch_shapes=[pltpu.VMEM((2, BLK, WIDE), jnp.float32)],
        compiler_params=params(10),
        name="block_weights",
    )(meta, *pieces, state)


def moved_kernel(count, features, meta, *refs):
    pieces = refs[:count]
    q_side, state, side, tab_ref, state_out = refs[count : count + 5]
    dprobs_s = refs[count + 5]
    tables = tab_ref.shape[1]
    stacked = features // HD * TEST
    blocks = state.shape[0]
    heads = features // HD
    first = tables * features
    units = units_of(blocks, features)
    query = lax.broadcasted_iota(jnp.int32, (features, TEST), 1)

    def store(at_slot, turned):
        live = query < meta[TESTN, meta[TABLE_OF, at_slot]]
        turned = jnp.where(live, turned, jnp.zeros_like(turned)).astype(jnp.float32)
        side[at_slot * features : (at_slot + 1) * features, :] = turned

    turn_pieces(pieces, store)
    means, masses = [None] * len(units), [None] * len(units)
    zero = jnp.zeros((8, WIDE), jnp.float32)
    for t in range(len(units) + 1):
        if t < len(units):
            b, p = units[t]
            grads = two_heads(side[rows_of(meta, b, p, features), :]).astype(jnp.bfloat16)
            mass = part = zero
        for r in range(0, BLK, CHUNK):
            rows = slice(r, r + CHUNK)
            if t > 0:
                last_b, last_p = units[t - 1]
                weights = state[last_b, rows, last_p * WIDE : (last_p + 1) * WIDE]
                moved = weights.astype(jnp.float32) * (dprobs_s[(t - 1) % 2, rows, :] - means[t - 1])
                lanes = slice(stacked + last_p * WIDE, stacked + (last_p + 1) * WIDE)
                state_out[last_b, rows, lanes] = moved.astype(jnp.bfloat16)
            if t < len(units):
                lane = 2 * stacked + features + p * LANES
                values = state[b, rows, lane : lane + LANES]
                dprobs = jnp.dot(values, grads, preferred_element_type=jnp.float32)
                weights = state[b, rows, p * WIDE : (p + 1) * WIDE].astype(jnp.float32)
                mass = mass + fold(weights, jnp.sum)
                part = part + fold(weights * dprobs, jnp.sum)
                dprobs_s[t % 2, rows, :] = dprobs
        if t < len(units):
            mass = jnp.sum(mass, axis=0, keepdims=True)
            masses[t] = mass
            means[t] = jnp.sum(part, axis=0, keepdims=True) / mass
    for (b, p), mean, mass in zip(units, means, masses):
        put_heads(side, first, b, p, features, mean)
        put_heads(side, first + blocks * heads, b, p, features, mass)
    table = lax.broadcasted_iota(jnp.int32, (tables, stacked), 0)
    peak = jnp.full((tables, stacked), NEG, jnp.float32)
    for b in range(blocks):
        own = table == meta[OWNER, b]
        block_peak = get_heads(q_side, first + b * heads, heads)
        peak = jnp.where(own, jnp.maximum(peak, block_peak), peak)
    total = part = jnp.zeros((tables, stacked), jnp.float32)
    for b in range(blocks):
        own = table == meta[OWNER, b]
        at = b * (features // LANES)
        mass = jnp.concatenate(masses[at : at + features // LANES], axis=1)
        mean = jnp.concatenate(means[at : at + features // LANES], axis=1)
        block_peak = get_heads(q_side, first + b * heads, heads)
        scaled = jnp.where(own, jnp.exp2(block_peak - peak) * mass, 0.0)
        total = total + scaled
        part = part + scaled * mean
    here = total > 0.0
    mass = jnp.where(here, total, 1.0)
    tab_ref[0] = jnp.where(here, peak + jnp.log2(mass), NEG)
    tab_ref[1] = part / mass


def moved_weights(meta, pieces, q_side, state, features, tables):
    blocks = state.shape[0]
    stacked = features // HD * TEST
    count = len(pieces)
    return pl.pallas_call(
        lambda *refs: moved_kernel(count, features, *refs),
        in_specs=[smem_spec()] + [vmem_spec()] * (count + 2),
        out_specs=[vmem_spec()] * 3,
        out_shape=[
            pltpu.VMEM((tables * features + 2 * blocks * features // HD, TEST), jnp.float32),
            jax.ShapeDtypeStruct((2, tables, stacked), jnp.float32),
            pltpu.VMEM(state.shape, jnp.bfloat16),
        ],
        input_output_aliases={count + 2: 2},
        scratch_shapes=[pltpu.VMEM((2, BLK, WIDE), jnp.float32)],
        compiler_params=params(10),
        name="moved_weights",
    )(meta, *pieces, q_side, state)


def merged(pieces):
    peak = pieces[0][0]
    for piece in pieces[1:]:
        peak = jnp.maximum(peak, piece[0])
    mass = part = 0.0
    for piece in pieces:
        weight = jnp.exp2(piece[0] - peak)
        mass = mass + weight
        part = part + piece[1] * weight
    return peak, mass, part / mass


def query_sums_kernel(state, ab_ref, state_out):
    blocks, _, features, _ = ab_ref.shape
    stacked = features // HD * TEST
    for b in range(blocks):
        for p in range(features // LANES):
            keys = state[b, :, 2 * stacked + p * LANES : 2 * stacked + (p + 1) * LANES]
            for n, first in enumerate((stacked, 0)):
                values = state[b, :, first + p * WIDE : first + (p + 1) * WIDE]
                product = lax.dot_general(
                    keys, values, (((0,), (0,)), ((), ())), preferred_element_type=jnp.float32
                )
                ab_ref[b, n, p * LANES : p * LANES + HD, :] = product[:HD, :TEST]
                ab_ref[b, n, p * LANES + HD : (p + 1) * LANES, :] = product[HD:, TEST:]


def query_sums(features, state):
    blocks = state.shape[0]
    return pl.pallas_call(
        query_sums_kernel,
        in_specs=[vmem_spec()],
        out_specs=[vmem_spec()] * 2,
        out_shape=[
            pltpu.VMEM((blocks, 2, features, TEST), jnp.float32),
            pltpu.VMEM(state.shape, jnp.bfloat16),
        ],
        input_output_aliases={0: 1},
        compiler_params=params(8),
        name="query_sums",
    )(state)


def chip_sums_kernel(count, meta, *refs):
    tabs = refs[:count]
    q_side, g_side, ab_ref, *sums, acc_s, tab_s = refs[count:]
    tables, _, features, _ = acc_s.shape
    blocks = ab_ref.shape[0]
    heads = features // HD
    tab_s[0], tab_s[1], tab_s[2] = merged(tabs)
    acc_s[...] = jnp.zeros_like(acc_s)
    for b in range(blocks):
        at = meta[SLOT_OUT, meta[OWNER, b]]
        table = pl.ds(meta[OWNER, b], 1)
        row = tables * features + b * heads
        c = jnp.exp2(get_heads(q_side, row, heads) - tab_s[0, table, :]) / tab_s[1, table, :]
        d = c * (get_heads(g_side, row, heads) - tab_s[2, table, :])
        for h in range(heads):
            rows = slice(h * HD, (h + 1) * HD)
            lanes = slice(h * TEST, (h + 1) * TEST)
            moved, plain = ab_ref[b, 0, rows, :], ab_ref[b, 1, rows, :]
            acc_s[at, 0, rows, :] += c[:, lanes] * moved + d[:, lanes] * plain
            acc_s[at, 1, rows, :] += c[:, lanes] * plain
    per = tables // len(sums)
    for n, ref in enumerate(sums):
        ref[...] = acc_s[n * per : (n + 1) * per].astype(ref.dtype)


def chip_sums(meta, tabs, q_side, g_side, ab, features, dtypes):
    tables, stacked = tabs[0].shape[1:]
    count = len(tabs)
    per = tables // len(dtypes)
    return pl.pallas_call(
        lambda *refs: chip_sums_kernel(count, *refs),
        in_specs=[smem_spec()] + [vmem_spec()] * (count + 3),
        out_specs=[vmem_spec()] * len(dtypes),
        out_shape=[jax.ShapeDtypeStruct((per, 2, features, TEST), dtype) for dtype in dtypes],
        scratch_shapes=[
            pltpu.VMEM((tables, 2, features, TEST), jnp.float32),
            pltpu.VMEM((3, tables, stacked), jnp.float32),
        ],
        compiler_params=params(10),
        name="chip_sums",
    )(meta, *tabs, q_side, g_side, ab)


def query_grad_kernel(near, count, held, meta, *refs):
    chip, pieces = refs[:near], refs[near : near + count]
    count += near
    sums = refs[count : count + held]
    q_side, g_side, c_ref, d_ref, *outs, chip_s, tab_s = refs[count + held :]
    blocks, stacked = c_ref.shape
    heads = stacked // TEST
    first = q_side.shape[0] - blocks * heads
    chip_s[0], chip_s[1], chip_s[2] = merged(chip)
    tab_s[0], tab_s[1], tab_s[2] = merged(pieces)
    for n, ref in enumerate(outs):
        table = pl.ds(meta[OUT_TABLE, n], 1)
        c = jnp.exp2(chip_s[0, table, :] - tab_s[0, table, :])
        c = c * chip_s[1, table, :] / tab_s[1, table, :]
        d = c * (chip_s[2, table, :] - tab_s[2, table, :])
        parts = []
        for h in range(heads):
            rows = slice(h * HD, (h + 1) * HD)
            lanes = slice(h * TEST, (h + 1) * TEST)
            moved = sum(value[n, 0, rows, :].astype(jnp.float32) for value in sums)
            plain = sum(value[n, 1, rows, :].astype(jnp.float32) for value in sums)
            parts.append(c[:, lanes] * moved + d[:, lanes] * plain)
        ref[...] = (jnp.concatenate(parts, axis=0) * SCORE_SCALE).T.astype(ref.dtype)
    for b in range(blocks):
        table = pl.ds(meta[OWNER, b], 1)
        row = first + b * heads
        c = jnp.exp2(get_heads(q_side, row, heads) - tab_s[0, table, :]) / tab_s[1, table, :]
        c_ref[b : b + 1, :] = c
        d_ref[b : b + 1, :] = c * (get_heads(g_side, row, heads) - tab_s[2, table, :])


def query_grads(meta, chip, pieces, sums, q_side, g_side, blocks, q_dtypes):
    tables, stacked = pieces[0].shape[1:]
    features = sums[0].shape[2]
    return pl.pallas_call(
        lambda *refs: query_grad_kernel(len(chip), len(pieces), len(sums), *refs),
        in_specs=[smem_spec()] + [vmem_spec()] * (len(chip) + len(pieces) + len(sums) + 2),
        out_specs=[vmem_spec()] * (2 + len(q_dtypes)),
        out_shape=[
            jax.ShapeDtypeStruct((blocks, stacked), jnp.float32),
            jax.ShapeDtypeStruct((blocks, stacked), jnp.float32),
        ]
        + [jax.ShapeDtypeStruct((TEST, features), dtype) for dtype in q_dtypes],
        scratch_shapes=[
            pltpu.VMEM((3, tables, stacked), jnp.float32),
            pltpu.VMEM((3, tables, stacked), jnp.float32),
        ],
        compiler_params=params(10),
        name="query_grads",
    )(meta, *chip, *pieces, *sums, q_side, g_side)


def row_grads_kernel(meta, c_ref, d_ref, q_side, g_side, state, dk_hbm, dv_hbm, dk_s, dv_s, out_sem):
    blocks, _, features = dk_s.shape
    stacked = features // HD * TEST
    turned = (((1,), (1,)), ((), ()))
    stores = []
    for b in range(blocks):
        for p in range(features // LANES):
            at = slice(p * LANES, (p + 1) * LANES)
            wide = slice(p * WIDE, (p + 1) * WIDE)
            c = c_ref[b : b + 1, wide]
            d = d_ref[b : b + 1, wide]
            q_t = two_heads(q_side[rows_of(meta, b, p, features), :])
            g_t = two_heads(g_side[rows_of(meta, b, p, features), :])
            for_u = (q_t * (c * SCORE_SCALE)).astype(jnp.bfloat16)
            for_e = jnp.concatenate([g_t * c, q_t * (d * SCORE_SCALE)], axis=0).astype(jnp.bfloat16)
            from_e = lax.dot_general(
                state[b, :, wide], for_e, turned, preferred_element_type=jnp.float32
            )
            moved = state[b, :, stacked + p * WIDE : stacked + (p + 1) * WIDE]
            from_u = lax.dot_general(moved, for_u, turned, preferred_element_type=jnp.float32)
            dv_s[b, :, at] = from_e[:, :LANES].astype(jnp.bfloat16)
            dk_s[b, :, at] = (from_u + from_e[:, LANES:]).astype(jnp.bfloat16)
        rows = pl.ds(b * BLK, BLK)
        stores += every_copy(
            [
                pltpu.make_async_copy(dk_s.at[b], dk_hbm.at[rows], out_sem.at[0, b]),
                pltpu.make_async_copy(dv_s.at[b], dv_hbm.at[rows], out_sem.at[1, b]),
            ]
        )
    for copy in stores:
        copy.wait()


def row_grads(meta, c, d, sides, state, features):
    blocks = state.shape[0]
    return pl.pallas_call(
        row_grads_kernel,
        in_specs=[smem_spec()] + [vmem_spec()] * 5,
        out_specs=[hbm_spec()] * 2,
        out_shape=[jax.ShapeDtypeStruct((blocks * BLK, features), jnp.bfloat16)] * 2,
        scratch_shapes=[
            pltpu.VMEM((blocks, BLK, features), jnp.bfloat16),
            pltpu.VMEM((blocks, BLK, features), jnp.bfloat16),
            pltpu.SemaphoreType.DMA((2, blocks)),
        ],
        compiler_params=params(10),
        name="row_grads",
    )(meta, c, d, *sides, state)


def local(small, query_rows, key_rows, value_rows, cotangent, train_rows, test_rows, block_table):
    features = query_rows.shape[1]
    blocks = key_rows.shape[0] // BLK
    tables = train_rows.shape[0]
    pair = lambda value: lax.ppermute(value, "pair", PAIR)
    step = lambda value, s: lax.ppermute(value, "rows", [(z, z ^ s) for z in range(4)])
    after = lambda value, other: lax.optimization_barrier((value, other))
    index = lambda entries: index_table(
        small, entries, train_rows, test_rows, query_rows, key_rows, value_rows
    )
    if small:
        near = [step(query_rows, s) for s in (1, 2, 3)]
        near_grads = [step(cotangent, 1), step(cotangent, 2)]
        near_grads.append(step(near_grads[1], 1))
        block_table, near[0] = after(block_table, near[0])
        meta, own, state = index(block_table)
        near[0], meta = after(near[0], meta)
        queries = [own, pair(own)]
        for value in near:
            queries += [value, pair(value)]
        q_side, state = block_weights(meta, queries, state, features, tables)
        near_grads[2], q_side = after(near_grads[2], q_side)
        grads = [cotangent, pair(cotangent)]
        for value in near_grads:
            grads += [value, pair(value)]
    else:
        meta, _, state = index(block_table)
        queries = [lax.all_gather(query_rows, RP, axis=0, tiled=True)]
        q_side, state = block_weights(meta, queries, state, features, tables)
        grads = [lax.all_gather(cotangent, RP, axis=0, tiled=True)]
    g_side, tab, state = moved_weights(meta, grads, q_side, state, features, tables)
    if small:
        near = [step(tab, s) for s in (3, 2, 1)]
        own = [tab, pair(tab)]
        ab, state = query_sums(features, state)
        *near, ab = lax.optimization_barrier((*near, ab))
        keep, send = chip_sums(
            meta, own, q_side, g_side, ab, features, [jnp.float32, jnp.bfloat16]
        )
        received = pair(send)
        stats = own
        for value in near:
            stats = stats + [value, pair(value)]
        dtypes = [jnp.bfloat16] * 3 + [jnp.float32]
        c, d, *low, query_grad = query_grads(
            meta, own, stats, [keep, received], q_side, g_side, blocks, dtypes
        )
        got = [step(low[s - 1], s) for s in (3, 2, 1)]
        *low, c = lax.optimization_barrier((*low, c))
        key_grad, value_grad = row_grads(meta, c, d, (q_side, g_side), state, features)
        for value in got:
            query_grad = query_grad + value.astype(jnp.float32)
    else:
        ab, state = query_sums(features, state)
        (sums,) = chip_sums(meta, [tab], q_side, g_side, ab, features, [jnp.float32])
        peak = lax.pmax(tab[0], RP)
        weight = jnp.exp2(tab[0] - peak)
        total, part = lax.psum(jnp.stack([weight, weight * tab[1]]), RP)
        rest = jnp.stack([peak + jnp.log2(total), part / total])
        c, d, *terms = query_grads(
            meta, [tab], [rest], [sums], q_side, g_side, blocks, [jnp.float32] * tables
        )
        query_grad = lax.psum_scatter(
            jnp.concatenate(terms, axis=0), RP, scatter_dimension=0, tiled=True
        )
        key_grad, value_grad = row_grads(meta, c, d, (q_side, g_side), state, features)
    return query_grad.astype(jnp.bfloat16), key_grad, value_grad


def solution(mesh):
    sizes = mesh.shape
    tables_of_rows = P(("groups", "rows", "pair"), "mp")
    in_specs = (tables_of_rows,) * 4 + (P("groups"),) * 3
    out_specs = (tables_of_rows,) * 3

    def run(query_rows, *rest):
        local_rows = query_rows.shape[0] // (sizes["groups"] * sizes["rows"] * sizes["pair"])
        small = sizes["rows"] == 4 and sizes["pair"] == 2 and local_rows == TEST
        return jax.shard_map(
            lambda *args: local(small, *args),
            mesh=mesh,
            in_specs=in_specs,
            out_specs=out_specs,
            check_vma=False,
        )(query_rows, *rest)

    return run
```

```python
import math

import jax
import jax.numpy as jnp
from jax import lax
from jax.experimental import pallas as pl
from jax.experimental.pallas import tpu as pltpu
from jax.sharding import PartitionSpec as P

HD = 64
TEST = 128
BLK = 512
LANES = 128
WIDE = 2 * TEST
CHUNK = 64

NEG = -1e30
SCORE_SCALE = 1.0 / math.sqrt(HD)
LOG2_SCALE = SCORE_SCALE * math.log2(math.e)
RP = ("rows", "pair")
PAIR = [(0, 1), (1, 0)]


def params(mib):
    return pltpu.CompilerParams(vmem_limit_bytes=mib * 1024 * 1024)


def two_heads(rows):
    feature = lax.broadcasted_iota(jnp.int32, rows.shape, 0)
    zero = jnp.zeros_like(rows)
    return jnp.concatenate(
        [jnp.where(feature < HD, rows, zero), jnp.where(feature < HD, zero, rows)], axis=1
    )


def every_copy(copies):
    for copy in copies:
        copy.start()
    return copies


OWNER, LIVE, TESTN, SLOT_IN, TABLE_OF, SLOT_OUT, OUT_TABLE = range(7)


def vmem_spec():
    return pl.BlockSpec(memory_space=pltpu.VMEM)


def smem_spec():
    return pl.BlockSpec(memory_space=pltpu.SMEM)


def hbm_spec():
    return pl.BlockSpec(memory_space=pltpu.HBM)


def in_hbm(value):
    return pltpu.with_memory_space_constraint(value, pltpu.HBM)


def index_kernel(small, table_hbm, train_hbm, test_hbm, *refs):
    query_hbm, key_hbm, value_hbm, meta, query_ref, state = refs[:6]
    block_table, train_rows, test_rows, count, small_sem, sem = refs[6:]
    blocks = state.shape[0]
    features = key_hbm.shape[1]
    stacked = features // HD * TEST
    entries = every_copy(
        [
            pltpu.make_async_copy(table_hbm, block_table, small_sem.at[0]),
            pltpu.make_async_copy(train_hbm, train_rows, small_sem.at[1]),
            pltpu.make_async_copy(test_hbm, test_rows, small_sem.at[2]),
        ]
    )
    loads = [pltpu.make_async_copy(query_hbm, query_ref, small_sem.at[3])]
    for n, source in enumerate((key_hbm, value_hbm)):
        lanes = pl.ds(2 * stacked + n * features, features)
        for b in range(blocks):
            rows = pl.ds(b * BLK, BLK)
            loads.append(
                pltpu.make_async_copy(source.at[rows], state.at[b, :, lanes], sem.at[n, b])
            )
    every_copy(loads)
    chip = lax.axis_index("rows").astype(jnp.int32)
    core = lax.axis_index("pair").astype(jnp.int32)
    first = lax.axis_index(RP).astype(jnp.int32) * blocks
    for copy in entries:
        copy.wait()
    for t in range(train_rows.shape[0]):
        count[t] = 0
        meta[TESTN, t] = test_rows[t]
        if small:
            away = (t // 2) ^ chip
            not_mine = (t % 2) ^ core
            meta[SLOT_IN, t] = 2 * away + not_mine
            meta[TABLE_OF, t] = 2 * away + not_mine
            meta[SLOT_OUT, t] = 4 * not_mine + ((away + 3) & 3)
            meta[OUT_TABLE, 4 * not_mine + ((away + 3) & 3)] = t
        else:
            for row in (SLOT_IN, TABLE_OF, SLOT_OUT, OUT_TABLE):
                meta[row, t] = t

    def earlier(n, carry):
        table = block_table[n]
        count[table] = count[table] + 1
        return carry

    lax.fori_loop(0, first, earlier, 0)
    for b in range(blocks):
        table = block_table[first + b]
        meta[OWNER, b] = table
        meta[LIVE, b] = jnp.minimum(train_rows[table] - count[table] * BLK, BLK)
        count[table] = count[table] + 1
    for copy in loads:
        copy.wait()


def index_table(small, block_table, train_rows, test_rows, query_rows, key_rows, value_rows):
    tables = train_rows.shape[0]
    features = key_rows.shape[1]
    blocks = key_rows.shape[0] // BLK
    stacked = features // HD * TEST
    arrays = (block_table, train_rows, test_rows, query_rows, key_rows, value_rows)
    return pl.pallas_call(
        lambda *refs: index_kernel(small, *refs),
        in_specs=[hbm_spec()] * 6,
        out_specs=[smem_spec(), vmem_spec(), vmem_spec()],
        out_shape=[
            pltpu.SMEM((7, max(blocks, tables)), jnp.int32),
            pltpu.VMEM(query_rows.shape, query_rows.dtype),
            pltpu.VMEM((blocks, BLK, 2 * stacked + 2 * features), jnp.bfloat16),
        ],
        scratch_shapes=[
            pltpu.SMEM(block_table.shape, jnp.int32),
            pltpu.SMEM((tables,), jnp.int32),
            pltpu.SMEM((tables,), jnp.int32),
            pltpu.SMEM((tables,), jnp.int32),
            pltpu.SemaphoreType.DMA((4,)),
            pltpu.SemaphoreType.DMA((2, blocks)),
        ],
        compiler_params=params(4),
        name="index_table",
    )(*map(in_hbm, arrays))


def turn_pieces(pieces, store):
    at_slot = 0
    for piece in pieces:
        for m in range(piece.shape[0] // TEST):
            store(at_slot, piece[m * TEST : (m + 1) * TEST, :].T)
            at_slot += 1


def fold(values, op):
    return op(values.reshape(CHUNK // 8, 8, WIDE), axis=0)


def rows_of(meta, b, p, features):
    at_slot = meta[SLOT_IN, meta[OWNER, b]]
    return pl.ds(pl.multiple_of(at_slot * features + p * LANES, LANES), LANES)


def put_heads(side, first, b, p, features, row):
    at = first + b * features // HD + 2 * p
    side[at : at + 1, :] = row[:, :TEST]
    side[at + 1 : at + 2, :] = row[:, TEST:]


def get_heads(side, row, heads):
    return jnp.concatenate([side[row + h : row + h + 1, :] for h in range(heads)], axis=1)


def units_of(blocks, features):
    return [(b, p) for b in range(blocks) for p in range(features // LANES)]


def weights_kernel(count, features, meta, *refs):
    pieces = refs[:count]
    state, side, state_out, scores_s = refs[count:]
    blocks = state.shape[0]
    stacked = features // HD * TEST
    first_peak = side.shape[0] - blocks * features // HD
    units = units_of(blocks, features)

    def store(at_slot, turned):
        side[at_slot * features : (at_slot + 1) * features, :] = turned.astype(jnp.float32)

    turn_pieces(pieces, store)
    peaks = [None] * len(units)
    for t in range(len(units) + 1):
        if t < len(units):
            b, p = units[t]
            live = meta[LIVE, b]
            queries = two_heads(side[rows_of(meta, b, p, features), :]).astype(jnp.bfloat16)
            peak = jnp.full((8, WIDE), NEG, jnp.float32)
        for r in range(0, BLK, CHUNK):
            rows = slice(r, r + CHUNK)
            if t > 0:
                last_b, last_p = units[t - 1]
                weights = jnp.exp2(scores_s[(t - 1) % 2, rows, :] * LOG2_SCALE - peaks[t - 1])
                state_out[last_b, rows, last_p * WIDE : (last_p + 1) * WIDE] = weights.astype(
                    jnp.bfloat16
                )
            if t < len(units):
                keys = state[b, rows, 2 * stacked + p * LANES : 2 * stacked + (p + 1) * LANES]
                scores = jnp.dot(keys, queries, preferred_element_type=jnp.float32)
                row = lax.broadcasted_iota(jnp.int32, scores.shape, 0)
                scores = jnp.where(row < live - r, scores, NEG)
                scores_s[t % 2, rows, :] = scores
                peak = jnp.maximum(peak, fold(scores, jnp.max))
        if t < len(units):
            peaks[t] = jnp.max(peak, axis=0, keepdims=True) * LOG2_SCALE
    for (b, p), peak in zip(units, peaks):
        put_heads(side, first_peak, b, p, features, peak)


def block_weights(meta, pieces, state, features, tables):
    blocks = state.shape[0]
    count = len(pieces)
    return pl.pallas_call(
        lambda *refs: weights_kernel(count, features, *refs),
        in_specs=[smem_spec()] + [vmem_spec()] * (count + 1),
        out_specs=[vmem_spec()] * 2,
        out_shape=[
            pltpu.VMEM((tables * features + blocks * features // HD, TEST), jnp.float32),
            pltpu.VMEM(state.shape, jnp.bfloat16),
        ],
        input_output_aliases={count + 1: 1},
        scratch_shapes=[pltpu.VMEM((2, BLK, WIDE), jnp.float32)],
        compiler_params=params(10),
        name="block_weights",
    )(meta, *pieces, state)


def moved_kernel(count, features, meta, *refs):
    pieces = refs[:count]
    q_side, state, side, tab_ref, state_out = refs[count : count + 5]
    dprobs_s = refs[count + 5]
    tables = tab_ref.shape[1]
    stacked = features // HD * TEST
    blocks = state.shape[0]
    heads = features // HD
    first = tables * features
    units = units_of(blocks, features)
    query = lax.broadcasted_iota(jnp.int32, (features, TEST), 1)

    def store(at_slot, turned):
        live = query < meta[TESTN, meta[TABLE_OF, at_slot]]
        turned = jnp.where(live, turned, jnp.zeros_like(turned)).astype(jnp.float32)
        side[at_slot * features : (at_slot + 1) * features, :] = turned

    turn_pieces(pieces, store)
    means, masses = [None] * len(units), [None] * len(units)
    zero = jnp.zeros((8, WIDE), jnp.float32)
    for t in range(len(units) + 1):
        if t < len(units):
            b, p = units[t]
            grads = two_heads(side[rows_of(meta, b, p, features), :]).astype(jnp.bfloat16)
            mass = part = zero
        for r in range(0, BLK, CHUNK):
            rows = slice(r, r + CHUNK)
            if t > 0:
                last_b, last_p = units[t - 1]
                weights = state[last_b, rows, last_p * WIDE : (last_p + 1) * WIDE]
                moved = weights.astype(jnp.float32) * (dprobs_s[(t - 1) % 2, rows, :] - means[t - 1])
                lanes = slice(stacked + last_p * WIDE, stacked + (last_p + 1) * WIDE)
                state_out[last_b, rows, lanes] = moved.astype(jnp.bfloat16)
            if t < len(units):
                lane = 2 * stacked + features + p * LANES
                values = state[b, rows, lane : lane + LANES]
                dprobs = jnp.dot(values, grads, preferred_element_type=jnp.float32)
                weights = state[b, rows, p * WIDE : (p + 1) * WIDE].astype(jnp.float32)
                mass = mass + fold(weights, jnp.sum)
                part = part + fold(weights * dprobs, jnp.sum)
                dprobs_s[t % 2, rows, :] = dprobs
        if t < len(units):
            mass = jnp.sum(mass, axis=0, keepdims=True)
            masses[t] = mass
            means[t] = jnp.sum(part, axis=0, keepdims=True) / mass
    for (b, p), mean, mass in zip(units, means, masses):
        put_heads(side, first, b, p, features, mean)
        put_heads(side, first + blocks * heads, b, p, features, mass)
    table = lax.broadcasted_iota(jnp.int32, (tables, stacked), 0)
    peak = jnp.full((tables, stacked), NEG, jnp.float32)
    for b in range(blocks):
        own = table == meta[OWNER, b]
        block_peak = get_heads(q_side, first + b * heads, heads)
        peak = jnp.where(own, jnp.maximum(peak, block_peak), peak)
    total = part = jnp.zeros((tables, stacked), jnp.float32)
    for b in range(blocks):
        own = table == meta[OWNER, b]
        at = b * (features // LANES)
        mass = jnp.concatenate(masses[at : at + features // LANES], axis=1)
        mean = jnp.concatenate(means[at : at + features // LANES], axis=1)
        block_peak = get_heads(q_side, first + b * heads, heads)
        scaled = jnp.where(own, jnp.exp2(block_peak - peak) * mass, 0.0)
        total = total + scaled
        part = part + scaled * mean
    here = total > 0.0
    mass = jnp.where(here, total, 1.0)
    tab_ref[0] = jnp.where(here, peak + jnp.log2(mass), NEG)
    tab_ref[1] = part / mass


def moved_weights(meta, pieces, q_side, state, features, tables):
    blocks = state.shape[0]
    stacked = features // HD * TEST
    count = len(pieces)
    return pl.pallas_call(
        lambda *refs: moved_kernel(count, features, *refs),
        in_specs=[smem_spec()] + [vmem_spec()] * (count + 2),
        out_specs=[vmem_spec()] * 3,
        out_shape=[
            pltpu.VMEM((tables * features + 2 * blocks * features // HD, TEST), jnp.float32),
            jax.ShapeDtypeStruct((2, tables, stacked), jnp.float32),
            pltpu.VMEM(state.shape, jnp.bfloat16),
        ],
        input_output_aliases={count + 2: 2},
        scratch_shapes=[pltpu.VMEM((2, BLK, WIDE), jnp.float32)],
        compiler_params=params(10),
        name="moved_weights",
    )(meta, *pieces, q_side, state)


def merged(pieces):
    peak = pieces[0][0]
    for piece in pieces[1:]:
        peak = jnp.maximum(peak, piece[0])
    mass = part = 0.0
    for piece in pieces:
        weight = jnp.exp2(piece[0] - peak)
        mass = mass + weight
        part = part + piece[1] * weight
    return peak, mass, part / mass


def query_sums_kernel(state, ab_ref, state_out):
    blocks, _, features, _ = ab_ref.shape
    stacked = features // HD * TEST
    for b in range(blocks):
        for p in range(features // LANES):
            keys = state[b, :, 2 * stacked + p * LANES : 2 * stacked + (p + 1) * LANES]
            for n, first in enumerate((stacked, 0)):
                values = state[b, :, first + p * WIDE : first + (p + 1) * WIDE]
                product = lax.dot_general(
                    keys, values, (((0,), (0,)), ((), ())), preferred_element_type=jnp.float32
                )
                ab_ref[b, n, p * LANES : p * LANES + HD, :] = product[:HD, :TEST]
                ab_ref[b, n, p * LANES + HD : (p + 1) * LANES, :] = product[HD:, TEST:]


def query_sums(features, state):
    blocks = state.shape[0]
    return pl.pallas_call(
        query_sums_kernel,
        in_specs=[vmem_spec()],
        out_specs=[vmem_spec()] * 2,
        out_shape=[
            pltpu.VMEM((blocks, 2, features, TEST), jnp.float32),
            pltpu.VMEM(state.shape, jnp.bfloat16),
        ],
        input_output_aliases={0: 1},
        compiler_params=params(8),
        name="query_sums",
    )(state)


def chip_sums_kernel(count, meta, *refs):
    tabs = refs[:count]
    q_side, g_side, ab_ref, *sums, acc_s, tab_s = refs[count:]
    tables, _, features, _ = acc_s.shape
    blocks = ab_ref.shape[0]
    heads = features // HD
    tab_s[0], tab_s[1], tab_s[2] = merged(tabs)
    acc_s[...] = jnp.zeros_like(acc_s)
    for b in range(blocks):
        at = meta[SLOT_OUT, meta[OWNER, b]]
        table = pl.ds(meta[OWNER, b], 1)
        row = tables * features + b * heads
        c = jnp.exp2(get_heads(q_side, row, heads) - tab_s[0, table, :]) / tab_s[1, table, :]
        d = c * (get_heads(g_side, row, heads) - tab_s[2, table, :])
        for h in range(heads):
            rows = slice(h * HD, (h + 1) * HD)
            lanes = slice(h * TEST, (h + 1) * TEST)
            moved, plain = ab_ref[b, 0, rows, :], ab_ref[b, 1, rows, :]
            acc_s[at, 0, rows, :] += c[:, lanes] * moved + d[:, lanes] * plain
            acc_s[at, 1, rows, :] += c[:, lanes] * plain
    per = tables // len(sums)
    for n, ref in enumerate(sums):
        ref[...] = acc_s[n * per : (n + 1) * per].astype(ref.dtype)


def chip_sums(meta, tabs, q_side, g_side, ab, features, dtypes):
    tables, stacked = tabs[0].shape[1:]
    count = len(tabs)
    per = tables // len(dtypes)
    return pl.pallas_call(
        lambda *refs: chip_sums_kernel(count, *refs),
        in_specs=[smem_spec()] + [vmem_spec()] * (count + 3),
        out_specs=[vmem_spec()] * len(dtypes),
        out_shape=[jax.ShapeDtypeStruct((per, 2, features, TEST), dtype) for dtype in dtypes],
        scratch_shapes=[
            pltpu.VMEM((tables, 2, features, TEST), jnp.float32),
            pltpu.VMEM((3, tables, stacked), jnp.float32),
        ],
        compiler_params=params(10),
        name="chip_sums",
    )(meta, *tabs, q_side, g_side, ab)


def query_grad_kernel(near, count, held, meta, *refs):
    chip, pieces = refs[:near], refs[near : near + count]
    count += near
    sums = refs[count : count + held]
    q_side, g_side, c_ref, d_ref, *outs, chip_s, tab_s = refs[count + held :]
    blocks, stacked = c_ref.shape
    heads = stacked // TEST
    first = q_side.shape[0] - blocks * heads
    chip_s[0], chip_s[1], chip_s[2] = merged(chip)
    tab_s[0], tab_s[1], tab_s[2] = merged(pieces)
    for n, ref in enumerate(outs):
        table = pl.ds(meta[OUT_TABLE, n], 1)
        c = jnp.exp2(chip_s[0, table, :] - tab_s[0, table, :])
        c = c * chip_s[1, table, :] / tab_s[1, table, :]
        d = c * (chip_s[2, table, :] - tab_s[2, table, :])
        parts = []
        for h in range(heads):
            rows = slice(h * HD, (h + 1) * HD)
            lanes = slice(h * TEST, (h + 1) * TEST)
            moved = sum(value[n, 0, rows, :].astype(jnp.float32) for value in sums)
            plain = sum(value[n, 1, rows, :].astype(jnp.float32) for value in sums)
            parts.append(c[:, lanes] * moved + d[:, lanes] * plain)
        ref[...] = (jnp.concatenate(parts, axis=0) * SCORE_SCALE).T.astype(ref.dtype)
    for b in range(blocks):
        table = pl.ds(meta[OWNER, b], 1)
        row = first + b * heads
        c = jnp.exp2(get_heads(q_side, row, heads) - tab_s[0, table, :]) / tab_s[1, table, :]
        c_ref[b : b + 1, :] = c
        d_ref[b : b + 1, :] = c * (get_heads(g_side, row, heads) - tab_s[2, table, :])


def query_grads(meta, chip, pieces, sums, q_side, g_side, blocks, q_dtypes):
    tables, stacked = pieces[0].shape[1:]
    features = sums[0].shape[2]
    return pl.pallas_call(
        lambda *refs: query_grad_kernel(len(chip), len(pieces), len(sums), *refs),
        in_specs=[smem_spec()] + [vmem_spec()] * (len(chip) + len(pieces) + len(sums) + 2),
        out_specs=[vmem_spec()] * (2 + len(q_dtypes)),
        out_shape=[
            jax.ShapeDtypeStruct((blocks, stacked), jnp.float32),
            jax.ShapeDtypeStruct((blocks, stacked), jnp.float32),
        ]
        + [jax.ShapeDtypeStruct((TEST, features), dtype) for dtype in q_dtypes],
        scratch_shapes=[
            pltpu.VMEM((3, tables, stacked), jnp.float32),
            pltpu.VMEM((3, tables, stacked), jnp.float32),
        ],
        compiler_params=params(10),
        name="query_grads",
    )(meta, *chip, *pieces, *sums, q_side, g_side)


def row_grads_kernel(meta, c_ref, d_ref, q_side, g_side, state, dk_hbm, dv_hbm, dk_s, dv_s, out_sem):
    blocks, _, features = dk_s.shape
    stacked = features // HD * TEST
    turned = (((1,), (1,)), ((), ()))
    stores = []
    for b in range(blocks):
        for p in range(features // LANES):
            at = slice(p * LANES, (p + 1) * LANES)
            wide = slice(p * WIDE, (p + 1) * WIDE)
            c = c_ref[b : b + 1, wide]
            d = d_ref[b : b + 1, wide]
            q_t = two_heads(q_side[rows_of(meta, b, p, features), :])
            g_t = two_heads(g_side[rows_of(meta, b, p, features), :])
            for_u = (q_t * (c * SCORE_SCALE)).astype(jnp.bfloat16)
            for_e = jnp.concatenate([g_t * c, q_t * (d * SCORE_SCALE)], axis=0).astype(jnp.bfloat16)
            from_e = lax.dot_general(
                state[b, :, wide], for_e, turned, preferred_element_type=jnp.float32
            )
            moved = state[b, :, stacked + p * WIDE : stacked + (p + 1) * WIDE]
            from_u = lax.dot_general(moved, for_u, turned, preferred_element_type=jnp.float32)
            dv_s[b, :, at] = from_e[:, :LANES].astype(jnp.bfloat16)
            dk_s[b, :, at] = (from_u + from_e[:, LANES:]).astype(jnp.bfloat16)
        rows = pl.ds(b * BLK, BLK)
        stores += every_copy(
            [
                pltpu.make_async_copy(dk_s.at[b], dk_hbm.at[rows], out_sem.at[0, b]),
                pltpu.make_async_copy(dv_s.at[b], dv_hbm.at[rows], out_sem.at[1, b]),
            ]
        )
    for copy in stores:
        copy.wait()


def row_grads(meta, c, d, sides, state, features):
    blocks = state.shape[0]
    return pl.pallas_call(
        row_grads_kernel,
        in_specs=[smem_spec()] + [vmem_spec()] * 5,
        out_specs=[hbm_spec()] * 2,
        out_shape=[jax.ShapeDtypeStruct((blocks * BLK, features), jnp.bfloat16)] * 2,
        scratch_shapes=[
            pltpu.VMEM((blocks, BLK, features), jnp.bfloat16),
            pltpu.VMEM((blocks, BLK, features), jnp.bfloat16),
            pltpu.SemaphoreType.DMA((2, blocks)),
        ],
        compiler_params=params(10),
        name="row_grads",
    )(meta, c, d, *sides, state)


def local(small, query_rows, key_rows, value_rows, cotangent, train_rows, test_rows, block_table):
    features = query_rows.shape[1]
    blocks = key_rows.shape[0] // BLK
    tables = train_rows.shape[0]
    pair = lambda value: lax.ppermute(value, "pair", PAIR)
    step = lambda value, s: lax.ppermute(value, "rows", [(z, z ^ s) for z in range(4)])
    after = lambda value, other: lax.optimization_barrier((value, other))
    index = lambda entries: index_table(
        small, entries, train_rows, test_rows, query_rows, key_rows, value_rows
    )
    if small:
        near = [step(query_rows, s) for s in (1, 2, 3)]
        near_grads = [step(cotangent, 1), step(cotangent, 2)]
        near_grads.append(step(near_grads[1], 1))
        block_table, near[1] = after(block_table, near[1])
        meta, own, state = index(block_table)
        near[0], meta = after(near[0], meta)
        queries = [own, pair(own)]
        for value in near:
            queries += [value, pair(value)]
        q_side, state = block_weights(meta, queries, state, features, tables)
        near_grads[2], q_side = after(near_grads[2], q_side)
        grads = [cotangent, pair(cotangent)]
        for value in near_grads:
            grads += [value, pair(value)]
    else:
        meta, _, state = index(block_table)
        queries = [lax.all_gather(query_rows, RP, axis=0, tiled=True)]
        q_side, state = block_weights(meta, queries, state, features, tables)
        grads = [lax.all_gather(cotangent, RP, axis=0, tiled=True)]
    g_side, tab, state = moved_weights(meta, grads, q_side, state, features, tables)
    if small:
        near = [step(tab, s) for s in (3, 2, 1)]
        own = [tab, pair(tab)]
        ab, state = query_sums(features, state)
        *near, ab = lax.optimization_barrier((*near, ab))
        keep, send = chip_sums(
            meta, own, q_side, g_side, ab, features, [jnp.float32, jnp.bfloat16]
        )
        received = pair(send)
        stats = own
        for value in near:
            stats = stats + [value, pair(value)]
        dtypes = [jnp.bfloat16] * 3 + [jnp.float32]
        c, d, *low, query_grad = query_grads(
            meta, own, stats, [keep, received], q_side, g_side, blocks, dtypes
        )
        got = [step(low[s - 1], s) for s in (3, 2, 1)]
        *low, c = lax.optimization_barrier((*low, c))
        key_grad, value_grad = row_grads(meta, c, d, (q_side, g_side), state, features)
        for value in got:
            query_grad = query_grad + value.astype(jnp.float32)
    else:
        ab, state = query_sums(features, state)
        (sums,) = chip_sums(meta, [tab], q_side, g_side, ab, features, [jnp.float32])
        peak = lax.pmax(tab[0], RP)
        weight = jnp.exp2(tab[0] - peak)
        total, part = lax.psum(jnp.stack([weight, weight * tab[1]]), RP)
        rest = jnp.stack([peak + jnp.log2(total), part / total])
        c, d, *terms = query_grads(
            meta, [tab], [rest], [sums], q_side, g_side, blocks, [jnp.float32] * tables
        )
        query_grad = lax.psum_scatter(
            jnp.concatenate(terms, axis=0), RP, scatter_dimension=0, tiled=True
        )
        key_grad, value_grad = row_grads(meta, c, d, (q_side, g_side), state, features)
    return query_grad.astype(jnp.bfloat16), key_grad, value_grad


def solution(mesh):
    sizes = mesh.shape
    tables_of_rows = P(("groups", "rows", "pair"), "mp")
    in_specs = (tables_of_rows,) * 4 + (P("groups"),) * 3
    out_specs = (tables_of_rows,) * 3

    def run(query_rows, *rest):
        local_rows = query_rows.shape[0] // (sizes["groups"] * sizes["rows"] * sizes["pair"])
        small = sizes["rows"] == 4 and sizes["pair"] == 2 and local_rows == TEST
        return jax.shard_map(
            lambda *args: local(small, *args),
            mesh=mesh,
            in_specs=in_specs,
            out_specs=out_specs,
            check_vma=False,
        )(query_rows, *rest)

    return run
```

```python
import math

import jax
import jax.numpy as jnp
from jax import lax
from jax.experimental import pallas as pl
from jax.experimental.pallas import tpu as pltpu
from jax.sharding import PartitionSpec as P

HD = 64
TEST = 128
BLK = 512
LANES = 128
WIDE = 2 * TEST
CHUNK = 64

NEG = -1e30
SCORE_SCALE = 1.0 / math.sqrt(HD)
LOG2_SCALE = SCORE_SCALE * math.log2(math.e)
RP = ("rows", "pair")
PAIR = [(0, 1), (1, 0)]


def params(mib):
    return pltpu.CompilerParams(vmem_limit_bytes=mib * 1024 * 1024)


def two_heads(rows):
    feature = lax.broadcasted_iota(jnp.int32, rows.shape, 0)
    zero = jnp.zeros_like(rows)
    return jnp.concatenate(
        [jnp.where(feature < HD, rows, zero), jnp.where(feature < HD, zero, rows)], axis=1
    )


def every_copy(copies):
    for copy in copies:
        copy.start()
    return copies


OWNER, LIVE, TESTN, SLOT_IN, TABLE_OF, SLOT_OUT, OUT_TABLE = range(7)


def vmem_spec():
    return pl.BlockSpec(memory_space=pltpu.VMEM)


def smem_spec():
    return pl.BlockSpec(memory_space=pltpu.SMEM)


def hbm_spec():
    return pl.BlockSpec(memory_space=pltpu.HBM)


def in_hbm(value):
    return pltpu.with_memory_space_constraint(value, pltpu.HBM)


def index_kernel(small, table_hbm, train_hbm, test_hbm, *refs):
    query_hbm, key_hbm, value_hbm, meta, query_ref, state = refs[:6]
    block_table, train_rows, test_rows, count, small_sem, sem = refs[6:]
    blocks = state.shape[0]
    features = key_hbm.shape[1]
    stacked = features // HD * TEST
    entries = every_copy(
        [
            pltpu.make_async_copy(table_hbm, block_table, small_sem.at[0]),
            pltpu.make_async_copy(train_hbm, train_rows, small_sem.at[1]),
            pltpu.make_async_copy(test_hbm, test_rows, small_sem.at[2]),
        ]
    )
    loads = [pltpu.make_async_copy(query_hbm, query_ref, small_sem.at[3])]
    for n, source in enumerate((key_hbm, value_hbm)):
        lanes = pl.ds(2 * stacked + n * features, features)
        for b in range(blocks):
            rows = pl.ds(b * BLK, BLK)
            loads.append(
                pltpu.make_async_copy(source.at[rows], state.at[b, :, lanes], sem.at[n, b])
            )
    every_copy(loads)
    chip = lax.axis_index("rows").astype(jnp.int32)
    core = lax.axis_index("pair").astype(jnp.int32)
    first = lax.axis_index(RP).astype(jnp.int32) * blocks
    for copy in entries:
        copy.wait()
    for t in range(train_rows.shape[0]):
        count[t] = 0
        meta[TESTN, t] = test_rows[t]
        if small:
            away = (t // 2) ^ chip
            not_mine = (t % 2) ^ core
            meta[SLOT_IN, t] = 2 * away + not_mine
            meta[TABLE_OF, t] = 2 * away + not_mine
            meta[SLOT_OUT, t] = 4 * not_mine + ((away + 3) & 3)
            meta[OUT_TABLE, 4 * not_mine + ((away + 3) & 3)] = t
        else:
            for row in (SLOT_IN, TABLE_OF, SLOT_OUT, OUT_TABLE):
                meta[row, t] = t

    def earlier(n, carry):
        table = block_table[n]
        count[table] = count[table] + 1
        return carry

    lax.fori_loop(0, first, earlier, 0)
    for b in range(blocks):
        table = block_table[first + b]
        meta[OWNER, b] = table
        meta[LIVE, b] = jnp.minimum(train_rows[table] - count[table] * BLK, BLK)
        count[table] = count[table] + 1
    for copy in loads:
        copy.wait()


def index_table(small, block_table, train_rows, test_rows, query_rows, key_rows, value_rows):
    tables = train_rows.shape[0]
    features = key_rows.shape[1]
    blocks = key_rows.shape[0] // BLK
    stacked = features // HD * TEST
    arrays = (block_table, train_rows, test_rows, query_rows, key_rows, value_rows)
    return pl.pallas_call(
        lambda *refs: index_kernel(small, *refs),
        in_specs=[hbm_spec()] * 6,
        out_specs=[smem_spec(), vmem_spec(), vmem_spec()],
        out_shape=[
            pltpu.SMEM((7, max(blocks, tables)), jnp.int32),
            pltpu.VMEM(query_rows.shape, query_rows.dtype),
            pltpu.VMEM((blocks, BLK, 2 * stacked + 2 * features), jnp.bfloat16),
        ],
        scratch_shapes=[
            pltpu.SMEM(block_table.shape, jnp.int32),
            pltpu.SMEM((tables,), jnp.int32),
            pltpu.SMEM((tables,), jnp.int32),
            pltpu.SMEM((tables,), jnp.int32),
            pltpu.SemaphoreType.DMA((4,)),
            pltpu.SemaphoreType.DMA((2, blocks)),
        ],
        compiler_params=params(4),
        name="index_table",
    )(*map(in_hbm, arrays))


def turn_pieces(pieces, store):
    at_slot = 0
    for piece in pieces:
        for m in range(piece.shape[0] // TEST):
            store(at_slot, piece[m * TEST : (m + 1) * TEST, :].T)
            at_slot += 1


def fold(values, op):
    return op(values.reshape(CHUNK // 8, 8, WIDE), axis=0)


def rows_of(meta, b, p, features):
    at_slot = meta[SLOT_IN, meta[OWNER, b]]
    return pl.ds(pl.multiple_of(at_slot * features + p * LANES, LANES), LANES)


def put_heads(side, first, b, p, features, row):
    at = first + b * features // HD + 2 * p
    side[at : at + 1, :] = row[:, :TEST]
    side[at + 1 : at + 2, :] = row[:, TEST:]


def get_heads(side, row, heads):
    return jnp.concatenate([side[row + h : row + h + 1, :] for h in range(heads)], axis=1)


def units_of(blocks, features):
    return [(b, p) for b in range(blocks) for p in range(features // LANES)]


def weights_kernel(count, features, meta, *refs):
    pieces = refs[:count]
    state, side, state_out, scores_s = refs[count:]
    blocks = state.shape[0]
    stacked = features // HD * TEST
    first_peak = side.shape[0] - blocks * features // HD
    units = units_of(blocks, features)

    def store(at_slot, turned):
        side[at_slot * features : (at_slot + 1) * features, :] = turned.astype(jnp.float32)

    turn_pieces(pieces, store)
    peaks = [None] * len(units)
    for t in range(len(units) + 1):
        if t < len(units):
            b, p = units[t]
            live = meta[LIVE, b]
            queries = two_heads(side[rows_of(meta, b, p, features), :]).astype(jnp.bfloat16)
            peak = jnp.full((8, WIDE), NEG, jnp.float32)
        for r in range(0, BLK, CHUNK):
            rows = slice(r, r + CHUNK)
            if t > 0:
                last_b, last_p = units[t - 1]
                weights = jnp.exp2(scores_s[(t - 1) % 2, rows, :] * LOG2_SCALE - peaks[t - 1])
                state_out[last_b, rows, last_p * WIDE : (last_p + 1) * WIDE] = weights.astype(
                    jnp.bfloat16
                )
            if t < len(units):
                keys = state[b, rows, 2 * stacked + p * LANES : 2 * stacked + (p + 1) * LANES]
                scores = jnp.dot(keys, queries, preferred_element_type=jnp.float32)
                row = lax.broadcasted_iota(jnp.int32, scores.shape, 0)
                scores = jnp.where(row < live - r, scores, NEG)
                scores_s[t % 2, rows, :] = scores
                peak = jnp.maximum(peak, fold(scores, jnp.max))
        if t < len(units):
            peaks[t] = jnp.max(peak, axis=0, keepdims=True) * LOG2_SCALE
    for (b, p), peak in zip(units, peaks):
        put_heads(side, first_peak, b, p, features, peak)


def block_weights(meta, pieces, state, features, tables):
    blocks = state.shape[0]
    count = len(pieces)
    return pl.pallas_call(
        lambda *refs: weights_kernel(count, features, *refs),
        in_specs=[smem_spec()] + [vmem_spec()] * (count + 1),
        out_specs=[vmem_spec()] * 2,
        out_shape=[
            pltpu.VMEM((tables * features + blocks * features // HD, TEST), jnp.float32),
            pltpu.VMEM(state.shape, jnp.bfloat16),
        ],
        input_output_aliases={count + 1: 1},
        scratch_shapes=[pltpu.VMEM((2, BLK, WIDE), jnp.float32)],
        compiler_params=params(10),
        name="block_weights",
    )(meta, *pieces, state)


def moved_kernel(count, features, meta, *refs):
    pieces = refs[:count]
    q_side, state, side, tab_ref, state_out = refs[count : count + 5]
    dprobs_s = refs[count + 5]
    tables = tab_ref.shape[1]
    stacked = features // HD * TEST
    blocks = state.shape[0]
    heads = features // HD
    first = tables * features
    units = units_of(blocks, features)
    query = lax.broadcasted_iota(jnp.int32, (features, TEST), 1)

    def store(at_slot, turned):
        live = query < meta[TESTN, meta[TABLE_OF, at_slot]]
        turned = jnp.where(live, turned, jnp.zeros_like(turned)).astype(jnp.float32)
        side[at_slot * features : (at_slot + 1) * features, :] = turned

    turn_pieces(pieces, store)
    means, masses = [None] * len(units), [None] * len(units)
    zero = jnp.zeros((8, WIDE), jnp.float32)
    for t in range(len(units) + 1):
        if t < len(units):
            b, p = units[t]
            grads = two_heads(side[rows_of(meta, b, p, features), :]).astype(jnp.bfloat16)
            mass = part = zero
        for r in range(0, BLK, CHUNK):
            rows = slice(r, r + CHUNK)
            if t > 0:
                last_b, last_p = units[t - 1]
                weights = state[last_b, rows, last_p * WIDE : (last_p + 1) * WIDE]
                moved = weights.astype(jnp.float32) * (dprobs_s[(t - 1) % 2, rows, :] - means[t - 1])
                lanes = slice(stacked + last_p * WIDE, stacked + (last_p + 1) * WIDE)
                state_out[last_b, rows, lanes] = moved.astype(jnp.bfloat16)
            if t < len(units):
                lane = 2 * stacked + features + p * LANES
                values = state[b, rows, lane : lane + LANES]
                dprobs = jnp.dot(values, grads, preferred_element_type=jnp.float32)
                weights = state[b, rows, p * WIDE : (p + 1) * WIDE].astype(jnp.float32)
                mass = mass + fold(weights, jnp.sum)
                part = part + fold(weights * dprobs, jnp.sum)
                dprobs_s[t % 2, rows, :] = dprobs
        if t < len(units):
            mass = jnp.sum(mass, axis=0, keepdims=True)
            masses[t] = mass
            means[t] = jnp.sum(part, axis=0, keepdims=True) / mass
    for (b, p), mean, mass in zip(units, means, masses):
        put_heads(side, first, b, p, features, mean)
        put_heads(side, first + blocks * heads, b, p, features, mass)
    table = lax.broadcasted_iota(jnp.int32, (tables, stacked), 0)
    peak = jnp.full((tables, stacked), NEG, jnp.float32)
    for b in range(blocks):
        own = table == meta[OWNER, b]
        block_peak = get_heads(q_side, first + b * heads, heads)
        peak = jnp.where(own, jnp.maximum(peak, block_peak), peak)
    total = part = jnp.zeros((tables, stacked), jnp.float32)
    for b in range(blocks):
        own = table == meta[OWNER, b]
        at = b * (features // LANES)
        mass = jnp.concatenate(masses[at : at + features // LANES], axis=1)
        mean = jnp.concatenate(means[at : at + features // LANES], axis=1)
        block_peak = get_heads(q_side, first + b * heads, heads)
        scaled = jnp.where(own, jnp.exp2(block_peak - peak) * mass, 0.0)
        total = total + scaled
        part = part + scaled * mean
    here = total > 0.0
    mass = jnp.where(here, total, 1.0)
    tab_ref[0] = jnp.where(here, peak + jnp.log2(mass), NEG)
    tab_ref[1] = part / mass


def moved_weights(meta, pieces, q_side, state, features, tables):
    blocks = state.shape[0]
    stacked = features // HD * TEST
    count = len(pieces)
    return pl.pallas_call(
        lambda *refs: moved_kernel(count, features, *refs),
        in_specs=[smem_spec()] + [vmem_spec()] * (count + 2),
        out_specs=[vmem_spec()] * 3,
        out_shape=[
            pltpu.VMEM((tables * features + 2 * blocks * features // HD, TEST), jnp.float32),
            jax.ShapeDtypeStruct((2, tables, stacked), jnp.float32),
            pltpu.VMEM(state.shape, jnp.bfloat16),
        ],
        input_output_aliases={count + 2: 2},
        scratch_shapes=[pltpu.VMEM((2, BLK, WIDE), jnp.float32)],
        compiler_params=params(10),
        name="moved_weights",
    )(meta, *pieces, q_side, state)


def merged(pieces):
    peak = pieces[0][0]
    for piece in pieces[1:]:
        peak = jnp.maximum(peak, piece[0])
    mass = part = 0.0
    for piece in pieces:
        weight = jnp.exp2(piece[0] - peak)
        mass = mass + weight
        part = part + piece[1] * weight
    return peak, mass, part / mass


def query_sums_kernel(state, ab_ref, state_out):
    blocks, _, features, _ = ab_ref.shape
    stacked = features // HD * TEST
    for b in range(blocks):
        for p in range(features // LANES):
            keys = state[b, :, 2 * stacked + p * LANES : 2 * stacked + (p + 1) * LANES]
            for n, first in enumerate((stacked, 0)):
                values = state[b, :, first + p * WIDE : first + (p + 1) * WIDE]
                product = lax.dot_general(
                    keys, values, (((0,), (0,)), ((), ())), preferred_element_type=jnp.float32
                )
                ab_ref[b, n, p * LANES : p * LANES + HD, :] = product[:HD, :TEST]
                ab_ref[b, n, p * LANES + HD : (p + 1) * LANES, :] = product[HD:, TEST:]


def query_sums(features, state):
    blocks = state.shape[0]
    return pl.pallas_call(
        query_sums_kernel,
        in_specs=[vmem_spec()],
        out_specs=[vmem_spec()] * 2,
        out_shape=[
            pltpu.VMEM((blocks, 2, features, TEST), jnp.float32),
            pltpu.VMEM(state.shape, jnp.bfloat16),
        ],
        input_output_aliases={0: 1},
        compiler_params=params(8),
        name="query_sums",
    )(state)


def chip_sums_kernel(count, meta, *refs):
    tabs = refs[:count]
    q_side, g_side, ab_ref, *sums, acc_s, tab_s = refs[count:]
    tables, _, features, _ = acc_s.shape
    blocks = ab_ref.shape[0]
    heads = features // HD
    tab_s[0], tab_s[1], tab_s[2] = merged(tabs)
    acc_s[...] = jnp.zeros_like(acc_s)
    for b in range(blocks):
        at = meta[SLOT_OUT, meta[OWNER, b]]
        table = pl.ds(meta[OWNER, b], 1)
        row = tables * features + b * heads
        c = jnp.exp2(get_heads(q_side, row, heads) - tab_s[0, table, :]) / tab_s[1, table, :]
        d = c * (get_heads(g_side, row, heads) - tab_s[2, table, :])
        for h in range(heads):
            rows = slice(h * HD, (h + 1) * HD)
            lanes = slice(h * TEST, (h + 1) * TEST)
            moved, plain = ab_ref[b, 0, rows, :], ab_ref[b, 1, rows, :]
            acc_s[at, 0, rows, :] += c[:, lanes] * moved + d[:, lanes] * plain
            acc_s[at, 1, rows, :] += c[:, lanes] * plain
    per = tables // len(sums)
    for n, ref in enumerate(sums):
        ref[...] = acc_s[n * per : (n + 1) * per].astype(ref.dtype)


def chip_sums(meta, tabs, q_side, g_side, ab, features, dtypes):
    tables, stacked = tabs[0].shape[1:]
    count = len(tabs)
    per = tables // len(dtypes)
    return pl.pallas_call(
        lambda *refs: chip_sums_kernel(count, *refs),
        in_specs=[smem_spec()] + [vmem_spec()] * (count + 3),
        out_specs=[vmem_spec()] * len(dtypes),
        out_shape=[jax.ShapeDtypeStruct((per, 2, features, TEST), dtype) for dtype in dtypes],
        scratch_shapes=[
            pltpu.VMEM((tables, 2, features, TEST), jnp.float32),
            pltpu.VMEM((3, tables, stacked), jnp.float32),
        ],
        compiler_params=params(10),
        name="chip_sums",
    )(meta, *tabs, q_side, g_side, ab)


def query_grad_kernel(near, count, held, meta, *refs):
    chip, pieces = refs[:near], refs[near : near + count]
    count += near
    sums = refs[count : count + held]
    q_side, g_side, c_ref, d_ref, *outs, chip_s, tab_s = refs[count + held :]
    blocks, stacked = c_ref.shape
    heads = stacked // TEST
    first = q_side.shape[0] - blocks * heads
    chip_s[0], chip_s[1], chip_s[2] = merged(chip)
    tab_s[0], tab_s[1], tab_s[2] = merged(pieces)
    for n, ref in enumerate(outs):
        table = pl.ds(meta[OUT_TABLE, n], 1)
        c = jnp.exp2(chip_s[0, table, :] - tab_s[0, table, :])
        c = c * chip_s[1, table, :] / tab_s[1, table, :]
        d = c * (chip_s[2, table, :] - tab_s[2, table, :])
        parts = []
        for h in range(heads):
            rows = slice(h * HD, (h + 1) * HD)
            lanes = slice(h * TEST, (h + 1) * TEST)
            moved = sum(value[n, 0, rows, :].astype(jnp.float32) for value in sums)
            plain = sum(value[n, 1, rows, :].astype(jnp.float32) for value in sums)
            parts.append(c[:, lanes] * moved + d[:, lanes] * plain)
        ref[...] = (jnp.concatenate(parts, axis=0) * SCORE_SCALE).T.astype(ref.dtype)
    for b in range(blocks):
        table = pl.ds(meta[OWNER, b], 1)
        row = first + b * heads
        c = jnp.exp2(get_heads(q_side, row, heads) - tab_s[0, table, :]) / tab_s[1, table, :]
        c_ref[b : b + 1, :] = c
        d_ref[b : b + 1, :] = c * (get_heads(g_side, row, heads) - tab_s[2, table, :])


def query_grads(meta, chip, pieces, sums, q_side, g_side, blocks, q_dtypes):
    tables, stacked = pieces[0].shape[1:]
    features = sums[0].shape[2]
    return pl.pallas_call(
        lambda *refs: query_grad_kernel(len(chip), len(pieces), len(sums), *refs),
        in_specs=[smem_spec()] + [vmem_spec()] * (len(chip) + len(pieces) + len(sums) + 2),
        out_specs=[vmem_spec()] * (2 + len(q_dtypes)),
        out_shape=[
            jax.ShapeDtypeStruct((blocks, stacked), jnp.float32),
            jax.ShapeDtypeStruct((blocks, stacked), jnp.float32),
        ]
        + [jax.ShapeDtypeStruct((TEST, features), dtype) for dtype in q_dtypes],
        scratch_shapes=[
            pltpu.VMEM((3, tables, stacked), jnp.float32),
            pltpu.VMEM((3, tables, stacked), jnp.float32),
        ],
        compiler_params=params(10),
        name="query_grads",
    )(meta, *chip, *pieces, *sums, q_side, g_side)


def row_grads_kernel(meta, c_ref, d_ref, q_side, g_side, state, dk_hbm, dv_hbm, dk_s, dv_s, out_sem):
    blocks, _, features = dk_s.shape
    stacked = features // HD * TEST
    turned = (((1,), (1,)), ((), ()))
    stores = []
    for b in range(blocks):
        for p in range(features // LANES):
            at = slice(p * LANES, (p + 1) * LANES)
            wide = slice(p * WIDE, (p + 1) * WIDE)
            c = c_ref[b : b + 1, wide]
            d = d_ref[b : b + 1, wide]
            q_t = two_heads(q_side[rows_of(meta, b, p, features), :])
            g_t = two_heads(g_side[rows_of(meta, b, p, features), :])
            for_u = (q_t * (c * SCORE_SCALE)).astype(jnp.bfloat16)
            for_e = jnp.concatenate([g_t * c, q_t * (d * SCORE_SCALE)], axis=0).astype(jnp.bfloat16)
            from_e = lax.dot_general(
                state[b, :, wide], for_e, turned, preferred_element_type=jnp.float32
            )
            moved = state[b, :, stacked + p * WIDE : stacked + (p + 1) * WIDE]
            from_u = lax.dot_general(moved, for_u, turned, preferred_element_type=jnp.float32)
            dv_s[b, :, at] = from_e[:, :LANES].astype(jnp.bfloat16)
            dk_s[b, :, at] = (from_u + from_e[:, LANES:]).astype(jnp.bfloat16)
        rows = pl.ds(b * BLK, BLK)
        stores += every_copy(
            [
                pltpu.make_async_copy(dk_s.at[b], dk_hbm.at[rows], out_sem.at[0, b]),
                pltpu.make_async_copy(dv_s.at[b], dv_hbm.at[rows], out_sem.at[1, b]),
            ]
        )
    for copy in stores:
        copy.wait()


def row_grads(meta, c, d, sides, state, features):
    blocks = state.shape[0]
    return pl.pallas_call(
        row_grads_kernel,
        in_specs=[smem_spec()] + [vmem_spec()] * 5,
        out_specs=[hbm_spec()] * 2,
        out_shape=[jax.ShapeDtypeStruct((blocks * BLK, features), jnp.bfloat16)] * 2,
        scratch_shapes=[
            pltpu.VMEM((blocks, BLK, features), jnp.bfloat16),
            pltpu.VMEM((blocks, BLK, features), jnp.bfloat16),
            pltpu.SemaphoreType.DMA((2, blocks)),
        ],
        compiler_params=params(10),
        name="row_grads",
    )(meta, c, d, *sides, state)


def local(small, query_rows, key_rows, value_rows, cotangent, train_rows, test_rows, block_table):
    features = query_rows.shape[1]
    blocks = key_rows.shape[0] // BLK
    tables = train_rows.shape[0]
    pair = lambda value: lax.ppermute(value, "pair", PAIR)
    step = lambda value, s: lax.ppermute(value, "rows", [(z, z ^ s) for z in range(4)])
    after = lambda value, other: lax.optimization_barrier((value, other))
    index = lambda entries: index_table(
        small, entries, train_rows, test_rows, query_rows, key_rows, value_rows
    )
    if small:
        near = [step(query_rows, s) for s in (1, 2, 3)]
        near_grads = [step(cotangent, 1), step(cotangent, 2)]
        near_grads.append(step(near_grads[1], 1))
        block_table, near[1] = after(block_table, near[1])
        meta, own, state = index(block_table)
        near[0], meta = after(near[0], meta)
        queries = [own, pair(own)]
        for value in near:
            queries += [value, pair(value)]
        q_side, state = block_weights(meta, queries, state, features, tables)
        near_grads[2], q_side = after(near_grads[2], q_side)
        grads = [cotangent, pair(cotangent)]
        for value in near_grads:
            grads += [value, pair(value)]
    else:
        meta, _, state = index(block_table)
        queries = [lax.all_gather(query_rows, RP, axis=0, tiled=True)]
        q_side, state = block_weights(meta, queries, state, features, tables)
        grads = [lax.all_gather(cotangent, RP, axis=0, tiled=True)]
    g_side, tab, state = moved_weights(meta, grads, q_side, state, features, tables)
    if small:
        near = [step(tab, s) for s in (2, 3, 1)]
        own = [tab, pair(tab)]
        ab, state = query_sums(features, state)
        *near, ab = lax.optimization_barrier((*near, ab))
        keep, send = chip_sums(
            meta, own, q_side, g_side, ab, features, [jnp.float32, jnp.bfloat16]
        )
        received = pair(send)
        stats = own
        for value in near:
            stats = stats + [value, pair(value)]
        dtypes = [jnp.bfloat16] * 3 + [jnp.float32]
        c, d, *low, query_grad = query_grads(
            meta, own, stats, [keep, received], q_side, g_side, blocks, dtypes
        )
        got = [step(low[s - 1], s) for s in (2, 3, 1)]
        *low, c = lax.optimization_barrier((*low, c))
        key_grad, value_grad = row_grads(meta, c, d, (q_side, g_side), state, features)
        for value in got:
            query_grad = query_grad + value.astype(jnp.float32)
    else:
        ab, state = query_sums(features, state)
        (sums,) = chip_sums(meta, [tab], q_side, g_side, ab, features, [jnp.float32])
        peak = lax.pmax(tab[0], RP)
        weight = jnp.exp2(tab[0] - peak)
        total, part = lax.psum(jnp.stack([weight, weight * tab[1]]), RP)
        rest = jnp.stack([peak + jnp.log2(total), part / total])
        c, d, *terms = query_grads(
            meta, [tab], [rest], [sums], q_side, g_side, blocks, [jnp.float32] * tables
        )
        query_grad = lax.psum_scatter(
            jnp.concatenate(terms, axis=0), RP, scatter_dimension=0, tiled=True
        )
        key_grad, value_grad = row_grads(meta, c, d, (q_side, g_side), state, features)
    return query_grad.astype(jnp.bfloat16), key_grad, value_grad


def solution(mesh):
    sizes = mesh.shape
    tables_of_rows = P(("groups", "rows", "pair"), "mp")
    in_specs = (tables_of_rows,) * 4 + (P("groups"),) * 3
    out_specs = (tables_of_rows,) * 3

    def run(query_rows, *rest):
        local_rows = query_rows.shape[0] // (sizes["groups"] * sizes["rows"] * sizes["pair"])
        small = sizes["rows"] == 4 and sizes["pair"] == 2 and local_rows == TEST
        return jax.shard_map(
            lambda *args: local(small, *args),
            mesh=mesh,
            in_specs=in_specs,
            out_specs=out_specs,
            check_vma=False,
        )(query_rows, *rest)

    return run
```

```python
import math

import jax
import jax.numpy as jnp
from jax import lax
from jax.experimental import pallas as pl
from jax.experimental.pallas import tpu as pltpu
from jax.sharding import PartitionSpec as P

HD = 64
TEST = 128
BLK = 512
LANES = 128
WIDE = 2 * TEST
CHUNK = 64

NEG = -1e30
SCORE_SCALE = 1.0 / math.sqrt(HD)
LOG2_SCALE = SCORE_SCALE * math.log2(math.e)
RP = ("rows", "pair")
PAIR = [(0, 1), (1, 0)]


def params(mib):
    return pltpu.CompilerParams(vmem_limit_bytes=mib * 1024 * 1024)


def two_heads(rows):
    feature = lax.broadcasted_iota(jnp.int32, rows.shape, 0)
    zero = jnp.zeros_like(rows)
    return jnp.concatenate(
        [jnp.where(feature < HD, rows, zero), jnp.where(feature < HD, zero, rows)], axis=1
    )


def every_copy(copies):
    for copy in copies:
        copy.start()
    return copies


OWNER, LIVE, TESTN, SLOT_IN, TABLE_OF, SLOT_OUT, OUT_TABLE = range(7)


def vmem_spec():
    return pl.BlockSpec(memory_space=pltpu.VMEM)


def smem_spec():
    return pl.BlockSpec(memory_space=pltpu.SMEM)


def hbm_spec():
    return pl.BlockSpec(memory_space=pltpu.HBM)


def in_hbm(value):
    return pltpu.with_memory_space_constraint(value, pltpu.HBM)


def index_kernel(small, table_hbm, train_hbm, test_hbm, *refs):
    query_hbm, key_hbm, value_hbm, meta, query_ref, state = refs[:6]
    block_table, train_rows, test_rows, count, small_sem, sem = refs[6:]
    blocks = state.shape[0]
    features = key_hbm.shape[1]
    stacked = features // HD * TEST
    entries = every_copy(
        [
            pltpu.make_async_copy(table_hbm, block_table, small_sem.at[0]),
            pltpu.make_async_copy(train_hbm, train_rows, small_sem.at[1]),
            pltpu.make_async_copy(test_hbm, test_rows, small_sem.at[2]),
        ]
    )
    loads = [pltpu.make_async_copy(query_hbm, query_ref, small_sem.at[3])]
    for n, source in enumerate((key_hbm, value_hbm)):
        lanes = pl.ds(2 * stacked + n * features, features)
        for b in range(blocks):
            rows = pl.ds(b * BLK, BLK)
            loads.append(
                pltpu.make_async_copy(source.at[rows], state.at[b, :, lanes], sem.at[n, b])
            )
    every_copy(loads)
    chip = lax.axis_index("rows").astype(jnp.int32)
    core = lax.axis_index("pair").astype(jnp.int32)
    first = lax.axis_index(RP).astype(jnp.int32) * blocks
    for copy in entries:
        copy.wait()
    for t in range(train_rows.shape[0]):
        count[t] = 0
        meta[TESTN, t] = test_rows[t]
        if small:
            away = (t // 2) ^ chip
            not_mine = (t % 2) ^ core
            meta[SLOT_IN, t] = 2 * away + not_mine
            meta[TABLE_OF, t] = 2 * away + not_mine
            meta[SLOT_OUT, t] = 4 * not_mine + ((away + 3) & 3)
            meta[OUT_TABLE, 4 * not_mine + ((away + 3) & 3)] = t
        else:
            for row in (SLOT_IN, TABLE_OF, SLOT_OUT, OUT_TABLE):
                meta[row, t] = t

    def earlier(n, carry):
        table = block_table[n]
        count[table] = count[table] + 1
        return carry

    lax.fori_loop(0, first, earlier, 0)
    for b in range(blocks):
        table = block_table[first + b]
        meta[OWNER, b] = table
        meta[LIVE, b] = jnp.minimum(train_rows[table] - count[table] * BLK, BLK)
        count[table] = count[table] + 1
    for copy in loads:
        copy.wait()


def index_table(small, block_table, train_rows, test_rows, query_rows, key_rows, value_rows):
    tables = train_rows.shape[0]
    features = key_rows.shape[1]
    blocks = key_rows.shape[0] // BLK
    stacked = features // HD * TEST
    arrays = (block_table, train_rows, test_rows, query_rows, key_rows, value_rows)
    return pl.pallas_call(
        lambda *refs: index_kernel(small, *refs),
        in_specs=[hbm_spec()] * 6,
        out_specs=[smem_spec(), vmem_spec(), vmem_spec()],
        out_shape=[
            pltpu.SMEM((7, max(blocks, tables)), jnp.int32),
            pltpu.VMEM(query_rows.shape, query_rows.dtype),
            pltpu.VMEM((blocks, BLK, 2 * stacked + 2 * features), jnp.bfloat16),
        ],
        scratch_shapes=[
            pltpu.SMEM(block_table.shape, jnp.int32),
            pltpu.SMEM((tables,), jnp.int32),
            pltpu.SMEM((tables,), jnp.int32),
            pltpu.SMEM((tables,), jnp.int32),
            pltpu.SemaphoreType.DMA((4,)),
            pltpu.SemaphoreType.DMA((2, blocks)),
        ],
        compiler_params=params(4),
        name="index_table",
    )(*map(in_hbm, arrays))


def turn_pieces(pieces, store):
    at_slot = 0
    for piece in pieces:
        for m in range(piece.shape[0] // TEST):
            store(at_slot, piece[m * TEST : (m + 1) * TEST, :].T)
            at_slot += 1


def fold(values, op):
    return op(values.reshape(CHUNK // 8, 8, WIDE), axis=0)


def rows_of(meta, b, p, features):
    at_slot = meta[SLOT_IN, meta[OWNER, b]]
    return pl.ds(pl.multiple_of(at_slot * features + p * LANES, LANES), LANES)


def put_heads(side, first, b, p, features, row):
    at = first + b * features // HD + 2 * p
    side[at : at + 1, :] = row[:, :TEST]
    side[at + 1 : at + 2, :] = row[:, TEST:]


def get_heads(side, row, heads):
    return jnp.concatenate([side[row + h : row + h + 1, :] for h in range(heads)], axis=1)


def units_of(blocks, features):
    return [(b, p) for b in range(blocks) for p in range(features // LANES)]


def weights_kernel(count, features, meta, *refs):
    pieces = refs[:count]
    state, side, state_out, scores_s = refs[count:]
    blocks = state.shape[0]
    stacked = features // HD * TEST
    first_peak = side.shape[0] - blocks * features // HD
    units = units_of(blocks, features)

    def store(at_slot, turned):
        side[at_slot * features : (at_slot + 1) * features, :] = turned.astype(jnp.float32)

    turn_pieces(pieces, store)
    peaks = [None] * len(units)
    for t in range(len(units) + 1):
        if t < len(units):
            b, p = units[t]
            live = meta[LIVE, b]
            queries = two_heads(side[rows_of(meta, b, p, features), :]).astype(jnp.bfloat16)
            peak = jnp.full((8, WIDE), NEG, jnp.float32)
        for r in range(0, BLK, CHUNK):
            rows = slice(r, r + CHUNK)
            if t > 0:
                last_b, last_p = units[t - 1]
                weights = jnp.exp2(scores_s[(t - 1) % 2, rows, :] * LOG2_SCALE - peaks[t - 1])
                state_out[last_b, rows, last_p * WIDE : (last_p + 1) * WIDE] = weights.astype(
                    jnp.bfloat16
                )
            if t < len(units):
                keys = state[b, rows, 2 * stacked + p * LANES : 2 * stacked + (p + 1) * LANES]
                scores = jnp.dot(keys, queries, preferred_element_type=jnp.float32)
                row = lax.broadcasted_iota(jnp.int32, scores.shape, 0)
                scores = jnp.where(row < live - r, scores, NEG)
                scores_s[t % 2, rows, :] = scores
                peak = jnp.maximum(peak, fold(scores, jnp.max))
        if t < len(units):
            peaks[t] = jnp.max(peak, axis=0, keepdims=True) * LOG2_SCALE
    for (b, p), peak in zip(units, peaks):
        put_heads(side, first_peak, b, p, features, peak)


def block_weights(meta, pieces, state, features, tables):
    blocks = state.shape[0]
    count = len(pieces)
    return pl.pallas_call(
        lambda *refs: weights_kernel(count, features, *refs),
        in_specs=[smem_spec()] + [vmem_spec()] * (count + 1),
        out_specs=[vmem_spec()] * 2,
        out_shape=[
            pltpu.VMEM((tables * features + blocks * features // HD, TEST), jnp.float32),
            pltpu.VMEM(state.shape, jnp.bfloat16),
        ],
        input_output_aliases={count + 1: 1},
        scratch_shapes=[pltpu.VMEM((2, BLK, WIDE), jnp.float32)],
        compiler_params=params(10),
        name="block_weights",
    )(meta, *pieces, state)


def moved_kernel(count, features, meta, *refs):
    pieces = refs[:count]
    q_side, state, side, tab_ref, state_out = refs[count : count + 5]
    dprobs_s = refs[count + 5]
    tables = tab_ref.shape[1]
    stacked = features // HD * TEST
    blocks = state.shape[0]
    heads = features // HD
    first = tables * features
    units = units_of(blocks, features)
    query = lax.broadcasted_iota(jnp.int32, (features, TEST), 1)

    def store(at_slot, turned):
        live = query < meta[TESTN, meta[TABLE_OF, at_slot]]
        turned = jnp.where(live, turned, jnp.zeros_like(turned)).astype(jnp.float32)
        side[at_slot * features : (at_slot + 1) * features, :] = turned

    turn_pieces(pieces, store)
    means, masses = [None] * len(units), [None] * len(units)
    zero = jnp.zeros((8, WIDE), jnp.float32)
    for t in range(len(units) + 1):
        if t < len(units):
            b, p = units[t]
            grads = two_heads(side[rows_of(meta, b, p, features), :]).astype(jnp.bfloat16)
            mass = part = zero
        for r in range(0, BLK, CHUNK):
            rows = slice(r, r + CHUNK)
            if t > 0:
                last_b, last_p = units[t - 1]
                weights = state[last_b, rows, last_p * WIDE : (last_p + 1) * WIDE]
                moved = weights.astype(jnp.float32) * (dprobs_s[(t - 1) % 2, rows, :] - means[t - 1])
                lanes = slice(stacked + last_p * WIDE, stacked + (last_p + 1) * WIDE)
                state_out[last_b, rows, lanes] = moved.astype(jnp.bfloat16)
            if t < len(units):
                lane = 2 * stacked + features + p * LANES
                values = state[b, rows, lane : lane + LANES]
                dprobs = jnp.dot(values, grads, preferred_element_type=jnp.float32)
                weights = state[b, rows, p * WIDE : (p + 1) * WIDE].astype(jnp.float32)
                mass = mass + fold(weights, jnp.sum)
                part = part + fold(weights * dprobs, jnp.sum)
                dprobs_s[t % 2, rows, :] = dprobs
        if t < len(units):
            mass = jnp.sum(mass, axis=0, keepdims=True)
            masses[t] = mass
            means[t] = jnp.sum(part, axis=0, keepdims=True) / mass
    for (b, p), mean, mass in zip(units, means, masses):
        put_heads(side, first, b, p, features, mean)
        put_heads(side, first + blocks * heads, b, p, features, mass)
    table = lax.broadcasted_iota(jnp.int32, (tables, stacked), 0)
    peak = jnp.full((tables, stacked), NEG, jnp.float32)
    for b in range(blocks):
        own = table == meta[OWNER, b]
        block_peak = get_heads(q_side, first + b * heads, heads)
        peak = jnp.where(own, jnp.maximum(peak, block_peak), peak)
    total = part = jnp.zeros((tables, stacked), jnp.float32)
    for b in range(blocks):
        own = table == meta[OWNER, b]
        at = b * (features // LANES)
        mass = jnp.concatenate(masses[at : at + features // LANES], axis=1)
        mean = jnp.concatenate(means[at : at + features // LANES], axis=1)
        block_peak = get_heads(q_side, first + b * heads, heads)
        scaled = jnp.where(own, jnp.exp2(block_peak - peak) * mass, 0.0)
        total = total + scaled
        part = part + scaled * mean
    here = total > 0.0
    mass = jnp.where(here, total, 1.0)
    tab_ref[0] = jnp.where(here, peak + jnp.log2(mass), NEG)
    tab_ref[1] = part / mass


def moved_weights(meta, pieces, q_side, state, features, tables):
    blocks = state.shape[0]
    stacked = features // HD * TEST
    count = len(pieces)
    return pl.pallas_call(
        lambda *refs: moved_kernel(count, features, *refs),
        in_specs=[smem_spec()] + [vmem_spec()] * (count + 2),
        out_specs=[vmem_spec()] * 3,
        out_shape=[
            pltpu.VMEM((tables * features + 2 * blocks * features // HD, TEST), jnp.float32),
            jax.ShapeDtypeStruct((2, tables, stacked), jnp.float32),
            pltpu.VMEM(state.shape, jnp.bfloat16),
        ],
        input_output_aliases={count + 2: 2},
        scratch_shapes=[pltpu.VMEM((2, BLK, WIDE), jnp.float32)],
        compiler_params=params(10),
        name="moved_weights",
    )(meta, *pieces, q_side, state)


def merged(pieces):
    peak = pieces[0][0]
    for piece in pieces[1:]:
        peak = jnp.maximum(peak, piece[0])
    mass = part = 0.0
    for piece in pieces:
        weight = jnp.exp2(piece[0] - peak)
        mass = mass + weight
        part = part + piece[1] * weight
    return peak, mass, part / mass


def query_sums_kernel(state, ab_ref, state_out):
    blocks, _, features, _ = ab_ref.shape
    stacked = features // HD * TEST
    for b in range(blocks):
        for p in range(features // LANES):
            keys = state[b, :, 2 * stacked + p * LANES : 2 * stacked + (p + 1) * LANES]
            for n, first in enumerate((stacked, 0)):
                values = state[b, :, first + p * WIDE : first + (p + 1) * WIDE]
                product = lax.dot_general(
                    keys, values, (((0,), (0,)), ((), ())), preferred_element_type=jnp.float32
                )
                ab_ref[b, n, p * LANES : p * LANES + HD, :] = product[:HD, :TEST]
                ab_ref[b, n, p * LANES + HD : (p + 1) * LANES, :] = product[HD:, TEST:]


def query_sums(features, state):
    blocks = state.shape[0]
    return pl.pallas_call(
        query_sums_kernel,
        in_specs=[vmem_spec()],
        out_specs=[vmem_spec()] * 2,
        out_shape=[
            pltpu.VMEM((blocks, 2, features, TEST), jnp.float32),
            pltpu.VMEM(state.shape, jnp.bfloat16),
        ],
        input_output_aliases={0: 1},
        compiler_params=params(8),
        name="query_sums",
    )(state)


def chip_sums_kernel(count, meta, *refs):
    tabs = refs[:count]
    q_side, g_side, ab_ref, *sums, acc_s, tab_s = refs[count:]
    tables, _, features, _ = acc_s.shape
    blocks = ab_ref.shape[0]
    heads = features // HD
    tab_s[0], tab_s[1], tab_s[2] = merged(tabs)
    acc_s[...] = jnp.zeros_like(acc_s)
    for b in range(blocks):
        at = meta[SLOT_OUT, meta[OWNER, b]]
        table = pl.ds(meta[OWNER, b], 1)
        row = tables * features + b * heads
        c = jnp.exp2(get_heads(q_side, row, heads) - tab_s[0, table, :]) / tab_s[1, table, :]
        d = c * (get_heads(g_side, row, heads) - tab_s[2, table, :])
        for h in range(heads):
            rows = slice(h * HD, (h + 1) * HD)
            lanes = slice(h * TEST, (h + 1) * TEST)
            moved, plain = ab_ref[b, 0, rows, :], ab_ref[b, 1, rows, :]
            acc_s[at, 0, rows, :] += c[:, lanes] * moved + d[:, lanes] * plain
            acc_s[at, 1, rows, :] += c[:, lanes] * plain
    per = tables // len(sums)
    for n, ref in enumerate(sums):
        ref[...] = acc_s[n * per : (n + 1) * per].astype(ref.dtype)


def chip_sums(meta, tabs, q_side, g_side, ab, features, dtypes):
    tables, stacked = tabs[0].shape[1:]
    count = len(tabs)
    per = tables // len(dtypes)
    return pl.pallas_call(
        lambda *refs: chip_sums_kernel(count, *refs),
        in_specs=[smem_spec()] + [vmem_spec()] * (count + 3),
        out_specs=[vmem_spec()] * len(dtypes),
        out_shape=[jax.ShapeDtypeStruct((per, 2, features, TEST), dtype) for dtype in dtypes],
        scratch_shapes=[
            pltpu.VMEM((tables, 2, features, TEST), jnp.float32),
            pltpu.VMEM((3, tables, stacked), jnp.float32),
        ],
        compiler_params=params(10),
        name="chip_sums",
    )(meta, *tabs, q_side, g_side, ab)


def query_grad_kernel(near, count, held, meta, *refs):
    chip, pieces = refs[:near], refs[near : near + count]
    count += near
    sums = refs[count : count + held]
    q_side, g_side, c_ref, d_ref, *outs, chip_s, tab_s = refs[count + held :]
    blocks, stacked = c_ref.shape
    heads = stacked // TEST
    first = q_side.shape[0] - blocks * heads
    chip_s[0], chip_s[1], chip_s[2] = merged(chip)
    tab_s[0], tab_s[1], tab_s[2] = merged(pieces)
    for n, ref in enumerate(outs):
        table = pl.ds(meta[OUT_TABLE, n], 1)
        c = jnp.exp2(chip_s[0, table, :] - tab_s[0, table, :])
        c = c * chip_s[1, table, :] / tab_s[1, table, :]
        d = c * (chip_s[2, table, :] - tab_s[2, table, :])
        parts = []
        for h in range(heads):
            rows = slice(h * HD, (h + 1) * HD)
            lanes = slice(h * TEST, (h + 1) * TEST)
            moved = sum(value[n, 0, rows, :].astype(jnp.float32) for value in sums)
            plain = sum(value[n, 1, rows, :].astype(jnp.float32) for value in sums)
            parts.append(c[:, lanes] * moved + d[:, lanes] * plain)
        ref[...] = (jnp.concatenate(parts, axis=0) * SCORE_SCALE).T.astype(ref.dtype)
    for b in range(blocks):
        table = pl.ds(meta[OWNER, b], 1)
        row = first + b * heads
        c = jnp.exp2(get_heads(q_side, row, heads) - tab_s[0, table, :]) / tab_s[1, table, :]
        c_ref[b : b + 1, :] = c
        d_ref[b : b + 1, :] = c * (get_heads(g_side, row, heads) - tab_s[2, table, :])


def query_grads(meta, chip, pieces, sums, q_side, g_side, blocks, q_dtypes):
    tables, stacked = pieces[0].shape[1:]
    features = sums[0].shape[2]
    return pl.pallas_call(
        lambda *refs: query_grad_kernel(len(chip), len(pieces), len(sums), *refs),
        in_specs=[smem_spec()] + [vmem_spec()] * (len(chip) + len(pieces) + len(sums) + 2),
        out_specs=[vmem_spec()] * (2 + len(q_dtypes)),
        out_shape=[
            jax.ShapeDtypeStruct((blocks, stacked), jnp.float32),
            jax.ShapeDtypeStruct((blocks, stacked), jnp.float32),
        ]
        + [jax.ShapeDtypeStruct((TEST, features), dtype) for dtype in q_dtypes],
        scratch_shapes=[
            pltpu.VMEM((3, tables, stacked), jnp.float32),
            pltpu.VMEM((3, tables, stacked), jnp.float32),
        ],
        compiler_params=params(10),
        name="query_grads",
    )(meta, *chip, *pieces, *sums, q_side, g_side)


def row_grads_kernel(meta, c_ref, d_ref, q_side, g_side, state, dk_hbm, dv_hbm, dk_s, dv_s, out_sem):
    blocks, _, features = dk_s.shape
    stacked = features // HD * TEST
    turned = (((1,), (1,)), ((), ()))
    stores = []
    for b in range(blocks):
        for p in range(features // LANES):
            at = slice(p * LANES, (p + 1) * LANES)
            wide = slice(p * WIDE, (p + 1) * WIDE)
            c = c_ref[b : b + 1, wide]
            d = d_ref[b : b + 1, wide]
            q_t = two_heads(q_side[rows_of(meta, b, p, features), :])
            g_t = two_heads(g_side[rows_of(meta, b, p, features), :])
            for_u = (q_t * (c * SCORE_SCALE)).astype(jnp.bfloat16)
            for_e = jnp.concatenate([g_t * c, q_t * (d * SCORE_SCALE)], axis=0).astype(jnp.bfloat16)
            from_e = lax.dot_general(
                state[b, :, wide], for_e, turned, preferred_element_type=jnp.float32
            )
            moved = state[b, :, stacked + p * WIDE : stacked + (p + 1) * WIDE]
            from_u = lax.dot_general(moved, for_u, turned, preferred_element_type=jnp.float32)
            dv_s[b, :, at] = from_e[:, :LANES].astype(jnp.bfloat16)
            dk_s[b, :, at] = (from_u + from_e[:, LANES:]).astype(jnp.bfloat16)
        rows = pl.ds(b * BLK, BLK)
        stores += every_copy(
            [
                pltpu.make_async_copy(dk_s.at[b], dk_hbm.at[rows], out_sem.at[0, b]),
                pltpu.make_async_copy(dv_s.at[b], dv_hbm.at[rows], out_sem.at[1, b]),
            ]
        )
    for copy in stores:
        copy.wait()


def row_grads(meta, c, d, sides, state, features):
    blocks = state.shape[0]
    return pl.pallas_call(
        row_grads_kernel,
        in_specs=[smem_spec()] + [vmem_spec()] * 5,
        out_specs=[hbm_spec()] * 2,
        out_shape=[jax.ShapeDtypeStruct((blocks * BLK, features), jnp.bfloat16)] * 2,
        scratch_shapes=[
            pltpu.VMEM((blocks, BLK, features), jnp.bfloat16),
            pltpu.VMEM((blocks, BLK, features), jnp.bfloat16),
            pltpu.SemaphoreType.DMA((2, blocks)),
        ],
        compiler_params=params(10),
        name="row_grads",
    )(meta, c, d, *sides, state)


def local(small, query_rows, key_rows, value_rows, cotangent, train_rows, test_rows, block_table):
    features = query_rows.shape[1]
    blocks = key_rows.shape[0] // BLK
    tables = train_rows.shape[0]
    pair = lambda value: lax.ppermute(value, "pair", PAIR)
    step = lambda value, s: lax.ppermute(value, "rows", [(z, z ^ s) for z in range(4)])
    after = lambda value, other: lax.optimization_barrier((value, other))
    index = lambda entries: index_table(
        small, entries, train_rows, test_rows, query_rows, key_rows, value_rows
    )
    if small:
        near = [step(query_rows, s) for s in (1, 2, 3)]
        near_grads = [step(cotangent, 1), step(cotangent, 2)]
        near_grads.append(step(near_grads[1], 1))
        block_table, near[1] = after(block_table, near[1])
        meta, own, state = index(block_table)
        near[0], meta = after(near[0], meta)
        queries = [own, pair(own)]
        for value in near:
            queries += [value, pair(value)]
        q_side, state = block_weights(meta, queries, state, features, tables)
        *near_grads[1:], q_side = lax.optimization_barrier((*near_grads[1:], q_side))
        grads = [cotangent, pair(cotangent)]
        for value in near_grads:
            grads += [value, pair(value)]
    else:
        meta, _, state = index(block_table)
        queries = [lax.all_gather(query_rows, RP, axis=0, tiled=True)]
        q_side, state = block_weights(meta, queries, state, features, tables)
        grads = [lax.all_gather(cotangent, RP, axis=0, tiled=True)]
    g_side, tab, state = moved_weights(meta, grads, q_side, state, features, tables)
    if small:
        near = [step(tab, s) for s in (3, 2, 1)]
        own = [tab, pair(tab)]
        ab, state = query_sums(features, state)
        *near, ab = lax.optimization_barrier((*near, ab))
        keep, send = chip_sums(
            meta, own, q_side, g_side, ab, features, [jnp.float32, jnp.bfloat16]
        )
        received = pair(send)
        stats = own
        for value in near:
            stats = stats + [value, pair(value)]
        dtypes = [jnp.bfloat16] * 3 + [jnp.float32]
        c, d, *low, query_grad = query_grads(
            meta, own, stats, [keep, received], q_side, g_side, blocks, dtypes
        )
        got = [step(low[s - 1], s) for s in (3, 2, 1)]
        *low, c = lax.optimization_barrier((*low, c))
        key_grad, value_grad = row_grads(meta, c, d, (q_side, g_side), state, features)
        for value in got:
            query_grad = query_grad + value.astype(jnp.float32)
    else:
        ab, state = query_sums(features, state)
        (sums,) = chip_sums(meta, [tab], q_side, g_side, ab, features, [jnp.float32])
        peak = lax.pmax(tab[0], RP)
        weight = jnp.exp2(tab[0] - peak)
        total, part = lax.psum(jnp.stack([weight, weight * tab[1]]), RP)
        rest = jnp.stack([peak + jnp.log2(total), part / total])
        c, d, *terms = query_grads(
            meta, [tab], [rest], [sums], q_side, g_side, blocks, [jnp.float32] * tables
        )
        query_grad = lax.psum_scatter(
            jnp.concatenate(terms, axis=0), RP, scatter_dimension=0, tiled=True
        )
        key_grad, value_grad = row_grads(meta, c, d, (q_side, g_side), state, features)
    return query_grad.astype(jnp.bfloat16), key_grad, value_grad


def solution(mesh):
    sizes = mesh.shape
    tables_of_rows = P(("groups", "rows", "pair"), "mp")
    in_specs = (tables_of_rows,) * 4 + (P("groups"),) * 3
    out_specs = (tables_of_rows,) * 3

    def run(query_rows, *rest):
        local_rows = query_rows.shape[0] // (sizes["groups"] * sizes["rows"] * sizes["pair"])
        small = sizes["rows"] == 4 and sizes["pair"] == 2 and local_rows == TEST
        return jax.shard_map(
            lambda *args: local(small, *args),
            mesh=mesh,
            in_specs=in_specs,
            out_specs=out_specs,
            check_vma=False,
        )(query_rows, *rest)

    return run
```
